32 devices in a mesh: segment: 2 (over x), dp: 16 (over z, y, core).
Axes of the slice: x: 2, y: 2, z: 4, core: 2. Of those that a mesh axis runs over, the one named last changes fastest.
Arguments:
- fine_inflow: bfloat16 [2, 16, 16, 16, 256], P('segment', 'dp'), may hold values from -250 to 250
- coarse_inflow: bfloat16 [2, 16, 8, 8, 512], P('segment', 'dp'), may hold values from -250 to 250
- fine_entries: bfloat16 [3, 16, 16, 16, 256], P(None, 'dp'), may hold values from -250 to 250
- fine_pending: bfloat16 [2, 2, 16, 16, 16, 256], P('segment', None, 'dp'), may hold values from -250 to 250, as said below
- coarse_pending: bfloat16 [2, 1, 16, 8, 8, 512], P('segment', None, 'dp'), may hold values from -250 to 250, as said below
- fine_kernels: bfloat16 [2, 2, 3, 3, 256, 256], P('segment'), may hold values from -0.125 to 0.125
- fine_mixing: bfloat16 [2, 256, 256], P('segment'), may hold values from -0.375 to 0.375
- fine_gains: float32 [2, 2, 256], P('segment'), may hold values from 0.5 to 1.5
- fine_shifts: float32 [2, 2, 256], P('segment'), may hold values from -3 to 3
- coarse_kernel: bfloat16 [2, 3, 3, 512, 512], P('segment'), may hold values from -0.09375 to 0.09375
- coarse_mixing: bfloat16 [2, 512, 512], P('segment'), may hold values from -0.25 to 0.25
- coarse_gains: float32 [2, 512], P('segment'), may hold values from 0.5 to 1.5
- coarse_shifts: float32 [2, 512], P('segment'), may hold values from -3 to 3
- descent_kernel: bfloat16 [2, 2, 256, 512], replicated, may hold values from -0.1875 to 0.1875
- upsample_kernel: bfloat16 [512, 2, 2, 256], replicated, may hold values from -0.25 to 0.25
Outputs:
- fine_stash: bfloat16 [2, 4, 16, 16, 16, 256], P('segment', None, 'dp')
- coarse_stash: bfloat16 [2, 4, 16, 8, 8, 512], P('segment', None, 'dp')
- fine_backlog: bfloat16 [2, 2, 16, 16, 16, 256], P('segment', None, 'dp')
- coarse_backlog: bfloat16 [2, 1, 16, 8, 8, 512], P('segment', None, 'dp')
The draws below stay inside these ranges and needn't reach their ends.
Inputs may be any that keep to these rules, and one draw needn't show every extreme that they name: `fine_pending`: at segments 1 and above only the first 1 slots are read. `coarse_pending`: at segments below 1 only the first 0 slots are read.
All inputs are finite; a program needn't handle non-finite values.
Results may differ from the reference program's by a relative error of at most 0.017.
Values may be sent and summed in bfloat16 or wider, within the bound.
A program may use at most 64 MiB of HBM per device.

```python
import jax
import jax.numpy as jnp
from jax import lax

FINE_CH = 256
COARSE_CH = 512
TILE = 16
TICKS = 4
CTILE = 8
HOLD_FINE = 2
RECV_FINE = 1
HOLD_COARSE = 1
RECV_COARSE = 0
N_SEGMENT = 2
N_DP = 16


def spread_tiles(key, tile_shape, dp_dim):
    base_key, rows_key, cols_key = jax.random.split(key, 3)
    normal_part = jnp.clip(jax.random.normal(base_key, tile_shape, jnp.float32), -6.0, 6.0)
    dp_place = lax.broadcasted_iota(jnp.float32, tile_shape, dp_dim)
    rising = 0.4 * jnp.exp(jnp.log(6.0) * dp_place / (N_DP - 1))
    row_scale = jnp.exp(jax.random.uniform(rows_key, tile_shape[:-1] + (1,), jnp.float32, jnp.log(0.3), jnp.log(3.0)))
    columns = jnp.exp(jax.random.uniform(cols_key, (tile_shape[-1],), jnp.float32, jnp.log(0.5), jnp.log(5.0)))
    return (normal_part * rising * row_scale * columns).astype(jnp.bfloat16)


def draw_fine_inflow(key, part):
    return spread_tiles(jax.random.fold_in(key, 11), (N_SEGMENT, N_DP, TILE, TILE, FINE_CH), 1)


def draw_coarse_inflow(key, part):
    return spread_tiles(jax.random.fold_in(key, 12), (N_SEGMENT, N_DP, CTILE, CTILE, COARSE_CH), 1)


def draw_fine_entries(key, part):
    return spread_tiles(jax.random.fold_in(key, 13), (TICKS - 1, N_DP, TILE, TILE, FINE_CH), 1)


def draw_fine_pending(key, part):
    return spread_tiles(jax.random.fold_in(key, 14), (N_SEGMENT, HOLD_FINE, N_DP, TILE, TILE, FINE_CH), 2)


def draw_coarse_pending(key, part):
    return spread_tiles(jax.random.fold_in(key, 15), (N_SEGMENT, HOLD_COARSE, N_DP, CTILE, CTILE, COARSE_CH), 2)


def block_scale(stream_key, shape, cuts, low, top_value):
    level, own = 1.0, jax.random.fold_in(stream_key, 6)
    for dim, parts in cuts:
        draws = jnp.exp(jax.random.uniform(jax.random.fold_in(own, dim), (parts,), jnp.float32, low / len(cuts), top_value / len(cuts)))
        level = level * jnp.repeat(draws, shape[dim] // parts).reshape([-1 if axis == dim else 1 for axis in range(len(shape))])
    return level


def bell_draw(key, extent, width, bound, pieces=(), kind=jnp.bfloat16):
    loudness = block_scale(key, extent, pieces, -0.22, 0.18) if pieces else 1.0
    array = jax.random.normal(key, extent, jnp.float32) * width * loudness
    return jnp.minimum(jnp.maximum(array, -bound), bound).astype(kind)


def setup_inputs(seed: int = 0) -> dict:
    seeds = jax.random.split(jax.random.key(seed), 16)
    return {
        "fine_inflow": draw_fine_inflow(jax.random.fold_in(seeds[15], 71), 0),
        "coarse_inflow": draw_coarse_inflow(jax.random.fold_in(seeds[15], 71), 0),
        "fine_entries": draw_fine_entries(jax.random.fold_in(seeds[15], 71), 0),
        "fine_pending": draw_fine_pending(jax.random.fold_in(seeds[15], 71), 0),
        "coarse_pending": draw_coarse_pending(jax.random.fold_in(seeds[15], 71), 0),
        "fine_kernels": bell_draw(seeds[5], (N_SEGMENT, 2, 3, 3, FINE_CH, FINE_CH), (9 * FINE_CH) ** -0.5, 0.125, ((0, 2),)),
        "fine_mixing": bell_draw(seeds[6], (N_SEGMENT, FINE_CH, FINE_CH), FINE_CH ** -0.5, 0.375, ((0, 2),)),
        "fine_gains": jnp.clip(0.5 + 1.0 * jax.random.uniform(seeds[7], (N_SEGMENT, 2, FINE_CH), jnp.float32) ** block_scale(seeds[7], (N_SEGMENT, 2, FINE_CH), ((0, 2),), -0.2, 0.2), 0.5, 1.5),
        "fine_shifts": bell_draw(seeds[8], (N_SEGMENT, 2, FINE_CH), 0.5, 3.0, ((0, 2),), jnp.float32),
        "coarse_kernel": bell_draw(seeds[9], (N_SEGMENT, 3, 3, COARSE_CH, COARSE_CH), (9 * COARSE_CH) ** -0.5, 0.09375, ((0, 2),)),
        "coarse_mixing": bell_draw(seeds[10], (N_SEGMENT, COARSE_CH, COARSE_CH), COARSE_CH ** -0.5, 0.25, ((0, 2),)),
        "coarse_gains": jnp.clip(0.5 + 1.0 * jax.random.uniform(seeds[11], (N_SEGMENT, COARSE_CH), jnp.float32) ** block_scale(seeds[11], (N_SEGMENT, COARSE_CH), ((0, 2),), -0.2, 0.2), 0.5, 1.5),
        "coarse_shifts": bell_draw(seeds[12], (N_SEGMENT, COARSE_CH), 0.5, 3.0, ((0, 2),), jnp.float32),
        "descent_kernel": bell_draw(seeds[13], (2, 2, FINE_CH, COARSE_CH), (4 * FINE_CH) ** -0.5, 0.1875),
        "upsample_kernel": bell_draw(seeds[14], (COARSE_CH, 2, 2, FINE_CH), COARSE_CH ** -0.5, 0.25),
    }


EPSILON = 1e-05

def convolve(images, kernel):
    return lax.conv_general_dilated(images, kernel, (1, 1), 'SAME', dimension_numbers=('NHWC', 'HWIO', 'NHWC'), preferred_element_type=jnp.float32)

def project(images, matrix):
    flat = images.reshape(-1, images.shape[-1])
    result = jnp.dot(flat, matrix, preferred_element_type=jnp.float32)
    return result.reshape(images.shape[:-1] + (matrix.shape[1],))

def descend(images, kernel):
    lowered = lax.conv_general_dilated(images, kernel, (2, 2), 'VALID', dimension_numbers=('NHWC', 'HWIO', 'NHWC'), preferred_element_type=jnp.float32)
    return lowered.astype(jnp.bfloat16)

def upsample(images, kernel):
    batches, height, breadth, coarse = images.shape
    fine_ch = kernel.shape[-1]
    spread = project(images, kernel.reshape(coarse, 4 * fine_ch))
    spread = spread.reshape(batches, height, breadth, 2, 2, fine_ch).transpose(0, 1, 3, 2, 4, 5)
    return spread.reshape(batches, 2 * height, 2 * breadth, fine_ch).astype(jnp.bfloat16)

def activate(values, gain, shift):
    center = lax.optimization_barrier(jnp.mean(values, axis=(0, 1, 2)))
    spread = lax.optimization_barrier(jnp.mean(jnp.square(values - center), axis=(0, 1, 2)))
    scaled = (values - center) * lax.rsqrt(spread + EPSILON) * gain + shift
    return jnp.maximum(scaled, 0.0).astype(jnp.bfloat16)

def reference(fine_inflow, coarse_inflow, fine_entries, fine_pending, coarse_pending, fine_kernels, fine_mixing, fine_gains, fine_shifts, coarse_kernel, coarse_mixing, coarse_gains, coarse_shifts, descent_kernel, upsample_kernel):
    half_depth = N_SEGMENT // 2
    fine_now = [fine_inflow[position] for position in range(N_SEGMENT)]
    coarse_now = [coarse_inflow[position] for position in range(N_SEGMENT)]
    sender_fine = [[fine_pending[pair_index, slot_index] for slot_index in range(HOLD_FINE)] for pair_index in range(half_depth)]
    receiver_fine = [[fine_pending[pair_index + half_depth, slot_index] for slot_index in range(RECV_FINE)] for pair_index in range(half_depth)]
    sender_coarse = [[coarse_pending[pair_index + half_depth, slot_index] for slot_index in range(HOLD_COARSE)] for pair_index in range(half_depth)]
    receiver_coarse = [[coarse_pending[pair_index, slot_index] for slot_index in range(RECV_COARSE)] for pair_index in range(half_depth)]
    fine_store = [[] for position in range(N_SEGMENT)]
    coarse_store = [[] for position in range(N_SEGMENT)]
    for tick_now in range(TICKS):
        if tick_now > 0:
            fine_last = [fine_store[position][-1] for position in range(N_SEGMENT)]
            coarse_last = [coarse_store[position][-1] for position in range(N_SEGMENT)]
            shifted_fine = [fine_entries[tick_now - 1]] + fine_last[:-1]
            shifted_coarse = [coarse_last[-1]] + coarse_last[:-1]
            shifted_fine[half_depth] = upsample(coarse_last[half_depth - 1], upsample_kernel)
            shifted_coarse[half_depth] = descend(fine_last[half_depth - 1], descent_kernel)
            fine_now = shifted_fine
            coarse_now = shifted_coarse
        for pair_index in range(half_depth):
            receiver_fine[pair_index].append(sender_fine[pair_index][tick_now])
            receiver_coarse[pair_index].append(sender_coarse[pair_index][tick_now])
        for position in range(N_SEGMENT):
            if position < half_depth:
                fine_input = fine_now[position]
                coarse_taken = receiver_coarse[position][tick_now]
                coarse_input = (project(coarse_now[position], coarse_mixing[position]) + coarse_taken.astype(jnp.float32)).astype(jnp.bfloat16)
            else:
                fine_taken = receiver_fine[position - half_depth][tick_now]
                fine_input = (project(fine_now[position], fine_mixing[position]) + fine_taken.astype(jnp.float32)).astype(jnp.bfloat16)
                coarse_input = coarse_now[position]
            fine_first = activate(convolve(fine_input, fine_kernels[position, 0]), fine_gains[position, 0], fine_shifts[position, 0])
            fine_out = activate(convolve(fine_first, fine_kernels[position, 1]), fine_gains[position, 1], fine_shifts[position, 1])
            coarse_out = activate(convolve(coarse_input, coarse_kernel[position]), coarse_gains[position], coarse_shifts[position])
            fine_store[position].append(fine_out)
            coarse_store[position].append(coarse_out)
            if position < half_depth:
                sender_fine[position].append(project(fine_out, fine_mixing[position]).astype(jnp.bfloat16))
            else:
                sender_coarse[position - half_depth].append(project(coarse_out, coarse_mixing[position]).astype(jnp.bfloat16))
    fine_stash = jnp.stack([jnp.stack(fine_store[position]) for position in range(N_SEGMENT)])
    coarse_stash = jnp.stack([jnp.stack(coarse_store[position]) for position in range(N_SEGMENT)])
    fine_zero = jnp.zeros_like(fine_inflow[0])
    coarse_zero = jnp.zeros_like(coarse_inflow[0])
    fine_rows = []
    coarse_rows = []
    for position in range(N_SEGMENT):
        if position < half_depth:
            fine_rows.append(jnp.stack(sender_fine[position][TICKS:TICKS + HOLD_FINE]))
            chosen = receiver_coarse[position][TICKS:TICKS + RECV_COARSE] + [coarse_zero] * (HOLD_COARSE - RECV_COARSE)
            coarse_rows.append(jnp.stack(chosen))
        else:
            chosen = receiver_fine[position - half_depth][TICKS:TICKS + RECV_FINE] + [fine_zero] * (HOLD_FINE - RECV_FINE)
            fine_rows.append(jnp.stack(chosen))
            coarse_rows.append(jnp.stack(sender_coarse[position - half_depth][TICKS:TICKS + HOLD_COARSE]))
    return (fine_stash, coarse_stash, jnp.stack(fine_rows), jnp.stack(coarse_rows))
```

```python
import functools

import jax
import jax.numpy as jnp
from jax import lax
from jax.experimental import pallas as pl
from jax.experimental.pallas import tpu as pltpu
from jax.sharding import PartitionSpec as P

EPSILON = 1e-05
LANES = 128
MESH = pl.DeviceIdType.MESH
F32 = jnp.float32
BF16 = jnp.bfloat16


def dot(a, b):
    return jnp.dot(a, b, preferred_element_type=F32)


def side_shifts(x, side):
    cells = x.shape[0]
    column = lax.rem(lax.broadcasted_iota(jnp.int32, x.shape, 0), side)
    before = jnp.where(column == 0, 0.0, pltpu.roll(x, 1, 0))
    after = jnp.where(column == side - 1, 0.0, pltpu.roll(x, cells - 1, 0))
    return before, x, after


def spread_taps(x, cols, side):
    cells, width = x.shape
    edge = jnp.zeros((side, width), F32)
    for dc, part in enumerate(side_shifts(x, side)):
        above = jnp.concatenate([edge, part[: cells - side]], axis=0)
        below = jnp.concatenate([part[side:], edge], axis=0)
        for dr, moved in enumerate((above, part, below)):
            start = (3 * dr + dc) * width
            cols[:, start : start + width] = moved.astype(BF16)


def put_stats(h, out):
    width = h.shape[1]
    rows = width // LANES
    total = jnp.sum(h, axis=0, keepdims=True)
    square = jnp.sum(h * h, axis=0, keepdims=True)
    for row in range(rows):
        lanes = slice(row * LANES, (row + 1) * LANES)
        out[row : row + 1, :] = total[:, lanes]
        out[rows + row : rows + row + 1, :] = square[:, lanes]


def norm_terms(total, gain, shift, count):
    rows = total.shape[0] // 2
    sums = jnp.concatenate([total[row : row + 1] for row in range(rows)], axis=1)
    squares = jnp.concatenate([total[rows + row : rows + row + 1] for row in range(rows)], axis=1)
    center = sums * (1.0 / count)
    spread = jnp.maximum(squares * (1.0 / count) - center * center, 0.0)
    scale = lax.rsqrt(spread + EPSILON) * gain
    return scale, shift - center * scale


def kernel(
    dims,
    fine_in, coarse_in, entries, fine_pend, coarse_pend,
    wf_hbm, mixf_hbm, fgain, fshift, wc_hbm, mixc_hbm, cgain, cshift, wd_hbm, wu_hbm,
    fst_out, cst_out, fback_out, cback_out,
    wf, mixf, wc, mixc, wd, wu,
    fin, cin, upin, skf, skc, fst, cst, dbuf,
    xs, hf, hg, hc, upscr, colf, colc, zf, zc,
    statf, statc, gotf, gotc,
    wu4, wuf, load_sem, save_sem,
    fin_r, cin_r, up_r, skf_r, skc_r,
    fin_s, cin_s, up_s, skf_s, skc_s,
    gotf_r, gotc_r, statf_s, statc_s,
):
    nseg, ndp, ticks, fside, cside, hold_f, recv_f, hold_c, recv_c = dims
    half = nseg // 2
    seg = lax.axis_index("segment")
    me = lax.axis_index("dp")
    lower = seg < half
    upper = seg >= half
    turn = seg == half - 1
    after = lax.rem(seg + 1, nseg)
    mate = lax.rem(seg + half, nseg)

    def load(k, src, dst):
        return pltpu.make_async_copy(src, dst, load_sem.at[k])

    get_fine = load(0, fine_in, fin.at[0])
    get_wf0 = load(1, wf_hbm.at[0], wf.at[0])
    get_mixf = load(2, mixf_hbm, mixf)
    get_coarse = load(3, coarse_in, cin.at[0])
    get_mixc = load(4, mixc_hbm, mixc)
    get_wc = load(5, wc_hbm, wc)
    get_wf1 = load(6, wf_hbm.at[1], wf.at[1])
    get_wd = load(7, wd_hbm, wd)
    get_wu = load(11, wu_hbm, wu4)
    own_entries = load(8, entries, fin.at[pl.ds(1, ticks - 1)])
    own_fine = hold_f if hold_f > ticks else 0
    own_coarse = hold_c if hold_c > ticks else 0

    def own_pend(k, src, dst, count):
        return load(k, src.at[pl.ds(0, count)], dst.at[pl.ds(0, count)])

    barrier = pltpu.get_barrier_semaphore()
    offsets = sorted({1 % nseg, nseg - 1, half})

    def greet(k, carry):
        pl.semaphore_signal(
            barrier, inc=1, device_id=(seg, lax.rem(me + k, ndp)), device_id_type=MESH
        )
        return carry

    lax.fori_loop(1, ndp, greet, 0)
    for offset in offsets:
        pl.semaphore_signal(
            barrier, inc=1, device_id=(lax.rem(seg + offset, nseg), me), device_id_type=MESH
        )
    @pl.when(upper)
    def _():
        if recv_f:
            own_pend(9, fine_pend, skf, recv_f).start()

    for item in (get_fine, get_wf0, get_mixf, get_coarse, get_mixc, get_wc, get_wf1):
        item.start()

    @pl.when(lower)
    def _():
        if recv_c:
            own_pend(10, coarse_pend, skc, recv_c).start()
        if own_fine:
            own_pend(9, fine_pend, skf, own_fine).start()

    @pl.when(upper)
    def _():
        if own_coarse:
            own_pend(10, coarse_pend, skc, own_coarse).start()

    @pl.when(seg == 0)
    def _():
        own_entries.start()

    @pl.when(turn)
    def _():
        get_wd.start()

    @pl.when(seg == half)
    def _():
        get_wu.start()

    zf[...] = jnp.zeros_like(zf)
    zc[...] = jnp.zeros_like(zc)
    pl.semaphore_wait(barrier, ndp - 1 + len(offsets))

    def push(src, dst, ssem, rsem, to):
        return pltpu.make_async_remote_copy(
            src_ref=src, dst_ref=dst, send_sem=ssem, recv_sem=rsem,
            device_id=(to, me), device_id_type=MESH,
        )

    def send_skf(j):
        return push(skf.at[j], skf.at[recv_f + j], skf_s.at[j], skf_r.at[j], mate)

    def send_pend_f(j):
        return push(fine_pend.at[j], skf.at[recv_f + j], skf_s.at[j], skf_r.at[j], mate)

    def send_pend_c(j):
        return push(coarse_pend.at[j], skc.at[recv_c + j], skc_s.at[j], skc_r.at[j], mate)

    def send_skc(j):
        return push(skc.at[j], skc.at[recv_c + j], skc_s.at[j], skc_r.at[j], mate)

    def send_up(t):
        return push(cst.at[t], upin.at[t], up_s.at[t], up_r.at[t], after)

    def send_co(t):
        return push(cst.at[t], cin.at[t + 1], cin_s.at[t], cin_r.at[t], after)

    def send_down(t):
        return push(dbuf.at[t], cin.at[t + 1], cin_s.at[t], cin_r.at[t], after)

    def send_fo(t):
        return push(fst.at[t], fin.at[t + 1], fin_s.at[t], fin_r.at[t], after)

    def exchange(src, dst, ssem, rsem):
        def one(k, carry):
            pltpu.make_async_remote_copy(
                src_ref=src, dst_ref=dst.at[k - 1], send_sem=ssem, recv_sem=rsem,
                device_id=(seg, lax.rem(me + k, ndp)), device_id_type=MESH,
            ).start()
            return carry

        lax.fori_loop(1, ndp, one, 0)

    def whole(dst, ssem, rsem):
        return pltpu.make_async_remote_copy(
            src_ref=dst, dst_ref=dst, send_sem=ssem, recv_sem=rsem,
            device_id=(seg, lax.rem(me + 1, ndp)), device_id_type=MESH,
        )

    @pl.when(lower)
    def _():
        for j in range(min(hold_f, ticks)):
            send_pend_f(j).start()

    @pl.when(upper)
    def _():
        for j in range(min(hold_c, ticks)):
            send_pend_c(j).start()

    fcount = ndp * fside * fside
    ccount = ndp * cside * cside

    def save_f(t):
        return pltpu.make_async_copy(fst.at[t], fst_out.at[t], save_sem.at[0, t])

    def save_c(t):
        return pltpu.make_async_copy(cst.at[t], cst_out.at[t], save_sem.at[1, t])

    def first(t, *items):
        @pl.when(t == 0)
        def _():
            for item in items:
                item.wait()

    def front(t):
        first(t, get_fine, get_mixf)

        @pl.when(lower)
        def _():
            @pl.when(jnp.logical_and(seg > 0, t > 0))
            def _():
                send_fo(t - 1).wait_recv()

            xs[...] = fin[t].astype(F32)

        @pl.when(upper)
        def _():
            @pl.when(jnp.logical_and(seg == half, t > 0))
            def _():
                send_up(t - 1).wait_recv()
                spread = dot(upin[t - 1], wu[...])
                width = spread.shape[1] // 4
                for a in range(2):
                    for c in range(2):
                        start = (2 * a + c) * width
                        part = spread[:, start : start + width].reshape(cside, cside, width)
                        for i in range(width // LANES):
                            lanes = slice(i * LANES, (i + 1) * LANES)
                            upscr[i, :, pl.ds(a * fside + c, cside, stride=2), :] = part[:, :, lanes]
                for i in range(width // LANES):
                    lanes = slice(i * LANES, (i + 1) * LANES)
                    fin[t, :, lanes] = upscr[i].reshape(fside * fside, LANES).astype(BF16)

            @pl.when(jnp.logical_and(seg != half, t > 0))
            def _():
                send_fo(t - 1).wait_recv()

            if recv_f:
                first(t, own_pend(9, fine_pend, skf, recv_f))

            @pl.when(t >= recv_f)
            def _():
                send_skf(t - recv_f).wait_recv()

            xs[...] = (dot(fin[t], mixf[...]) + skf[t].astype(F32)).astype(BF16).astype(F32)

        spread_taps(xs[...], colf, fside)
        first(t, get_wf0)
        hf[...] = dot(colf[...], wf[0])
        put_stats(hf[...], statf.at[2 * t])
        exchange(statf.at[2 * t], gotf.at[2 * t], statf_s.at[2 * t], gotf_r.at[2 * t])

    def later(which, t):
        @pl.when(jnp.logical_and(which, t < ticks - 1))
        def _():
            front(t + 1)

    def own_pieces(t):
        @pl.when(t == 0)
        def _():
            get_wf1.wait()

            @pl.when(turn)
            def _():
                get_wd.wait()

            @pl.when(seg == 0)
            def _():
                own_entries.wait()

            @pl.when(seg == half)
            def _():
                get_wu.wait()
                width = wu4.shape[3]
                depth = wuf.shape[1] // 4

                def rows_of(n, carry):
                    rows = pl.multiple_of(n * depth, depth)
                    piece = wu4[pl.ds(rows, depth)].astype(F32).reshape(4 * depth, width)
                    for i in range(width // LANES):
                        wuf[i] = piece[:, i * LANES : (i + 1) * LANES]
                    for q in range(4):
                        for i in range(width // LANES):
                            start = q * width + i * LANES
                            part = wuf[i, pl.ds(q, depth, stride=4), :]
                            wu[pl.ds(rows, depth), start : start + LANES] = part.astype(BF16)
                    return carry

                lax.fori_loop(0, wu4.shape[0] // depth, rows_of, 0)

    front(jnp.int32(0))
    own_pieces(jnp.int32(0))

    def tick(t, carry):
        first(t, get_coarse, get_mixc)

        @pl.when(t > 0)
        def _():
            send_co(t - 1).wait_recv()

        @pl.when(lower)
        def _():
            if recv_c:
                first(t, own_pend(10, coarse_pend, skc, recv_c))

            @pl.when(t >= recv_c)
            def _():
                send_skc(t - recv_c).wait_recv()

            hc[...] = (dot(cin[t], mixc[...]) + skc[t].astype(F32)).astype(BF16).astype(F32)

        @pl.when(upper)
        def _():
            hc[...] = cin[t].astype(F32)

        spread_taps(hc[...], colc, cside)
        first(t, get_wc)
        hc[...] = dot(colc[...], wc[...])
        put_stats(hc[...], statc.at[t])
        exchange(statc.at[t], gotc.at[t], statc_s.at[t], gotc_r.at[t])

        whole(gotf.at[2 * t], statf_s.at[2 * t], gotf_r.at[2 * t]).wait_recv()
        total = statf[2 * t] + jnp.sum(gotf[2 * t], axis=0)
        scale, offset = norm_terms(total, fgain[0:1, :], fshift[0:1, :], fcount)
        xs[...] = jnp.maximum(hf[...] * scale + offset, 0.0).astype(BF16).astype(F32)
        spread_taps(xs[...], colf, fside)
        hg[...] = dot(colf[...], wf[1])
        put_stats(hg[...], statf.at[2 * t + 1])
        exchange(
            statf.at[2 * t + 1], gotf.at[2 * t + 1], statf_s.at[2 * t + 1], gotf_r.at[2 * t + 1]
        )

        whole(gotc.at[t], statc_s.at[t], gotc_r.at[t]).wait_recv()
        total = statc[t] + jnp.sum(gotc[t], axis=0)
        scale, offset = norm_terms(total, cgain[...], cshift[...], ccount)
        cst[t] = jnp.maximum(hc[...] * scale + offset, 0.0).astype(BF16)

        @pl.when(t < ticks - 1)
        def _():
            @pl.when(turn)
            def _():
                send_up(t).start()

            @pl.when(jnp.logical_not(turn))
            def _():
                send_co(t).start()

        save_c(t).start()

        @pl.when(upper)
        def _():
            skc[hold_c + t] = dot(cst[t], mixc[...]).astype(BF16)

            @pl.when(hold_c + t < ticks)
            def _():
                send_skc(hold_c + t).start()

        later(seg == 0, t)

        whole(gotf.at[2 * t + 1], statf_s.at[2 * t + 1], gotf_r.at[2 * t + 1]).wait_recv()
        total = statf[2 * t + 1] + jnp.sum(gotf[2 * t + 1], axis=0)
        scale, offset = norm_terms(total, fgain[1:2, :], fshift[1:2, :], fcount)
        fst[t] = jnp.maximum(hg[...] * scale + offset, 0.0).astype(BF16)

        @pl.when(t < ticks - 1)
        def _():
            @pl.when(turn)
            def _():
                width = fst.shape[2]
                for i in range(width // LANES):
                    lanes = slice(i * LANES, (i + 1) * LANES)
                    upscr[i] = fst[t, :, lanes].astype(F32).reshape(cside, 2 * fside, LANES)
                lowered = None
                for a in range(2):
                    for c in range(2):
                        for i in range(width // LANES):
                            part = upscr[i, :, pl.ds(a * fside + c, cside, stride=2), :]
                            part = part.reshape(cside * cside, LANES).astype(BF16)
                            start = (2 * a + c) * width + i * LANES
                            term = dot(part, wd[start : start + LANES, :])
                            lowered = term if lowered is None else lowered + term
                dbuf[t] = lowered.astype(BF16)
                send_down(t).start()

            @pl.when(jnp.logical_and(jnp.logical_not(turn), seg < nseg - 1))
            def _():
                send_fo(t).start()

        save_f(t).start()

        @pl.when(lower)
        def _():
            skf[hold_f + t] = dot(fst[t], mixf[...]).astype(BF16)

            @pl.when(hold_f + t < ticks)
            def _():
                send_skf(hold_f + t).start()

        later(seg > 0, t)
        return carry

    lax.fori_loop(0, ticks, tick, 0)

    def back_f(first, src):
        return pltpu.make_async_copy(src, fback_out.at[first], save_sem.at[2, first])

    def back_c(first, src):
        return pltpu.make_async_copy(src, cback_out.at[first], save_sem.at[3, first])

    lower_backs = [back_f(j, skf.at[ticks + j]) for j in range(hold_f)]
    lower_backs += [
        back_c(j, skc.at[ticks + j] if j < recv_c else zc) for j in range(hold_c)
    ]
    upper_backs = [
        back_f(j, skf.at[ticks + j] if j < recv_f else zf) for j in range(hold_f)
    ]
    upper_backs += [back_c(j, skc.at[ticks + j]) for j in range(hold_c)]

    @pl.when(lower)
    def _():
        if own_fine:
            own_pend(9, fine_pend, skf, own_fine).wait()
        for j in range(max(ticks - recv_c, 0), ticks):
            send_skc(j).wait_recv()
        for item in lower_backs:
            item.start()
        for j in range(ticks):
            send_skf(j).wait_send()
        for item in lower_backs:
            item.wait()

    @pl.when(upper)
    def _():
        if own_coarse:
            own_pend(10, coarse_pend, skc, own_coarse).wait()
        for j in range(max(ticks - recv_f, 0), ticks):
            send_skf(j).wait_recv()
        for item in upper_backs:
            item.start()
        for j in range(ticks):
            send_skc(j).wait_send()
        for item in upper_backs:
            item.wait()

    @pl.when(turn)
    def _():
        for t in range(ticks - 1):
            send_up(t).wait_send()

    @pl.when(jnp.logical_and(jnp.logical_not(turn), seg < nseg - 1))
    def _():
        for t in range(ticks - 1):
            send_fo(t).wait_send()

    for t in range(ticks - 1):
        send_co(t).wait_send()
    for t in range(ticks):
        whole(gotf.at[2 * t], statf_s.at[2 * t], gotf_r.at[2 * t]).wait_send()
        whole(gotf.at[2 * t + 1], statf_s.at[2 * t + 1], gotf_r.at[2 * t + 1]).wait_send()
        whole(gotc.at[t], statc_s.at[t], gotc_r.at[t]).wait_send()
        save_f(t).wait()
        save_c(t).wait()


def sums_of(total):
    rows = total.shape[0] // 2
    sums = jnp.concatenate([total[row : row + 1] for row in range(rows)], axis=1)
    squares = jnp.concatenate([total[rows + row : rows + row + 1] for row in range(rows)], axis=1)
    return sums, squares


def moments(total, count):
    sums, squares = sums_of(total)
    center = sums * (1.0 / count)
    spread = jnp.maximum(squares * (1.0 / count) - center * center, 0.0)
    return center, lax.rsqrt(spread + EPSILON)


def pair_kernel(
    dims,
    fine_in, coarse_in, entries, fine_pend, coarse_pend,
    wf_hbm, mixf_hbm, fgain, fshift, wc_hbm, mixc_hbm, cgain, cshift, wd_hbm, wu_hbm,
    fst, cst, fback, cback,
    wf, mixf, wc, mixc, mixm, wd, wu, wu4, wuf,
    fin, cin, skf, skc, mate_fgain, mate_fshift, mate_cgain, mate_cshift,
    h1, h2, hc, xs, hx, upscr, colf, colc, cold,
    rawf_out, rawf_in, rawc_out, rawc_in,
    st1, st2, stc, got1, got2, gotc, farf, farc,
    load_sem, s1, r1, s2, r2, sc, rc, sfarf, rfarf, sfarc, rfarc,
    srawf, rrawf, srawc, rrawc, skf_s, skf_r, one_s, one_r,
):
    nseg, ndp, ticks, fside, cside, hold_f, recv_f, hold_c, recv_c = dims
    seg = lax.axis_index("segment")
    me = lax.axis_index("dp")
    other = 1 - seg
    lower = seg == 0
    upper = seg == 1
    fcells, ccells = fside * fside, cside * cside
    fcount, ccount = ndp * fcells, ndp * ccells
    last = ticks - 1

    barrier = pltpu.get_barrier_semaphore()

    def greet(k, carry):
        pl.semaphore_signal(
            barrier, inc=1, device_id=(seg, lax.rem(me + k, ndp)), device_id_type=MESH
        )
        return carry

    def greet_far(k, carry):
        pl.semaphore_signal(
            barrier, inc=1, device_id=(other, lax.rem(me + k, ndp)), device_id_type=MESH
        )
        return carry

    lax.fori_loop(0, ndp, greet_far, 0)
    lax.fori_loop(1, ndp, greet, 0)

    def load(k, src, dst):
        return pltpu.make_async_copy(src, dst, load_sem.at[k])

    get_fine = load(0, fine_in, fin.at[0])
    get_wf0 = load(1, wf_hbm.at[0], wf.at[0])
    get_mixf = load(2, mixf_hbm, mixf)
    get_coarse = load(3, coarse_in, cin)
    get_mixc = load(4, mixc_hbm, mixc)
    get_wc = load(5, wc_hbm, wc)
    get_wf1 = load(6, wf_hbm.at[1], wf.at[1])
    get_wd = load(7, wd_hbm, wd)
    get_entries = load(8, entries, fin.at[pl.ds(1, last)])
    get_pend = load(9, fine_pend.at[pl.ds(0, recv_f)], skf.at[pl.ds(0, recv_f)])
    get_wu = load(10, wu_hbm, wu4)

    get_fine.start()

    @pl.when(upper)
    def _():
        get_mixf.start()
        get_pend.start()

    get_wf0.start()

    @pl.when(lower)
    def _():
        for item in (get_entries, get_wf1, get_mixf, get_coarse, get_mixc, get_wc):
            item.start()

    @pl.when(upper)
    def _():
        for item in (get_coarse, get_wc, get_wf1, get_wd, get_wu, get_mixc):
            item.start()

    bits = ndp.bit_length() - 1

    def partner(k):
        if 1 << bits != ndp:
            return lax.rem(me + k, ndp)
        to = 0
        for b in range(bits):
            step = 1 << b
            to = to + step * lax.rem(lax.div(me, step) + lax.div(k, step), 2)
        return to

    def push(src, dst, ssem, rsem):
        return pltpu.make_async_remote_copy(
            src_ref=src, dst_ref=dst, send_sem=ssem, recv_sem=rsem,
            device_id=(other, me), device_id_type=MESH,
        )

    def share(src, dst, ssem, rsem):
        def one(i, carry):
            k = ndp - 1 - i
            pltpu.make_async_remote_copy(
                src_ref=src, dst_ref=dst.at[k - 1], send_sem=ssem, recv_sem=rsem,
                device_id=(seg, partner(k)), device_id_type=MESH,
            ).start()
            return carry

        lax.fori_loop(0, ndp - 1, one, 0)

    def cast_far(src, dst, ssem, rsem):
        def one(i, carry):
            k = ndp - 1 - i
            pltpu.make_async_remote_copy(
                src_ref=src, dst_ref=dst.at[k], send_sem=ssem, recv_sem=rsem,
                device_id=(other, partner(k)), device_id_type=MESH,
            ).start()
            return carry

        lax.fori_loop(0, ndp, one, 0)

    def of_1(t):
        return push(got1.at[t], got1.at[t], s1.at[t], r1.at[t])

    def of_2(t):
        return push(got2.at[t], got2.at[t], s2.at[t], r2.at[t])

    def of_c(t):
        return push(gotc.at[t], gotc.at[t], sc.at[t], rc.at[t])

    def of_farf(t):
        return push(farf.at[t], farf.at[t], sfarf.at[t], rfarf.at[t])

    def of_farc(t):
        return push(farc.at[t], farc.at[t], sfarc.at[t], rfarc.at[t])

    def send_rawf(t):
        return push(rawf_out.at[t], rawf_in.at[t], srawf.at[t], rrawf.at[t])

    def send_rawc(t):
        return push(rawc_out.at[t], rawc_in.at[t], srawc.at[t], rrawc.at[t])

    def send_skf(j):
        return push(skf.at[j], skf.at[recv_f + j], skf_s.at[j], skf_r.at[j])

    def send_pend_f(j):
        return push(fine_pend.at[j], skf.at[recv_f + j], skf_s.at[j], skf_r.at[j])

    send_pend_c = push(coarse_pend.at[0], skc, one_s.at[0], one_r.at[0])
    send_mix = push(mixc_hbm, mixm, one_s.at[1], one_r.at[1])
    send_norms = [
        push(fgain, mate_fgain, one_s.at[2], one_r.at[2]),
        push(fshift, mate_fshift, one_s.at[3], one_r.at[3]),
        push(cgain, mate_cgain, one_s.at[4], one_r.at[4]),
        push(cshift, mate_cshift, one_s.at[5], one_r.at[5]),
    ]

    def conv_fine(layer, out):
        spread_taps(xs[...], colf, fside)
        out[...] = dot(colf[...], wf[layer])

    def conv_coarse(out):
        spread_taps(hx[...], colc, cside)
        out[...] = dot(colc[...], wc[...])

    def centred(h, stats, cells):
        sums, _ = sums_of(stats)
        return (h - sums * (1.0 / cells)).astype(BF16)

    def arrived(raw, got, gain, shift, count, cells):
        center, inverse = moments(jnp.sum(got[...], axis=0), count)
        own, _ = sums_of(got[0])
        scale = inverse * gain
        offset = shift + (own * (1.0 / cells) - center) * scale
        return jnp.maximum(raw[...].astype(F32) * scale + offset, 0.0).astype(BF16)

    def normed(h, stats, got, gain, shift, count):
        scale, offset = norm_terms(stats[...] + jnp.sum(got[...], axis=0), gain, shift, count)
        return jnp.maximum(h[...] * scale + offset, 0.0).astype(BF16)

    def first_stats(t):
        put_stats(h1[t], st1.at[t])

    def first_share(t):
        share(st1.at[t], got1.at[t], s1.at[t], r1.at[t])

    def second(t):
        of_1(t).wait_recv()
        xs[...] = normed(
            h1.at[t], st1.at[t], got1.at[t], fgain[0:1, :], fshift[0:1, :], fcount
        ).astype(F32)
        conv_fine(1, h2.at[t])
        put_stats(h2[t], st2.at[t])

    def second_share(t):
        share(st2.at[t], got2.at[t], s2.at[t], r2.at[t])

    def finish_fine(t):
        of_2(t).wait_recv()
        fst[t] = normed(h2.at[t], st2.at[t], got2.at[t], fgain[1:2, :], fshift[1:2, :], fcount)

    def finish_coarse(t):
        of_c(t).wait_recv()
        cst[t] = normed(hc.at[t], stc.at[t], gotc.at[t], cgain[...], cshift[...], ccount)

    def coarse(t):
        conv_coarse(hc.at[t])
        put_stats(hc[t], stc.at[t])

        @pl.when(t < last)
        def _():
            cast_far(stc.at[t], farc.at[t], sfarc.at[t], rfarc.at[t])
            rawc_out[t] = centred(hc[t], stc[t], ccells)
            send_rawc(t).start()

        share(stc.at[t], gotc.at[t], sc.at[t], rc.at[t])

    def mate_coarse(t):
        of_farc(t).wait_recv()
        send_rawc(t).wait_recv()
        return arrived(rawc_in.at[t], farc.at[t], mate_cgain[...], mate_cshift[...], ccount, ccells)

    get_fine.wait()

    @pl.when(lower)
    def _():
        xs[...] = fin[0].astype(F32)

    @pl.when(upper)
    def _():
        get_mixf.wait()
        get_pend.wait()
        xs[...] = (dot(fin[0], mixf[...]) + skf[0].astype(F32)).astype(BF16).astype(F32)

    get_wf0.wait()
    conv_fine(0, h1.at[0])
    first_stats(0)
    pl.semaphore_wait(barrier, 2 * ndp - 1)
    first_share(0)
    for item in send_norms:
        item.start()

    @pl.when(lower)
    def _():
        for j in range(hold_f):
            send_pend_f(j).start()
        get_entries.wait()

        def early(t, carry):
            xs[...] = fin[t].astype(F32)
            conv_fine(0, h1.at[t])
            first_stats(t)
            first_share(t)
            return carry

        lax.fori_loop(1, ticks, early, 0)
        for item in (get_wf1, get_mixf, get_coarse, get_mixc, get_wc):
            item.wait()

        def term(t, carry):
            finish_fine(t)
            fresh = dot(fst[t], mixf[...]).astype(BF16)

            @pl.when(hold_f + t < ticks)
            def _():
                skf[hold_f + t] = fresh
                send_skf(hold_f + t).start()

            @pl.when(hold_f + t >= ticks)
            def _():
                fback[hold_f + t - ticks] = fresh

            return carry

        def encode(i, carry):
            @pl.when(i < ticks)
            def _():
                second(i)

                @pl.when(i < last)
                def _():
                    cast_far(st2.at[i], farf.at[i], sfarf.at[i], rfarf.at[i])
                    rawf_out[i] = centred(h2[i], st2[i], fcells)
                    send_rawf(i).start()

                second_share(i)

            t = jnp.maximum(i - last + 1, 0)

            @pl.when(i == 0)
            def _():
                send_pend_c.wait_recv()
                hx[...] = (dot(cin[...], mixc[...]) + skc[...].astype(F32)).astype(BF16).astype(F32)

            @pl.when(i >= last)
            def _():
                @pl.when(i == last)
                def _():
                    send_mix.wait_recv()
                    for item in send_norms:
                        item.wait_recv()

                taken = mate_coarse(t - 1)
                fresh = dot(taken, mixm[...]).astype(BF16)
                hx[...] = (dot(taken, mixc[...]) + fresh.astype(F32)).astype(BF16).astype(F32)

            @pl.when(jnp.logical_or(i == 0, i >= last))
            def _():
                coarse(t)

            @pl.when(i == last)
            def _():
                lax.fori_loop(0, ticks, term, 0)
                finish_coarse(0)

            @pl.when(i > last)
            def _():
                finish_coarse(t - 1)

            return carry

        lax.fori_loop(0, 2 * ticks - 2, encode, 0)
        cback[...] = jnp.zeros_like(cback)
        finish_coarse(last)
        for t in range(last):
            of_farf(t).wait_send()
            send_rawf(t).wait_send()
        for j in range(ticks):
            send_skf(j).wait_send()

    @pl.when(upper)
    def _():
        send_pend_c.start()
        for item in (get_coarse, get_wc, get_wf1, get_wd, get_wu, get_mixc):
            item.wait()

        def spread_weights():
            width = wu4.shape[3]
            depth = wuf.shape[1] // 4

            def rows_of(n, carry):
                rows = pl.multiple_of(n * depth, depth)
                piece = wu4[pl.ds(rows, depth)].astype(F32).reshape(4 * depth, width)
                for i in range(width // LANES):
                    wuf[i] = piece[:, i * LANES : (i + 1) * LANES]
                for q in range(4):
                    for i in range(width // LANES):
                        start = q * width + i * LANES
                        part = wuf[i, pl.ds(q, depth, stride=4), :]
                        wu[pl.ds(rows, depth), start : start + LANES] = part.astype(BF16)
                return carry

            lax.fori_loop(0, wu4.shape[0] // depth, rows_of, 0)

        def decode(t, carry):
            @pl.when(t == 0)
            def _():
                hx[...] = cin[...].astype(F32)

            @pl.when(t > 0)
            def _():
                @pl.when(t == 1)
                def _():
                    for item in send_norms:
                        item.wait_recv()

                of_farf(t - 1).wait_recv()
                send_rawf(t - 1).wait_recv()
                taken = arrived(
                    rawf_in.at[t - 1], farf.at[t - 1], mate_fgain[1:2, :], mate_fshift[1:2, :],
                    fcount, fcells,
                ).astype(F32)
                width = taken.shape[1]
                for i in range(width // LANES):
                    lanes = slice(i * LANES, (i + 1) * LANES)
                    upscr[i] = taken[:, lanes].reshape(cside, 2 * fside, LANES)
                for a in range(2):
                    for c in range(2):
                        for i in range(width // LANES):
                            part = upscr[i, :, pl.ds(a * fside + c, cside, stride=2), :]
                            start = (2 * a + c) * width + i * LANES
                            cold[:, start : start + LANES] = part.reshape(ccells, LANES).astype(BF16)
                hx[...] = dot(cold[...], wd[...]).astype(BF16).astype(F32)

            coarse(t)

            @pl.when(t == 0)
            def _():
                send_mix.start()
                spread_weights()

            @pl.when(t == last)
            def _():
                finish_fine(0)
                lax.fori_loop(0, last, lambda n, c: (finish_coarse(n), c)[1], 0)

                def rest(n, c):
                    finish_fine(n)
                    return c

                lax.fori_loop(1, last - 1, rest, 0)

            @pl.when(t > 0)
            def _():
                @pl.when(t >= recv_f)
                def _():
                    send_skf(t - recv_f).wait_recv()

                spread = dot(mate_coarse(t - 1), wu[...])
                width = spread.shape[1] // 4
                for a in range(2):
                    for c in range(2):
                        start = (2 * a + c) * width
                        part = spread[:, start : start + width].reshape(cside, cside, width)
                        for i in range(width // LANES):
                            lanes = slice(i * LANES, (i + 1) * LANES)
                            upscr[i, :, pl.ds(a * fside + c, cside, stride=2), :] = part[:, :, lanes]
                for i in range(width // LANES):
                    lanes = slice(i * LANES, (i + 1) * LANES)
                    fin[t, :, lanes] = upscr[i].reshape(fcells, LANES).astype(BF16)
                xs[...] = (dot(fin[t], mixf[...]) + skf[t].astype(F32)).astype(BF16).astype(F32)
                conv_fine(0, h1.at[t])
                first_stats(t)
                first_share(t)

            n = jnp.where(t < last, t, last) - 1

            @pl.when(t > 0)
            def _():
                second(n)
                second_share(n)

            return carry

        lax.fori_loop(0, ticks, decode, 0)
        finish_coarse(last)
        cback[0] = dot(cst[last], mixc[...]).astype(BF16)
        for j in range(max(ticks - recv_f, 0), ticks):
            send_skf(j).wait_recv()
        for j in range(hold_f):
            fback[j] = skf[ticks + j] if j < recv_f else jnp.zeros_like(skf[0])
        second(last)
        second_share(last)
        finish_fine(last - 1)
        send_pend_c.wait_send()
        send_mix.wait_send()
        finish_fine(last)

    for item in send_norms:
        item.wait_send()
    for t in range(ticks):
        of_1(t).wait_send()
        of_2(t).wait_send()
        of_c(t).wait_send()
    for t in range(last):
        of_farc(t).wait_send()
        send_rawc(t).wait_send()


def put_out_kernel(*refs):
    count = (len(refs) - 1) // 2
    sources, results, sem = refs[:count], refs[count : 2 * count], refs[2 * count]
    given = [
        pltpu.make_async_copy(source, result, sem.at[i])
        for i, (source, result) in enumerate(zip(sources, results))
    ]
    for item in given:
        item.start()
    for item in given:
        item.wait()


def put_out(arrays):
    any_spec = pl.BlockSpec(memory_space=pl.ANY)
    vmem_spec = pl.BlockSpec(memory_space=pltpu.VMEM)
    held = [pltpu.with_memory_space_constraint(a, pltpu.VMEM) for a in arrays]
    return pl.pallas_call(
        put_out_kernel,
        out_shape=tuple(jax.ShapeDtypeStruct(a.shape, a.dtype) for a in arrays),
        in_specs=[vmem_spec] * len(arrays),
        out_specs=(any_spec,) * len(arrays),
        scratch_shapes=[pltpu.SemaphoreType.DMA((len(arrays),))],
    )(*held)


def run_pair(dims, fch, cch, args):
    nseg, ndp, ticks, fside, cside, hold_f, recv_f, hold_c, recv_c = dims
    fcells, ccells = fside * fside, cside * cside
    frows, crows = 2 * fch // LANES, 2 * cch // LANES
    last = ticks - 1
    any_spec = pl.BlockSpec(memory_space=pl.ANY)
    vmem_spec = pl.BlockSpec(memory_space=pltpu.VMEM)
    dma, vmem = pltpu.SemaphoreType.DMA, pltpu.VMEM
    outs = pl.pallas_call(
        functools.partial(pair_kernel, dims),
        out_shape=(
            vmem((ticks, fcells, fch), BF16),
            vmem((ticks, ccells, cch), BF16),
            vmem((hold_f, fcells, fch), BF16),
            vmem((hold_c, ccells, cch), BF16),
        ),
        in_specs=[any_spec] * 7 + [vmem_spec] * 2 + [any_spec] * 2 + [vmem_spec] * 2 + [any_spec] * 2,
        out_specs=(vmem_spec,) * 4,
        scratch_shapes=[
            vmem((2, 9 * fch, fch), BF16),
            vmem((fch, fch), BF16),
            vmem((9 * cch, cch), BF16),
            vmem((cch, cch), BF16),
            vmem((cch, cch), BF16),
            vmem((4 * fch, cch), BF16),
            vmem((cch, 4 * fch), BF16),
            vmem((cch, 2, 2, fch), BF16),
            vmem((fch // LANES, 256, LANES), F32),
            vmem((ticks, fcells, fch), BF16),
            vmem((ccells, cch), BF16),
            vmem((max(hold_f, recv_f) + ticks, fcells, fch), BF16),
            vmem((ccells, cch), BF16),
            vmem((2, fch), F32),
            vmem((2, fch), F32),
            vmem((1, cch), F32),
            vmem((1, cch), F32),
            vmem((ticks, fcells, fch), F32),
            vmem((ticks, fcells, fch), F32),
            vmem((ticks, ccells, cch), F32),
            vmem((fcells, fch), F32),
            vmem((ccells, cch), F32),
            vmem((fch // LANES, cside, 2 * fside, LANES), F32),
            vmem((fcells, 9 * fch), BF16),
            vmem((ccells, 9 * cch), BF16),
            vmem((ccells, 4 * fch), BF16),
            vmem((last, fcells, fch), BF16),
            vmem((last, fcells, fch), BF16),
            vmem((last, ccells, cch), BF16),
            vmem((last, ccells, cch), BF16),
            vmem((ticks, frows, LANES), F32),
            vmem((ticks, frows, LANES), F32),
            vmem((ticks, crows, LANES), F32),
            vmem((ticks, ndp - 1, frows, LANES), F32),
            vmem((ticks, ndp - 1, frows, LANES), F32),
            vmem((ticks, ndp - 1, crows, LANES), F32),
            vmem((last, ndp, frows, LANES), F32),
            vmem((last, ndp, crows, LANES), F32),
            dma((11,)),
            dma((ticks,)), dma((ticks,)), dma((ticks,)), dma((ticks,)), dma((ticks,)), dma((ticks,)),
            dma((last,)), dma((last,)), dma((last,)), dma((last,)),
            dma((last,)), dma((last,)), dma((last,)), dma((last,)),
            dma((ticks,)), dma((ticks,)), dma((6,)), dma((6,)),
        ],
        compiler_params=pltpu.CompilerParams(
            collective_id=0, has_side_effects=True, vmem_limit_bytes=56 << 20
        ),
    )(*args)
    return put_out(outs)


def hand_over_kernel(*refs):
    count = (len(refs) - 2) // 3
    sources, results, held = refs[:count], refs[count : 2 * count], refs[2 * count : 3 * count]
    in_sem, out_sem = refs[3 * count :]
    taken, given = [], []
    for i in range(count):
        for j in range(held[i].shape[0]):
            taken.append(pltpu.make_async_copy(sources[i].at[j], held[i].at[j], in_sem.at[i, j]))
            given.append(pltpu.make_async_copy(held[i].at[j], results[i].at[j], out_sem.at[i, j]))
    for item in taken:
        item.start()
    for item, other in zip(taken, given):
        item.wait()
        other.start()
    for item in given:
        item.wait()


def hand_over(arrays):
    most = max(array.shape[0] for array in arrays)
    any_spec = pl.BlockSpec(memory_space=pl.ANY)
    return pl.pallas_call(
        hand_over_kernel,
        out_shape=tuple(jax.ShapeDtypeStruct(a.shape, a.dtype) for a in arrays),
        in_specs=[any_spec] * len(arrays),
        out_specs=(any_spec,) * len(arrays),
        scratch_shapes=[pltpu.VMEM(a.shape, a.dtype) for a in arrays]
        + [pltpu.SemaphoreType.DMA((len(arrays), most))] * 2,
    )(*arrays)


def on_device(
    fine_inflow, coarse_inflow, fine_entries, fine_pending, coarse_pending,
    fine_kernels, fine_mixing, fine_gains, fine_shifts,
    coarse_kernel, coarse_mixing, coarse_gains, coarse_shifts,
    descent_kernel, upsample_kernel,
):
    nseg = lax.axis_size("segment")
    ndp = lax.axis_size("dp")
    half = nseg // 2
    ticks = fine_entries.shape[0] + 1
    hold_f, hold_c = fine_pending.shape[1], coarse_pending.shape[1]
    recv_f, recv_c = 3 * half - hold_f, half - hold_c
    fside, fch = fine_inflow.shape[3], fine_inflow.shape[4]
    cside, cch = coarse_inflow.shape[3], coarse_inflow.shape[4]
    fcells, ccells = fside * fside, cside * cside
    dims = (nseg, ndp, ticks, fside, cside, hold_f, recv_f, hold_c, recv_c)
    frows, crows = 2 * fch // LANES, 2 * cch // LANES
    any_spec = pl.BlockSpec(memory_space=pl.ANY)
    vmem_spec = pl.BlockSpec(memory_space=pltpu.VMEM)
    dma = pltpu.SemaphoreType.DMA
    args = (
        fine_inflow.reshape(fcells, fch),
        coarse_inflow.reshape(ccells, cch),
        fine_entries.reshape(ticks - 1, fcells, fch),
        fine_pending.reshape(hold_f, fcells, fch),
        coarse_pending.reshape(hold_c, ccells, cch),
        fine_kernels.reshape(2, 9 * fch, fch),
        fine_mixing.reshape(fch, fch),
        fine_gains.reshape(2, fch),
        fine_shifts.reshape(2, fch),
        coarse_kernel.reshape(9 * cch, cch),
        coarse_mixing.reshape(cch, cch),
        coarse_gains.reshape(1, cch),
        coarse_shifts.reshape(1, cch),
        descent_kernel.reshape(4 * fch, cch),
        upsample_kernel,
    )
    if nseg == 2 and recv_f == 1 and recv_c == 0 and ticks > hold_f + recv_f:
        fst, cst, fback, cback = run_pair(dims, fch, cch, args)
    else:
        outs = pl.pallas_call(
            functools.partial(kernel, dims),
            out_shape=(
                jax.ShapeDtypeStruct((ticks, fcells, fch), BF16),
                jax.ShapeDtypeStruct((ticks, ccells, cch), BF16),
                jax.ShapeDtypeStruct((hold_f, fcells, fch), BF16),
                jax.ShapeDtypeStruct((hold_c, ccells, cch), BF16),
            ),
            in_specs=[any_spec] * 7 + [vmem_spec] * 2 + [any_spec] * 2 + [vmem_spec] * 2 + [any_spec] * 2,
            out_specs=(any_spec,) * 4,
            scratch_shapes=[
                pltpu.VMEM((2, 9 * fch, fch), BF16),
                pltpu.VMEM((fch, fch), BF16),
                pltpu.VMEM((9 * cch, cch), BF16),
                pltpu.VMEM((cch, cch), BF16),
                pltpu.VMEM((4 * fch, cch), BF16),
                pltpu.VMEM((cch, 4 * fch), BF16),
                pltpu.VMEM((ticks, fcells, fch), BF16),
                pltpu.VMEM((ticks, ccells, cch), BF16),
                pltpu.VMEM((ticks, ccells, cch), BF16),
                pltpu.VMEM((max(hold_f, recv_f) + ticks, fcells, fch), BF16),
                pltpu.VMEM((max(hold_c, recv_c) + ticks, ccells, cch), BF16),
                pltpu.VMEM((ticks, fcells, fch), BF16),
                pltpu.VMEM((ticks, ccells, cch), BF16),
                pltpu.VMEM((ticks, ccells, cch), BF16),
                pltpu.VMEM((fcells, fch), F32),
                pltpu.VMEM((fcells, fch), F32),
                pltpu.VMEM((fcells, fch), F32),
                pltpu.VMEM((ccells, cch), F32),
                pltpu.VMEM((fch // LANES, cside, 2 * fside, LANES), F32),
                pltpu.VMEM((fcells, 9 * fch), BF16),
                pltpu.VMEM((ccells, 9 * cch), BF16),
                pltpu.VMEM((fcells, fch), BF16),
                pltpu.VMEM((ccells, cch), BF16),
                pltpu.VMEM((2 * ticks, frows, LANES), F32),
                pltpu.VMEM((ticks, crows, LANES), F32),
                pltpu.VMEM((2 * ticks, ndp - 1, frows, LANES), F32),
                pltpu.VMEM((ticks, ndp - 1, crows, LANES), F32),
                pltpu.VMEM((cch, 2, 2, fch), BF16),
                pltpu.VMEM((fch // LANES, 256, LANES), F32),
                dma((12,)),
                dma((4, max(ticks, hold_f, hold_c))),
                dma((ticks,)), dma((ticks,)), dma((ticks,)), dma((ticks,)), dma((ticks,)),
                dma((ticks,)), dma((ticks,)), dma((ticks,)), dma((ticks,)), dma((ticks,)),
                dma((2 * ticks,)), dma((ticks,)), dma((2 * ticks,)), dma((ticks,)),
            ],
            compiler_params=pltpu.CompilerParams(
                collective_id=0, has_side_effects=True, vmem_limit_bytes=56 << 20
            ),
        )(*args)
        fst, cst, fback, cback = hand_over(outs)
    return (
        fst.reshape(1, ticks, 1, fside, fside, fch),
        cst.reshape(1, ticks, 1, cside, cside, cch),
        fback.reshape(1, hold_f, 1, fside, fside, fch),
        cback.reshape(1, hold_c, 1, cside, cside, cch),
    )


def solution(mesh):
    placed = (
        P("segment", "dp", None, None, None),
        P("segment", "dp", None, None, None),
        P(None, "dp", None, None, None),
        P("segment", None, "dp", None, None, None),
        P("segment", None, "dp", None, None, None),
        P("segment", None, None, None, None, None),
        P("segment", None, None),
        P("segment", None, None),
        P("segment", None, None),
        P("segment", None, None, None, None),
        P("segment", None, None),
        P("segment", None),
        P("segment", None),
        P(),
        P(),
    )
    return jax.shard_map(
        on_device,
        mesh=mesh,
        in_specs=placed,
        out_specs=(
            P("segment", None, "dp", None, None, None),
            P("segment", None, "dp", None, None, None),
            P("segment", None, "dp", None, None, None),
            P("segment", None, "dp", None, None, None),
        ),
        check_vma=False,
    )
```

```python
import functools

import jax
import jax.numpy as jnp
from jax import lax
from jax.experimental import pallas as pl
from jax.experimental.pallas import tpu as pltpu
from jax.sharding import PartitionSpec as P

EPSILON = 1e-05
LANES = 128
MESH = pl.DeviceIdType.MESH
F32 = jnp.float32
BF16 = jnp.bfloat16


def dot(a, b):
    return jnp.dot(a, b, preferred_element_type=F32)


def side_shifts(x, side):
    cells = x.shape[0]
    column = lax.rem(lax.broadcasted_iota(jnp.int32, x.shape, 0), side)
    before = jnp.where(column == 0, 0.0, pltpu.roll(x, 1, 0))
    after = jnp.where(column == side - 1, 0.0, pltpu.roll(x, cells - 1, 0))
    return before, x, after


def spread_taps(x, cols, side):
    cells, width = x.shape
    edge = jnp.zeros((side, width), F32)
    for dc, part in enumerate(side_shifts(x, side)):
        above = jnp.concatenate([edge, part[: cells - side]], axis=0)
        below = jnp.concatenate([part[side:], edge], axis=0)
        for dr, moved in enumerate((above, part, below)):
            start = (3 * dr + dc) * width
            cols[:, start : start + width] = moved.astype(BF16)


def put_stats(h, out):
    width = h.shape[1]
    rows = width // LANES
    total = jnp.sum(h, axis=0, keepdims=True)
    square = jnp.sum(h * h, axis=0, keepdims=True)
    for row in range(rows):
        lanes = slice(row * LANES, (row + 1) * LANES)
        out[row : row + 1, :] = total[:, lanes]
        out[rows + row : rows + row + 1, :] = square[:, lanes]


def norm_terms(total, gain, shift, count):
    rows = total.shape[0] // 2
    sums = jnp.concatenate([total[row : row + 1] for row in range(rows)], axis=1)
    squares = jnp.concatenate([total[rows + row : rows + row + 1] for row in range(rows)], axis=1)
    center = sums * (1.0 / count)
    spread = jnp.maximum(squares * (1.0 / count) - center * center, 0.0)
    scale = lax.rsqrt(spread + EPSILON) * gain
    return scale, shift - center * scale


def kernel(
    dims,
    fine_in, coarse_in, entries, fine_pend, coarse_pend,
    wf_hbm, mixf_hbm, fgain, fshift, wc_hbm, mixc_hbm, cgain, cshift, wd_hbm, wu_hbm,
    fst_out, cst_out, fback_out, cback_out,
    wf, mixf, wc, mixc, wd, wu,
    fin, cin, upin, skf, skc, fst, cst, dbuf,
    xs, hf, hg, hc, upscr, colf, colc, zf, zc,
    statf, statc, gotf, gotc,
    wu4, wuf, load_sem, save_sem,
    fin_r, cin_r, up_r, skf_r, skc_r,
    fin_s, cin_s, up_s, skf_s, skc_s,
    gotf_r, gotc_r, statf_s, statc_s,
):
    nseg, ndp, ticks, fside, cside, hold_f, recv_f, hold_c, recv_c = dims
    half = nseg // 2
    seg = lax.axis_index("segment")
    me = lax.axis_index("dp")
    lower = seg < half
    upper = seg >= half
    turn = seg == half - 1
    after = lax.rem(seg + 1, nseg)
    mate = lax.rem(seg + half, nseg)

    def load(k, src, dst):
        return pltpu.make_async_copy(src, dst, load_sem.at[k])

    get_fine = load(0, fine_in, fin.at[0])
    get_wf0 = load(1, wf_hbm.at[0], wf.at[0])
    get_mixf = load(2, mixf_hbm, mixf)
    get_coarse = load(3, coarse_in, cin.at[0])
    get_mixc = load(4, mixc_hbm, mixc)
    get_wc = load(5, wc_hbm, wc)
    get_wf1 = load(6, wf_hbm.at[1], wf.at[1])
    get_wd = load(7, wd_hbm, wd)
    get_wu = load(11, wu_hbm, wu4)
    own_entries = load(8, entries, fin.at[pl.ds(1, ticks - 1)])
    own_fine = hold_f if hold_f > ticks else 0
    own_coarse = hold_c if hold_c > ticks else 0

    def own_pend(k, src, dst, count):
        return load(k, src.at[pl.ds(0, count)], dst.at[pl.ds(0, count)])

    barrier = pltpu.get_barrier_semaphore()
    offsets = sorted({1 % nseg, nseg - 1, half})

    def greet(k, carry):
        pl.semaphore_signal(
            barrier, inc=1, device_id=(seg, lax.rem(me + k, ndp)), device_id_type=MESH
        )
        return carry

    lax.fori_loop(1, ndp, greet, 0)
    for offset in offsets:
        pl.semaphore_signal(
            barrier, inc=1, device_id=(lax.rem(seg + offset, nseg), me), device_id_type=MESH
        )
    @pl.when(upper)
    def _():
        if recv_f:
            own_pend(9, fine_pend, skf, recv_f).start()

    for item in (get_fine, get_wf0, get_mixf, get_coarse, get_mixc, get_wc, get_wf1):
        item.start()

    @pl.when(lower)
    def _():
        if recv_c:
            own_pend(10, coarse_pend, skc, recv_c).start()
        if own_fine:
            own_pend(9, fine_pend, skf, own_fine).start()

    @pl.when(upper)
    def _():
        if own_coarse:
            own_pend(10, coarse_pend, skc, own_coarse).start()

    @pl.when(seg == 0)
    def _():
        own_entries.start()

    @pl.when(turn)
    def _():
        get_wd.start()

    @pl.when(seg == half)
    def _():
        get_wu.start()

    zf[...] = jnp.zeros_like(zf)
    zc[...] = jnp.zeros_like(zc)
    pl.semaphore_wait(barrier, ndp - 1 + len(offsets))

    def push(src, dst, ssem, rsem, to):
        return pltpu.make_async_remote_copy(
            src_ref=src, dst_ref=dst, send_sem=ssem, recv_sem=rsem,
            device_id=(to, me), device_id_type=MESH,
        )

    def send_skf(j):
        return push(skf.at[j], skf.at[recv_f + j], skf_s.at[j], skf_r.at[j], mate)

    def send_pend_f(j):
        return push(fine_pend.at[j], skf.at[recv_f + j], skf_s.at[j], skf_r.at[j], mate)

    def send_pend_c(j):
        return push(coarse_pend.at[j], skc.at[recv_c + j], skc_s.at[j], skc_r.at[j], mate)

    def send_skc(j):
        return push(skc.at[j], skc.at[recv_c + j], skc_s.at[j], skc_r.at[j], mate)

    def send_up(t):
        return push(cst.at[t], upin.at[t], up_s.at[t], up_r.at[t], after)

    def send_co(t):
        return push(cst.at[t], cin.at[t + 1], cin_s.at[t], cin_r.at[t], after)

    def send_down(t):
        return push(dbuf.at[t], cin.at[t + 1], cin_s.at[t], cin_r.at[t], after)

    def send_fo(t):
        return push(fst.at[t], fin.at[t + 1], fin_s.at[t], fin_r.at[t], after)

    def exchange(src, dst, ssem, rsem):
        def one(k, carry):
            pltpu.make_async_remote_copy(
                src_ref=src, dst_ref=dst.at[k - 1], send_sem=ssem, recv_sem=rsem,
                device_id=(seg, lax.rem(me + k, ndp)), device_id_type=MESH,
            ).start()
            return carry

        lax.fori_loop(1, ndp, one, 0)

    def whole(dst, ssem, rsem):
        return pltpu.make_async_remote_copy(
            src_ref=dst, dst_ref=dst, send_sem=ssem, recv_sem=rsem,
            device_id=(seg, lax.rem(me + 1, ndp)), device_id_type=MESH,
        )

    @pl.when(lower)
    def _():
        for j in range(min(hold_f, ticks)):
            send_pend_f(j).start()

    @pl.when(upper)
    def _():
        for j in range(min(hold_c, ticks)):
            send_pend_c(j).start()

    fcount = ndp * fside * fside
    ccount = ndp * cside * cside

    def save_f(t):
        return pltpu.make_async_copy(fst.at[t], fst_out.at[t], save_sem.at[0, t])

    def save_c(t):
        return pltpu.make_async_copy(cst.at[t], cst_out.at[t], save_sem.at[1, t])

    def first(t, *items):
        @pl.when(t == 0)
        def _():
            for item in items:
                item.wait()

    def front(t):
        first(t, get_fine, get_mixf)

        @pl.when(lower)
        def _():
            @pl.when(jnp.logical_and(seg > 0, t > 0))
            def _():
                send_fo(t - 1).wait_recv()

            xs[...] = fin[t].astype(F32)

        @pl.when(upper)
        def _():
            @pl.when(jnp.logical_and(seg == half, t > 0))
            def _():
                send_up(t - 1).wait_recv()
                spread = dot(upin[t - 1], wu[...])
                width = spread.shape[1] // 4
                for a in range(2):
                    for c in range(2):
                        start = (2 * a + c) * width
                        part = spread[:, start : start + width].reshape(cside, cside, width)
                        for i in range(width // LANES):
                            lanes = slice(i * LANES, (i + 1) * LANES)
                            upscr[i, :, pl.ds(a * fside + c, cside, stride=2), :] = part[:, :, lanes]
                for i in range(width // LANES):
                    lanes = slice(i * LANES, (i + 1) * LANES)
                    fin[t, :, lanes] = upscr[i].reshape(fside * fside, LANES).astype(BF16)

            @pl.when(jnp.logical_and(seg != half, t > 0))
            def _():
                send_fo(t - 1).wait_recv()

            if recv_f:
                first(t, own_pend(9, fine_pend, skf, recv_f))

            @pl.when(t >= recv_f)
            def _():
                send_skf(t - recv_f).wait_recv()

            xs[...] = (dot(fin[t], mixf[...]) + skf[t].astype(F32)).astype(BF16).astype(F32)

        spread_taps(xs[...], colf, fside)
        first(t, get_wf0)
        hf[...] = dot(colf[...], wf[0])
        put_stats(hf[...], statf.at[2 * t])
        exchange(statf.at[2 * t], gotf.at[2 * t], statf_s.at[2 * t], gotf_r.at[2 * t])

    def later(which, t):
        @pl.when(jnp.logical_and(which, t < ticks - 1))
        def _():
            front(t + 1)

    def own_pieces(t):
        @pl.when(t == 0)
        def _():
            get_wf1.wait()

            @pl.when(turn)
            def _():
                get_wd.wait()

            @pl.when(seg == 0)
            def _():
                own_entries.wait()

            @pl.when(seg == half)
            def _():
                get_wu.wait()
                width = wu4.shape[3]
                depth = wuf.shape[1] // 4

                def rows_of(n, carry):
                    rows = pl.multiple_of(n * depth, depth)
                    piece = wu4[pl.ds(rows, depth)].astype(F32).reshape(4 * depth, width)
                    for i in range(width // LANES):
                        wuf[i] = piece[:, i * LANES : (i + 1) * LANES]
                    for q in range(4):
                        for i in range(width // LANES):
                            start = q * width + i * LANES
                            part = wuf[i, pl.ds(q, depth, stride=4), :]
                            wu[pl.ds(rows, depth), start : start + LANES] = part.astype(BF16)
                    return carry

                lax.fori_loop(0, wu4.shape[0] // depth, rows_of, 0)

    front(jnp.int32(0))
    own_pieces(jnp.int32(0))

    def tick(t, carry):
        first(t, get_coarse, get_mixc)

        @pl.when(t > 0)
        def _():
            send_co(t - 1).wait_recv()

        @pl.when(lower)
        def _():
            if recv_c:
                first(t, own_pend(10, coarse_pend, skc, recv_c))

            @pl.when(t >= recv_c)
            def _():
                send_skc(t - recv_c).wait_recv()

            hc[...] = (dot(cin[t], mixc[...]) + skc[t].astype(F32)).astype(BF16).astype(F32)

        @pl.when(upper)
        def _():
            hc[...] = cin[t].astype(F32)

        spread_taps(hc[...], colc, cside)
        first(t, get_wc)
        hc[...] = dot(colc[...], wc[...])
        put_stats(hc[...], statc.at[t])
        exchange(statc.at[t], gotc.at[t], statc_s.at[t], gotc_r.at[t])

        whole(gotf.at[2 * t], statf_s.at[2 * t], gotf_r.at[2 * t]).wait_recv()
        total = statf[2 * t] + jnp.sum(gotf[2 * t], axis=0)
        scale, offset = norm_terms(total, fgain[0:1, :], fshift[0:1, :], fcount)
        xs[...] = jnp.maximum(hf[...] * scale + offset, 0.0).astype(BF16).astype(F32)
        spread_taps(xs[...], colf, fside)
        hg[...] = dot(colf[...], wf[1])
        put_stats(hg[...], statf.at[2 * t + 1])
        exchange(
            statf.at[2 * t + 1], gotf.at[2 * t + 1], statf_s.at[2 * t + 1], gotf_r.at[2 * t + 1]
        )

        whole(gotc.at[t], statc_s.at[t], gotc_r.at[t]).wait_recv()
        total = statc[t] + jnp.sum(gotc[t], axis=0)
        scale, offset = norm_terms(total, cgain[...], cshift[...], ccount)
        cst[t] = jnp.maximum(hc[...] * scale + offset, 0.0).astype(BF16)

        @pl.when(t < ticks - 1)
        def _():
            @pl.when(turn)
            def _():
                send_up(t).start()

            @pl.when(jnp.logical_not(turn))
            def _():
                send_co(t).start()

        save_c(t).start()

        @pl.when(upper)
        def _():
            skc[hold_c + t] = dot(cst[t], mixc[...]).astype(BF16)

            @pl.when(hold_c + t < ticks)
            def _():
                send_skc(hold_c + t).start()

        later(seg == 0, t)

        whole(gotf.at[2 * t + 1], statf_s.at[2 * t + 1], gotf_r.at[2 * t + 1]).wait_recv()
        total = statf[2 * t + 1] + jnp.sum(gotf[2 * t + 1], axis=0)
        scale, offset = norm_terms(total, fgain[1:2, :], fshift[1:2, :], fcount)
        fst[t] = jnp.maximum(hg[...] * scale + offset, 0.0).astype(BF16)

        @pl.when(t < ticks - 1)
        def _():
            @pl.when(turn)
            def _():
                width = fst.shape[2]
                for i in range(width // LANES):
                    lanes = slice(i * LANES, (i + 1) * LANES)
                    upscr[i] = fst[t, :, lanes].astype(F32).reshape(cside, 2 * fside, LANES)
                lowered = None
                for a in range(2):
                    for c in range(2):
                        for i in range(width // LANES):
                            part = upscr[i, :, pl.ds(a * fside + c, cside, stride=2), :]
                            part = part.reshape(cside * cside, LANES).astype(BF16)
                            start = (2 * a + c) * width + i * LANES
                            term = dot(part, wd[start : start + LANES, :])
                            lowered = term if lowered is None else lowered + term
                dbuf[t] = lowered.astype(BF16)
                send_down(t).start()

            @pl.when(jnp.logical_and(jnp.logical_not(turn), seg < nseg - 1))
            def _():
                send_fo(t).start()

        save_f(t).start()

        @pl.when(lower)
        def _():
            skf[hold_f + t] = dot(fst[t], mixf[...]).astype(BF16)

            @pl.when(hold_f + t < ticks)
            def _():
                send_skf(hold_f + t).start()

        later(seg > 0, t)
        return carry

    lax.fori_loop(0, ticks, tick, 0)

    def back_f(first, src):
        return pltpu.make_async_copy(src, fback_out.at[first], save_sem.at[2, first])

    def back_c(first, src):
        return pltpu.make_async_copy(src, cback_out.at[first], save_sem.at[3, first])

    lower_backs = [back_f(j, skf.at[ticks + j]) for j in range(hold_f)]
    lower_backs += [
        back_c(j, skc.at[ticks + j] if j < recv_c else zc) for j in range(hold_c)
    ]
    upper_backs = [
        back_f(j, skf.at[ticks + j] if j < recv_f else zf) for j in range(hold_f)
    ]
    upper_backs += [back_c(j, skc.at[ticks + j]) for j in range(hold_c)]

    @pl.when(lower)
    def _():
        if own_fine:
            own_pend(9, fine_pend, skf, own_fine).wait()
        for j in range(max(ticks - recv_c, 0), ticks):
            send_skc(j).wait_recv()
        for item in lower_backs:
            item.start()
        for j in range(ticks):
            send_skf(j).wait_send()
        for item in lower_backs:
            item.wait()

    @pl.when(upper)
    def _():
        if own_coarse:
            own_pend(10, coarse_pend, skc, own_coarse).wait()
        for j in range(max(ticks - recv_f, 0), ticks):
            send_skf(j).wait_recv()
        for item in upper_backs:
            item.start()
        for j in range(ticks):
            send_skc(j).wait_send()
        for item in upper_backs:
            item.wait()

    @pl.when(turn)
    def _():
        for t in range(ticks - 1):
            send_up(t).wait_send()

    @pl.when(jnp.logical_and(jnp.logical_not(turn), seg < nseg - 1))
    def _():
        for t in range(ticks - 1):
            send_fo(t).wait_send()

    for t in range(ticks - 1):
        send_co(t).wait_send()
    for t in range(ticks):
        whole(gotf.at[2 * t], statf_s.at[2 * t], gotf_r.at[2 * t]).wait_send()
        whole(gotf.at[2 * t + 1], statf_s.at[2 * t + 1], gotf_r.at[2 * t + 1]).wait_send()
        whole(gotc.at[t], statc_s.at[t], gotc_r.at[t]).wait_send()
        save_f(t).wait()
        save_c(t).wait()


def sums_of(total):
    rows = total.shape[0] // 2
    sums = jnp.concatenate([total[row : row + 1] for row in range(rows)], axis=1)
    squares = jnp.concatenate([total[rows + row : rows + row + 1] for row in range(rows)], axis=1)
    return sums, squares


def moments(total, count):
    sums, squares = sums_of(total)
    center = sums * (1.0 / count)
    spread = jnp.maximum(squares * (1.0 / count) - center * center, 0.0)
    return center, lax.rsqrt(spread + EPSILON)


def pair_kernel(
    dims,
    fine_in, coarse_in, entries, fine_pend, coarse_pend,
    wf_hbm, mixf_hbm, fgain, fshift, wc_hbm, mixc_hbm, cgain, cshift, wd_hbm, wu_hbm,
    fst, cst, fback, cback,
    wf, mixf, wc, mixc, mixm, wd, wu, wu4, wuf,
    fin, cin, skf, skc, dbuf, co_in, mate_fgain, mate_fshift, mate_cgain, mate_cshift,
    hf, hc, xs, hx, upscr, colf, colc, cold,
    rawf_out, rawf_in, rawc_out, rawc_in,
    stf, stc, gotf, gotc, farf, farc,
    load_sem, sf, rf, sc, rc, sfarf, rfarf, sfarc, rfarc,
    srawf, rrawf, srawc, rrawc, skf_s, skf_r, dbuf_s, dbuf_r, co_s, co_r, one_s, one_r, ready,
):
    nseg, ndp, ticks, fside, cside, hold_f, recv_f, hold_c, recv_c = dims
    seg = lax.axis_index("segment")
    me = lax.axis_index("dp")
    other = 1 - seg
    lower = seg == 0
    upper = seg == 1
    fcells, ccells = fside * fside, cside * cside
    fcount, ccount = ndp * fcells, ndp * ccells
    last = ticks - 1

    barrier = pltpu.get_barrier_semaphore()

    def load(k, src, dst):
        return pltpu.make_async_copy(src, dst, load_sem.at[k])

    get_fine = load(0, fine_in, fin.at[0])
    get_wf0 = load(1, wf_hbm.at[0], wf.at[0])
    get_mixf = load(2, mixf_hbm, mixf)
    get_coarse = load(3, coarse_in, cin)
    get_mixc = load(4, mixc_hbm, mixc)
    get_wc = load(5, wc_hbm, wc)
    get_wf1 = load(6, wf_hbm.at[1], wf.at[1])
    get_wd = load(7, wd_hbm, wd)
    get_entries = load(8, entries, fin.at[pl.ds(1, last)])
    get_pend = load(9, fine_pend.at[pl.ds(0, recv_f)], skf.at[pl.ds(0, recv_f)])
    get_wu = load(10, wu_hbm, wu4)

    get_fine.start()

    @pl.when(upper)
    def _():
        get_mixf.start()
        get_pend.start()

    get_wf0.start()

    bits = ndp.bit_length() - 1

    def partner(k):
        if 1 << bits != ndp:
            return lax.rem(me + k, ndp)
        to = 0
        for b in range(bits):
            bit = lax.rem(lax.div(me, 1 << b), 2)
            to = to + (1 << b) * (1 - bit if (k >> b) & 1 else bit)
        return to

    partners = [partner(k) for k in range(ndp)]
    twin = me + 1 - 2 * lax.rem(me, 2)
    for k in range(ndp - 1, 0, -1):
        pl.semaphore_signal(barrier, inc=1, device_id=(seg, partners[k]), device_id_type=MESH)
    pl.semaphore_signal(barrier, inc=1, device_id=(other, me), device_id_type=MESH)

    @pl.when(lower)
    def _():
        for item in (get_entries, get_wf1, get_mixf, get_coarse, get_mixc, get_wc, get_wd):
            item.start()

    @pl.when(upper)
    def _():
        for item in (get_coarse, get_wc, get_wf1, get_wd, get_wu, get_mixc):
            item.start()

    def push(src, dst, ssem, rsem):
        return pltpu.make_async_remote_copy(
            src_ref=src, dst_ref=dst, send_sem=ssem, recv_sem=rsem,
            device_id=(other, me), device_id_type=MESH,
        )

    def share(src, dst, ssem, rsem):
        for k in range(ndp - 1, 0, -1):
            pltpu.make_async_remote_copy(
                src_ref=src, dst_ref=dst.at[k - 1], send_sem=ssem, recv_sem=rsem,
                device_id=(seg, partners[k]), device_id_type=MESH,
            ).start()

    def cast_far(src, dst, ssem, rsem):
        for k in range(ndp - 1, -1, -1):
            pltpu.make_async_remote_copy(
                src_ref=src, dst_ref=dst.at[k], send_sem=ssem, recv_sem=rsem,
                device_id=(other, partners[k]), device_id_type=MESH,
            ).start()

    def of_f(n):
        return push(gotf.at[n], gotf.at[n], sf.at[n], rf.at[n])

    def of_c(t):
        return push(gotc.at[t], gotc.at[t], sc.at[t], rc.at[t])

    of_farf = push(farf, farf, sfarf, rfarf)
    send_rawf = push(rawf_out, rawf_in, srawf, rrawf)

    def of_farc(t):
        return push(farc.at[t], farc.at[t], sfarc.at[t], rfarc.at[t])

    def send_down(t):
        return push(dbuf.at[t], dbuf.at[t], dbuf_s.at[t], dbuf_r.at[t])

    def send_rawc(t):
        return push(rawc_out.at[t], rawc_in.at[t], srawc.at[t], rrawc.at[t])

    def send_co(t):
        return push(cst.at[t], co_in.at[t], co_s.at[t], co_r.at[t])

    def send_skf(j):
        return push(skf.at[j], skf.at[recv_f + j], skf_s.at[j], skf_r.at[j])

    def send_pend_f(j):
        return push(fine_pend.at[j], skf.at[recv_f + j], skf_s.at[j], skf_r.at[j])

    send_pend_c = push(coarse_pend.at[0], skc, one_s.at[0], one_r.at[0])
    part = mixm.shape[0] // 2
    own_rows = pl.ds(pl.multiple_of(lax.rem(me, 2) * part, part), part)
    twin_rows = pl.ds(pl.multiple_of(lax.rem(twin, 2) * part, part), part)
    send_mix = push(mixc_hbm.at[own_rows], mixm.at[own_rows], one_s.at[1], one_r.at[1])

    def hand_mix(rows):
        return pltpu.make_async_remote_copy(
            src_ref=mixm.at[rows], dst_ref=mixm.at[rows],
            send_sem=one_s.at[6], recv_sem=one_r.at[6],
            device_id=(seg, twin), device_id_type=MESH,
        )

    send_norms = [
        push(fgain, mate_fgain, one_s.at[2], one_r.at[2]),
        push(fshift, mate_fshift, one_s.at[3], one_r.at[3]),
        push(cgain, mate_cgain, one_s.at[4], one_r.at[4]),
        push(cshift, mate_cshift, one_s.at[5], one_r.at[5]),
    ]

    def conv_fine(layer, out):
        spread_taps(xs[...], colf, fside)
        out[...] = dot(colf[...], wf[layer])

    def conv_coarse(out):
        spread_taps(hx[...], colc, cside)
        out[...] = dot(colc[...], wc[...])

    def centred(h, stats, cells):
        sums, _ = sums_of(stats)
        return (h - sums * (1.0 / cells)).astype(BF16)

    def arrived(raw, got, gain, shift, count, cells):
        center, inverse = moments(jnp.sum(got[...], axis=0), count)
        own, _ = sums_of(got[0])
        scale = inverse * gain
        offset = shift + (own * (1.0 / cells) - center) * scale
        return jnp.maximum(raw[...].astype(F32) * scale + offset, 0.0).astype(BF16)

    def descended(x):
        width = x.shape[1]
        for i in range(width // LANES):
            lanes = slice(i * LANES, (i + 1) * LANES)
            upscr[i] = x[:, lanes].reshape(cside, 2 * fside, LANES)
        for a in range(2):
            for c in range(2):
                for i in range(width // LANES):
                    piece = upscr[i, :, pl.ds(a * fside + c, cside, stride=2), :]
                    start = (2 * a + c) * width + i * LANES
                    cold[:, start : start + LANES] = piece.reshape(ccells, LANES).astype(BF16)
        return dot(cold[...], wd[...]).astype(BF16)

    def normed(h, stats, got, gain, shift, count):
        scale, offset = norm_terms(stats[...] + jnp.sum(got[...], axis=0), gain, shift, count)
        return jnp.maximum(h[...] * scale + offset, 0.0).astype(BF16)

    def share_fine(n):
        share(stf.at[n], gotf.at[n], sf.at[n], rf.at[n])

    def conv_stats(layer, n):
        conv_fine(layer, hf.at[n])
        put_stats(hf[n], stf.at[n])

    def take_first(t):
        of_f(t).wait_recv()
        xs[...] = normed(
            hf.at[t], stf.at[t], gotf.at[t], fgain[0:1, :], fshift[0:1, :], fcount
        ).astype(F32)

    def finish_fine(t):
        n = ticks + t
        of_f(n).wait_recv()
        fst[t] = normed(hf.at[n], stf.at[n], gotf.at[n], fgain[1:2, :], fshift[1:2, :], fcount)

    def finish_coarse(t):
        of_c(t).wait_recv()
        cst[t] = normed(hc.at[t], stc.at[t], gotc.at[t], cgain[...], cshift[...], ccount)

    def coarse(t, raw):
        conv_coarse(hc.at[t])
        put_stats(hc[t], stc.at[t])

        @pl.when(raw)
        def _():
            cast_far(stc.at[t], farc.at[t], sfarc.at[t], rfarc.at[t])
            rawc_out[t] = centred(hc[t], stc[t], ccells)
            send_rawc(t).start()

        share(stc.at[t], gotc.at[t], sc.at[t], rc.at[t])

    def mate_coarse(t):
        of_farc(t).wait_recv()
        send_rawc(t).wait_recv()
        return arrived(rawc_in.at[t], farc.at[t], mate_cgain[...], mate_cshift[...], ccount, ccells)

    get_fine.wait()

    @pl.when(lower)
    def _():
        xs[...] = fin[0].astype(F32)

    @pl.when(upper)
    def _():
        get_mixf.wait()
        get_pend.wait()
        xs[...] = (dot(fin[0], mixf[...]) + skf[0].astype(F32)).astype(BF16).astype(F32)

    get_wf0.wait()
    conv_stats(0, 0)
    pl.semaphore_wait(barrier, ndp)
    share_fine(0)
    pl.semaphore_signal(ready, inc=1, device_id=(other, me), device_id_type=MESH)

    @pl.when(lower)
    def _():
        for j in range(hold_f):
            send_pend_f(j).start()
        for item in send_norms:
            item.start()
        get_entries.wait()

        def early(t, carry):
            xs[...] = fin[t].astype(F32)
            conv_stats(0, t)
            share_fine(t)
            return carry

        lax.fori_loop(1, ticks, early, 0)
        for item in (get_wf1, get_mixf, get_coarse, get_mixc, get_wc, get_wd):
            item.wait()
        pl.semaphore_wait(ready, 1)

        def term(t, carry):
            finish_fine(t)

            @pl.when(jnp.logical_and(t > 0, t < last))
            def _():
                dbuf[t] = descended(fst[t].astype(F32))
                send_down(t).start()

            fresh = dot(fst[t], mixf[...]).astype(BF16)

            @pl.when(hold_f + t < ticks)
            def _():
                skf[hold_f + t] = fresh

                @pl.when(t == 0)
                def _():
                    send_skf(hold_f).start()

            @pl.when(hold_f + t >= ticks)
            def _():
                fback[hold_f + t - ticks] = fresh

            return carry

        def encode(i, carry):
            t = jnp.maximum(i - last + 1, 0)

            @pl.when(i < ticks)
            def _():
                take_first(i)
                conv_stats(1, ticks + i)

                @pl.when(i == 0)
                def _():
                    cast_far(stf.at[ticks], farf, sfarf, rfarf)
                    rawf_out[...] = centred(hf[ticks], stf[ticks], fcells)
                    send_rawf.start()

                share_fine(ticks + i)

            @pl.when(i == last - 1)
            def _():
                send_mix.wait_recv()
                hand_mix(own_rows).start()

            @pl.when(i == 0)
            def _():
                send_pend_c.wait_recv()
                hx[...] = (dot(cin[...], mixc[...]) + skc[...].astype(F32)).astype(BF16).astype(F32)

            def mixed(taken):
                fresh = dot(taken, mixm[...]).astype(BF16)
                hx[...] = (dot(taken, mixc[...]) + fresh.astype(F32)).astype(BF16).astype(F32)

            @pl.when(i == last)
            def _():
                term(0, 0)
                hand_mix(twin_rows).wait_recv()
                for item in send_norms:
                    item.wait_recv()
                send_co(0).wait_recv()
                mixed(co_in[0])

            @pl.when(i > last)
            def _():
                finish_coarse(t - 1)

                @pl.when(t < last)
                def _():
                    send_co(t - 1).start()

                mixed(mate_coarse(t - 1))

            @pl.when(jnp.logical_or(i == 0, i >= last))
            def _():
                coarse(t, t == last - 1)

            @pl.when(i == last)
            def _():
                finish_coarse(0)
                send_co(0).start()
                lax.fori_loop(1, ticks, term, 0)

            @pl.when(t == last - 1)
            def _():
                for j in range(hold_f + 1, ticks):
                    send_skf(j).start()

            return carry

        lax.fori_loop(0, 2 * ticks - 2, encode, 0)
        cback[...] = jnp.zeros_like(cback)
        finish_coarse(last)
        of_farf.wait_send()
        send_rawf.wait_send()
        hand_mix(own_rows).wait_send()
        of_farc(last - 1).wait_send()
        send_rawc(last - 1).wait_send()
        for t in range(last - 1):
            send_co(t).wait_send()
        for t in range(1, last):
            send_down(t).wait_send()
        for j in range(ticks):
            send_skf(j).wait_send()

    @pl.when(upper)
    def _():
        send_pend_c.start()
        send_mix.start()
        for item in send_norms:
            item.start()
        for item in (get_coarse, get_wc, get_wf1, get_wd, get_wu, get_mixc):
            item.wait()

        def spread_weights():
            width = wu4.shape[3]
            depth = wuf.shape[1] // 4

            def rows_of(n, carry):
                rows = pl.multiple_of(n * depth, depth)
                piece = wu4[pl.ds(rows, depth)].astype(F32).reshape(4 * depth, width)
                for i in range(width // LANES):
                    wuf[i] = piece[:, i * LANES : (i + 1) * LANES]
                for q in range(4):
                    for i in range(width // LANES):
                        start = q * width + i * LANES
                        part = wuf[i, pl.ds(q, depth, stride=4), :]
                        wu[pl.ds(rows, depth), start : start + LANES] = part.astype(BF16)
                return carry

            lax.fori_loop(0, wu4.shape[0] // depth, rows_of, 0)

        pl.semaphore_wait(ready, 1)

        def encode(t, carry):
            @pl.when(t == 0)
            def _():
                hx[...] = cin[...].astype(F32)

            @pl.when(t == 1)
            def _():
                for item in send_norms:
                    item.wait_recv()
                of_farf.wait_recv()
                send_rawf.wait_recv()
                taken = arrived(
                    rawf_in, farf, mate_fgain[1:2, :], mate_fshift[1:2, :], fcount, fcells
                )
                hx[...] = descended(taken.astype(F32)).astype(F32)

            @pl.when(t > 1)
            def _():
                send_down(t - 1).wait_recv()
                hx[...] = dbuf[t - 1].astype(F32)

            coarse(t, jnp.logical_and(t > 0, t < last))
            return carry

        def raised(taken, t):
            spread = dot(taken, wu[...])
            width = spread.shape[1] // 4
            for a in range(2):
                for c in range(2):
                    start = (2 * a + c) * width
                    part = spread[:, start : start + width].reshape(cside, cside, width)
                    for i in range(width // LANES):
                        lanes = slice(i * LANES, (i + 1) * LANES)
                        upscr[i, :, pl.ds(a * fside + c, cside, stride=2), :] = part[:, :, lanes]
            for i in range(width // LANES):
                lanes = slice(i * LANES, (i + 1) * LANES)
                fin[t, :, lanes] = upscr[i].reshape(fcells, LANES).astype(BF16)
            xs[...] = (dot(fin[t], mixf[...]) + skf[t].astype(F32)).astype(BF16).astype(F32)

        def step(o, carry):
            coarse_end = jnp.where(o < 2, o + 1, jnp.where(o == 2, ticks, o))
            lax.fori_loop(o, coarse_end, encode, 0)
            half_o = lax.div(o, 2)
            odd = lax.rem(o, 2) == 1
            is_first = jnp.logical_or(
                o == 1, jnp.logical_and(jnp.logical_and(o > 1, o < 2 * last), jnp.logical_not(odd))
            )
            t = jnp.where(
                o == 0, 0, jnp.where(is_first, jnp.where(o == 1, 1, half_o + 1),
                                     jnp.where(o == 2 * last, last, half_o))
            )

            @pl.when(o == 0)
            def _():
                spread_weights()

            @pl.when(o == 1)
            def _():
                finish_fine(0)

            @pl.when(o == 2)
            def _():
                finish_coarse(1)

            @pl.when(is_first)
            def _():
                send_skf(t - recv_f).wait_recv()

                @pl.when(t < last)
                def _():
                    send_co(t - 1).wait_recv()
                    raised(co_in[t - 1], t)

                @pl.when(t == last)
                def _():
                    raised(mate_coarse(t - 1), t)

            @pl.when(jnp.logical_not(is_first))
            def _():
                take_first(t)

            layer = jnp.where(is_first, 0, 1)
            n = layer * ticks + t
            conv_stats(layer, n)
            share_fine(n)

            @pl.when(o == 0)
            def _():
                finish_coarse(0)
                send_co(0).start()

            @pl.when(o == 2 * last - 2)
            def _():
                def rest(n, c):
                    finish_coarse(n)
                    return c

                lax.fori_loop(2, ticks, rest, 0)
                cback[0] = dot(cst[last], mixc[...]).astype(BF16)

                def rest_fine(n, c):
                    finish_fine(n)
                    return c

                lax.fori_loop(1, last - 1, rest_fine, 0)
                for j in range(max(ticks - recv_f, 0), ticks):
                    send_skf(j).wait_recv()
                for j in range(hold_f):
                    fback[j] = skf[ticks + j] if j < recv_f else jnp.zeros_like(skf[0])

            return carry

        lax.fori_loop(0, 2 * ticks - 1, step, 0)
        finish_fine(last - 1)
        send_pend_c.wait_send()
        send_mix.wait_send()
        send_co(0).wait_send()
        for t in range(1, last):
            of_farc(t).wait_send()
            send_rawc(t).wait_send()
        finish_fine(last)

    for item in send_norms:
        item.wait_send()
    for t in range(ticks):
        of_f(t).wait_send()
        of_f(ticks + t).wait_send()
        of_c(t).wait_send()


def put_out_kernel(*refs):
    count = (len(refs) - 1) // 2
    sources, results, sem = refs[:count], refs[count : 2 * count], refs[2 * count]
    given = [
        pltpu.make_async_copy(source, result, sem.at[i])
        for i, (source, result) in enumerate(zip(sources, results))
    ]
    for item in given:
        item.start()
    for item in given:
        item.wait()


def put_out(arrays):
    any_spec = pl.BlockSpec(memory_space=pl.ANY)
    vmem_spec = pl.BlockSpec(memory_space=pltpu.VMEM)
    held = [pltpu.with_memory_space_constraint(a, pltpu.VMEM) for a in arrays]
    return pl.pallas_call(
        put_out_kernel,
        out_shape=tuple(jax.ShapeDtypeStruct(a.shape, a.dtype) for a in arrays),
        in_specs=[vmem_spec] * len(arrays),
        out_specs=(any_spec,) * len(arrays),
        scratch_shapes=[pltpu.SemaphoreType.DMA((len(arrays),))],
    )(*held)


def run_pair(dims, fch, cch, args):
    nseg, ndp, ticks, fside, cside, hold_f, recv_f, hold_c, recv_c = dims
    fcells, ccells = fside * fside, cside * cside
    frows, crows = 2 * fch // LANES, 2 * cch // LANES
    last = ticks - 1
    any_spec = pl.BlockSpec(memory_space=pl.ANY)
    vmem_spec = pl.BlockSpec(memory_space=pltpu.VMEM)
    dma, vmem = pltpu.SemaphoreType.DMA, pltpu.VMEM
    outs = pl.pallas_call(
        functools.partial(pair_kernel, dims),
        out_shape=(
            vmem((ticks, fcells, fch), BF16),
            vmem((ticks, ccells, cch), BF16),
            vmem((hold_f, fcells, fch), BF16),
            vmem((hold_c, ccells, cch), BF16),
        ),
        in_specs=[any_spec] * 7 + [vmem_spec] * 2 + [any_spec] * 2 + [vmem_spec] * 2 + [any_spec] * 2,
        out_specs=(vmem_spec,) * 4,
        scratch_shapes=[
            vmem((2, 9 * fch, fch), BF16),
            vmem((fch, fch), BF16),
            vmem((9 * cch, cch), BF16),
            vmem((cch, cch), BF16),
            vmem((cch, cch), BF16),
            vmem((4 * fch, cch), BF16),
            vmem((cch, 4 * fch), BF16),
            vmem((cch, 2, 2, fch), BF16),
            vmem((fch // LANES, 256, LANES), F32),
            vmem((ticks, fcells, fch), BF16),
            vmem((ccells, cch), BF16),
            vmem((max(hold_f, recv_f) + ticks, fcells, fch), BF16),
            vmem((ccells, cch), BF16),
            vmem((ticks, ccells, cch), BF16),
            vmem((last, ccells, cch), BF16),
            vmem((2, fch), F32),
            vmem((2, fch), F32),
            vmem((1, cch), F32),
            vmem((1, cch), F32),
            vmem((2 * ticks, fcells, fch), F32),
            vmem((ticks, ccells, cch), F32),
            vmem((fcells, fch), F32),
            vmem((ccells, cch), F32),
            vmem((fch // LANES, cside, 2 * fside, LANES), F32),
            vmem((fcells, 9 * fch), BF16),
            vmem((ccells, 9 * cch), BF16),
            vmem((ccells, 4 * fch), BF16),
            vmem((fcells, fch), BF16),
            vmem((fcells, fch), BF16),
            vmem((last, ccells, cch), BF16),
            vmem((last, ccells, cch), BF16),
            vmem((2 * ticks, frows, LANES), F32),
            vmem((ticks, crows, LANES), F32),
            vmem((2 * ticks, ndp - 1, frows, LANES), F32),
            vmem((ticks, ndp - 1, crows, LANES), F32),
            vmem((ndp, frows, LANES), F32),
            vmem((last, ndp, crows, LANES), F32),
            dma((11,)),
            dma((2 * ticks,)), dma((2 * ticks,)), dma((ticks,)), dma((ticks,)),
            dma, dma, dma((last,)), dma((last,)),
            dma, dma, dma((last,)), dma((last,)),
            dma((ticks,)), dma((ticks,)), dma((ticks,)), dma((ticks,)), dma((ticks,)), dma((ticks,)),
            dma((7,)), dma((7,)),
            pltpu.SemaphoreType.REGULAR,
        ],
        compiler_params=pltpu.CompilerParams(
            collective_id=0, has_side_effects=True, vmem_limit_bytes=56 << 20
        ),
    )(*args)
    return put_out(outs)


def hand_over_kernel(*refs):
    count = (len(refs) - 2) // 3
    sources, results, held = refs[:count], refs[count : 2 * count], refs[2 * count : 3 * count]
    in_sem, out_sem = refs[3 * count :]
    taken, given = [], []
    for i in range(count):
        for j in range(held[i].shape[0]):
            taken.append(pltpu.make_async_copy(sources[i].at[j], held[i].at[j], in_sem.at[i, j]))
            given.append(pltpu.make_async_copy(held[i].at[j], results[i].at[j], out_sem.at[i, j]))
    for item in taken:
        item.start()
    for item, other in zip(taken, given):
        item.wait()
        other.start()
    for item in given:
        item.wait()


def hand_over(arrays):
    most = max(array.shape[0] for array in arrays)
    any_spec = pl.BlockSpec(memory_space=pl.ANY)
    return pl.pallas_call(
        hand_over_kernel,
        out_shape=tuple(jax.ShapeDtypeStruct(a.shape, a.dtype) for a in arrays),
        in_specs=[any_spec] * len(arrays),
        out_specs=(any_spec,) * len(arrays),
        scratch_shapes=[pltpu.VMEM(a.shape, a.dtype) for a in arrays]
        + [pltpu.SemaphoreType.DMA((len(arrays), most))] * 2,
    )(*arrays)


def on_device(
    fine_inflow, coarse_inflow, fine_entries, fine_pending, coarse_pending,
    fine_kernels, fine_mixing, fine_gains, fine_shifts,
    coarse_kernel, coarse_mixing, coarse_gains, coarse_shifts,
    descent_kernel, upsample_kernel,
):
    nseg = lax.axis_size("segment")
    ndp = lax.axis_size("dp")
    half = nseg // 2
    ticks = fine_entries.shape[0] + 1
    hold_f, hold_c = fine_pending.shape[1], coarse_pending.shape[1]
    recv_f, recv_c = 3 * half - hold_f, half - hold_c
    fside, fch = fine_inflow.shape[3], fine_inflow.shape[4]
    cside, cch = coarse_inflow.shape[3], coarse_inflow.shape[4]
    fcells, ccells = fside * fside, cside * cside
    dims = (nseg, ndp, ticks, fside, cside, hold_f, recv_f, hold_c, recv_c)
    frows, crows = 2 * fch // LANES, 2 * cch // LANES
    any_spec = pl.BlockSpec(memory_space=pl.ANY)
    vmem_spec = pl.BlockSpec(memory_space=pltpu.VMEM)
    dma = pltpu.SemaphoreType.DMA
    args = (
        fine_inflow.reshape(fcells, fch),
        coarse_inflow.reshape(ccells, cch),
        fine_entries.reshape(ticks - 1, fcells, fch),
        fine_pending.reshape(hold_f, fcells, fch),
        coarse_pending.reshape(hold_c, ccells, cch),
        fine_kernels.reshape(2, 9 * fch, fch),
        fine_mixing.reshape(fch, fch),
        fine_gains.reshape(2, fch),
        fine_shifts.reshape(2, fch),
        coarse_kernel.reshape(9 * cch, cch),
        coarse_mixing.reshape(cch, cch),
        coarse_gains.reshape(1, cch),
        coarse_shifts.reshape(1, cch),
        descent_kernel.reshape(4 * fch, cch),
        upsample_kernel,
    )
    paired = nseg == 2 and ndp % 2 == 0 and recv_f == 1 and recv_c == 0
    if paired and ticks > hold_f + recv_f:
        fst, cst, fback, cback = run_pair(dims, fch, cch, args)
    else:
        outs = pl.pallas_call(
            functools.partial(kernel, dims),
            out_shape=(
                jax.ShapeDtypeStruct((ticks, fcells, fch), BF16),
                jax.ShapeDtypeStruct((ticks, ccells, cch), BF16),
                jax.ShapeDtypeStruct((hold_f, fcells, fch), BF16),
                jax.ShapeDtypeStruct((hold_c, ccells, cch), BF16),
            ),
            in_specs=[any_spec] * 7 + [vmem_spec] * 2 + [any_spec] * 2 + [vmem_spec] * 2 + [any_spec] * 2,
            out_specs=(any_spec,) * 4,
            scratch_shapes=[
                pltpu.VMEM((2, 9 * fch, fch), BF16),
                pltpu.VMEM((fch, fch), BF16),
                pltpu.VMEM((9 * cch, cch), BF16),
                pltpu.VMEM((cch, cch), BF16),
                pltpu.VMEM((4 * fch, cch), BF16),
                pltpu.VMEM((cch, 4 * fch), BF16),
                pltpu.VMEM((ticks, fcells, fch), BF16),
                pltpu.VMEM((ticks, ccells, cch), BF16),
                pltpu.VMEM((ticks, ccells, cch), BF16),
                pltpu.VMEM((max(hold_f, recv_f) + ticks, fcells, fch), BF16),
                pltpu.VMEM((max(hold_c, recv_c) + ticks, ccells, cch), BF16),
                pltpu.VMEM((ticks, fcells, fch), BF16),
                pltpu.VMEM((ticks, ccells, cch), BF16),
                pltpu.VMEM((ticks, ccells, cch), BF16),
                pltpu.VMEM((fcells, fch), F32),
                pltpu.VMEM((fcells, fch), F32),
                pltpu.VMEM((fcells, fch), F32),
                pltpu.VMEM((ccells, cch), F32),
                pltpu.VMEM((fch // LANES, cside, 2 * fside, LANES), F32),
                pltpu.VMEM((fcells, 9 * fch), BF16),
                pltpu.VMEM((ccells, 9 * cch), BF16),
                pltpu.VMEM((fcells, fch), BF16),
                pltpu.VMEM((ccells, cch), BF16),
                pltpu.VMEM((2 * ticks, frows, LANES), F32),
                pltpu.VMEM((ticks, crows, LANES), F32),
                pltpu.VMEM((2 * ticks, ndp - 1, frows, LANES), F32),
                pltpu.VMEM((ticks, ndp - 1, crows, LANES), F32),
                pltpu.VMEM((cch, 2, 2, fch), BF16),
                pltpu.VMEM((fch // LANES, 256, LANES), F32),
                dma((12,)),
                dma((4, max(ticks, hold_f, hold_c))),
                dma((ticks,)), dma((ticks,)), dma((ticks,)), dma((ticks,)), dma((ticks,)),
                dma((ticks,)), dma((ticks,)), dma((ticks,)), dma((ticks,)), dma((ticks,)),
                dma((2 * ticks,)), dma((ticks,)), dma((2 * ticks,)), dma((ticks,)),
            ],
            compiler_params=pltpu.CompilerParams(
                collective_id=0, has_side_effects=True, vmem_limit_bytes=56 << 20
            ),
        )(*args)
        fst, cst, fback, cback = hand_over(outs)
    return (
        fst.reshape(1, ticks, 1, fside, fside, fch),
        cst.reshape(1, ticks, 1, cside, cside, cch),
        fback.reshape(1, hold_f, 1, fside, fside, fch),
        cback.reshape(1, hold_c, 1, cside, cside, cch),
    )


def solution(mesh):
    placed = (
        P("segment", "dp", None, None, None),
        P("segment", "dp", None, None, None),
        P(None, "dp", None, None, None),
        P("segment", None, "dp", None, None, None),
        P("segment", None, "dp", None, None, None),
        P("segment", None, None, None, None, None),
        P("segment", None, None),
        P("segment", None, None),
        P("segment", None, None),
        P("segment", None, None, None, None),
        P("segment", None, None),
        P("segment", None),
        P("segment", None),
        P(),
        P(),
    )
    return jax.shard_map(
        on_device,
        mesh=mesh,
        in_specs=placed,
        out_specs=(
            P("segment", None, "dp", None, None, None),
            P("segment", None, "dp", None, None, None),
            P("segment", None, "dp", None, None, None),
            P("segment", None, "dp", None, None, None),
        ),
        check_vma=False,
    )
```

```python
import functools

import jax
import jax.numpy as jnp
from jax import lax
from jax.experimental import pallas as pl
from jax.experimental.pallas import tpu as pltpu
from jax.sharding import PartitionSpec as P

EPSILON = 1e-05
LANES = 128
MESH = pl.DeviceIdType.MESH
F32 = jnp.float32
BF16 = jnp.bfloat16


def dot(a, b):
    return jnp.dot(a, b, preferred_element_type=F32)


def side_shifts(x, side):
    cells = x.shape[0]
    column = lax.rem(lax.broadcasted_iota(jnp.int32, x.shape, 0), side)
    before = jnp.where(column == 0, 0.0, pltpu.roll(x, 1, 0))
    after = jnp.where(column == side - 1, 0.0, pltpu.roll(x, cells - 1, 0))
    return before, x, after


def spread_taps(x, cols, side):
    cells, width = x.shape
    edge = jnp.zeros((side, width), F32)
    for dc, part in enumerate(side_shifts(x, side)):
        above = jnp.concatenate([edge, part[: cells - side]], axis=0)
        below = jnp.concatenate([part[side:], edge], axis=0)
        for dr, moved in enumerate((above, part, below)):
            start = (3 * dr + dc) * width
            cols[:, start : start + width] = moved.astype(BF16)


def put_stats(h, out):
    width = h.shape[1]
    rows = width // LANES
    total = jnp.sum(h, axis=0, keepdims=True)
    square = jnp.sum(h * h, axis=0, keepdims=True)
    for row in range(rows):
        lanes = slice(row * LANES, (row + 1) * LANES)
        out[row : row + 1, :] = total[:, lanes]
        out[rows + row : rows + row + 1, :] = square[:, lanes]


def norm_terms(total, gain, shift, count):
    rows = total.shape[0] // 2
    sums = jnp.concatenate([total[row : row + 1] for row in range(rows)], axis=1)
    squares = jnp.concatenate([total[rows + row : rows + row + 1] for row in range(rows)], axis=1)
    center = sums * (1.0 / count)
    spread = jnp.maximum(squares * (1.0 / count) - center * center, 0.0)
    scale = lax.rsqrt(spread + EPSILON) * gain
    return scale, shift - center * scale


def kernel(
    dims,
    fine_in, coarse_in, entries, fine_pend, coarse_pend,
    wf_hbm, mixf_hbm, fgain, fshift, wc_hbm, mixc_hbm, cgain, cshift, wd_hbm, wu_hbm,
    fst_out, cst_out, fback_out, cback_out,
    wf, mixf, wc, mixc, wd, wu,
    fin, cin, upin, skf, skc, fst, cst, dbuf,
    xs, hf, hg, hc, upscr, colf, colc, zf, zc,
    statf, statc, gotf, gotc,
    wu4, wuf, load_sem, save_sem,
    fin_r, cin_r, up_r, skf_r, skc_r,
    fin_s, cin_s, up_s, skf_s, skc_s,
    gotf_r, gotc_r, statf_s, statc_s,
):
    nseg, ndp, ticks, fside, cside, hold_f, recv_f, hold_c, recv_c = dims
    half = nseg // 2
    seg = lax.axis_index("segment")
    me = lax.axis_index("dp")
    lower = seg < half
    upper = seg >= half
    turn = seg == half - 1
    after = lax.rem(seg + 1, nseg)
    mate = lax.rem(seg + half, nseg)

    def load(k, src, dst):
        return pltpu.make_async_copy(src, dst, load_sem.at[k])

    get_fine = load(0, fine_in, fin.at[0])
    get_wf0 = load(1, wf_hbm.at[0], wf.at[0])
    get_mixf = load(2, mixf_hbm, mixf)
    get_coarse = load(3, coarse_in, cin.at[0])
    get_mixc = load(4, mixc_hbm, mixc)
    get_wc = load(5, wc_hbm, wc)
    get_wf1 = load(6, wf_hbm.at[1], wf.at[1])
    get_wd = load(7, wd_hbm, wd)
    get_wu = load(11, wu_hbm, wu4)
    own_entries = load(8, entries, fin.at[pl.ds(1, ticks - 1)])
    own_fine = hold_f if hold_f > ticks else 0
    own_coarse = hold_c if hold_c > ticks else 0

    def own_pend(k, src, dst, count):
        return load(k, src.at[pl.ds(0, count)], dst.at[pl.ds(0, count)])

    barrier = pltpu.get_barrier_semaphore()
    offsets = sorted({1 % nseg, nseg - 1, half})

    def greet(k, carry):
        pl.semaphore_signal(
            barrier, inc=1, device_id=(seg, lax.rem(me + k, ndp)), device_id_type=MESH
        )
        return carry

    lax.fori_loop(1, ndp, greet, 0)
    for offset in offsets:
        pl.semaphore_signal(
            barrier, inc=1, device_id=(lax.rem(seg + offset, nseg), me), device_id_type=MESH
        )
    @pl.when(upper)
    def _():
        if recv_f:
            own_pend(9, fine_pend, skf, recv_f).start()

    for item in (get_fine, get_wf0, get_mixf, get_coarse, get_mixc, get_wc, get_wf1):
        item.start()

    @pl.when(lower)
    def _():
        if recv_c:
            own_pend(10, coarse_pend, skc, recv_c).start()
        if own_fine:
            own_pend(9, fine_pend, skf, own_fine).start()

    @pl.when(upper)
    def _():
        if own_coarse:
            own_pend(10, coarse_pend, skc, own_coarse).start()

    @pl.when(seg == 0)
    def _():
        own_entries.start()

    @pl.when(turn)
    def _():
        get_wd.start()

    @pl.when(seg == half)
    def _():
        get_wu.start()

    zf[...] = jnp.zeros_like(zf)
    zc[...] = jnp.zeros_like(zc)
    pl.semaphore_wait(barrier, ndp - 1 + len(offsets))

    def push(src, dst, ssem, rsem, to):
        return pltpu.make_async_remote_copy(
            src_ref=src, dst_ref=dst, send_sem=ssem, recv_sem=rsem,
            device_id=(to, me), device_id_type=MESH,
        )

    def send_skf(j):
        return push(skf.at[j], skf.at[recv_f + j], skf_s.at[j], skf_r.at[j], mate)

    def send_pend_f(j):
        return push(fine_pend.at[j], skf.at[recv_f + j], skf_s.at[j], skf_r.at[j], mate)

    def send_pend_c(j):
        return push(coarse_pend.at[j], skc.at[recv_c + j], skc_s.at[j], skc_r.at[j], mate)

    def send_skc(j):
        return push(skc.at[j], skc.at[recv_c + j], skc_s.at[j], skc_r.at[j], mate)

    def send_up(t):
        return push(cst.at[t], upin.at[t], up_s.at[t], up_r.at[t], after)

    def send_co(t):
        return push(cst.at[t], cin.at[t + 1], cin_s.at[t], cin_r.at[t], after)

    def send_down(t):
        return push(dbuf.at[t], cin.at[t + 1], cin_s.at[t], cin_r.at[t], after)

    def send_fo(t):
        return push(fst.at[t], fin.at[t + 1], fin_s.at[t], fin_r.at[t], after)

    def exchange(src, dst, ssem, rsem):
        def one(k, carry):
            pltpu.make_async_remote_copy(
                src_ref=src, dst_ref=dst.at[k - 1], send_sem=ssem, recv_sem=rsem,
                device_id=(seg, lax.rem(me + k, ndp)), device_id_type=MESH,
            ).start()
            return carry

        lax.fori_loop(1, ndp, one, 0)

    def whole(dst, ssem, rsem):
        return pltpu.make_async_remote_copy(
            src_ref=dst, dst_ref=dst, send_sem=ssem, recv_sem=rsem,
            device_id=(seg, lax.rem(me + 1, ndp)), device_id_type=MESH,
        )

    @pl.when(lower)
    def _():
        for j in range(min(hold_f, ticks)):
            send_pend_f(j).start()

    @pl.when(upper)
    def _():
        for j in range(min(hold_c, ticks)):
            send_pend_c(j).start()

    fcount = ndp * fside * fside
    ccount = ndp * cside * cside

    def save_f(t):
        return pltpu.make_async_copy(fst.at[t], fst_out.at[t], save_sem.at[0, t])

    def save_c(t):
        return pltpu.make_async_copy(cst.at[t], cst_out.at[t], save_sem.at[1, t])

    def first(t, *items):
        @pl.when(t == 0)
        def _():
            for item in items:
                item.wait()

    def front(t):
        first(t, get_fine, get_mixf)

        @pl.when(lower)
        def _():
            @pl.when(jnp.logical_and(seg > 0, t > 0))
            def _():
                send_fo(t - 1).wait_recv()

            xs[...] = fin[t].astype(F32)

        @pl.when(upper)
        def _():
            @pl.when(jnp.logical_and(seg == half, t > 0))
            def _():
                send_up(t - 1).wait_recv()
                spread = dot(upin[t - 1], wu[...])
                width = spread.shape[1] // 4
                for a in range(2):
                    for c in range(2):
                        start = (2 * a + c) * width
                        part = spread[:, start : start + width].reshape(cside, cside, width)
                        for i in range(width // LANES):
                            lanes = slice(i * LANES, (i + 1) * LANES)
                            upscr[i, :, pl.ds(a * fside + c, cside, stride=2), :] = part[:, :, lanes]
                for i in range(width // LANES):
                    lanes = slice(i * LANES, (i + 1) * LANES)
                    fin[t, :, lanes] = upscr[i].reshape(fside * fside, LANES).astype(BF16)

            @pl.when(jnp.logical_and(seg != half, t > 0))
            def _():
                send_fo(t - 1).wait_recv()

            if recv_f:
                first(t, own_pend(9, fine_pend, skf, recv_f))

            @pl.when(t >= recv_f)
            def _():
                send_skf(t - recv_f).wait_recv()

            xs[...] = (dot(fin[t], mixf[...]) + skf[t].astype(F32)).astype(BF16).astype(F32)

        spread_taps(xs[...], colf, fside)
        first(t, get_wf0)
        hf[...] = dot(colf[...], wf[0])
        put_stats(hf[...], statf.at[2 * t])
        exchange(statf.at[2 * t], gotf.at[2 * t], statf_s.at[2 * t], gotf_r.at[2 * t])

    def later(which, t):
        @pl.when(jnp.logical_and(which, t < ticks - 1))
        def _():
            front(t + 1)

    def own_pieces(t):
        @pl.when(t == 0)
        def _():
            get_wf1.wait()

            @pl.when(turn)
            def _():
                get_wd.wait()

            @pl.when(seg == 0)
            def _():
                own_entries.wait()

            @pl.when(seg == half)
            def _():
                get_wu.wait()
                width = wu4.shape[3]
                depth = wuf.shape[1] // 4

                def rows_of(n, carry):
                    rows = pl.multiple_of(n * depth, depth)
                    piece = wu4[pl.ds(rows, depth)].astype(F32).reshape(4 * depth, width)
                    for i in range(width // LANES):
                        wuf[i] = piece[:, i * LANES : (i + 1) * LANES]
                    for q in range(4):
                        for i in range(width // LANES):
                            start = q * width + i * LANES
                            part = wuf[i, pl.ds(q, depth, stride=4), :]
                            wu[pl.ds(rows, depth), start : start + LANES] = part.astype(BF16)
                    return carry

                lax.fori_loop(0, wu4.shape[0] // depth, rows_of, 0)

    front(jnp.int32(0))
    own_pieces(jnp.int32(0))

    def tick(t, carry):
        first(t, get_coarse, get_mixc)

        @pl.when(t > 0)
        def _():
            send_co(t - 1).wait_recv()

        @pl.when(lower)
        def _():
            if recv_c:
                first(t, own_pend(10, coarse_pend, skc, recv_c))

            @pl.when(t >= recv_c)
            def _():
                send_skc(t - recv_c).wait_recv()

            hc[...] = (dot(cin[t], mixc[...]) + skc[t].astype(F32)).astype(BF16).astype(F32)

        @pl.when(upper)
        def _():
            hc[...] = cin[t].astype(F32)

        spread_taps(hc[...], colc, cside)
        first(t, get_wc)
        hc[...] = dot(colc[...], wc[...])
        put_stats(hc[...], statc.at[t])
        exchange(statc.at[t], gotc.at[t], statc_s.at[t], gotc_r.at[t])

        whole(gotf.at[2 * t], statf_s.at[2 * t], gotf_r.at[2 * t]).wait_recv()
        total = statf[2 * t] + jnp.sum(gotf[2 * t], axis=0)
        scale, offset = norm_terms(total, fgain[0:1, :], fshift[0:1, :], fcount)
        xs[...] = jnp.maximum(hf[...] * scale + offset, 0.0).astype(BF16).astype(F32)
        spread_taps(xs[...], colf, fside)
        hg[...] = dot(colf[...], wf[1])
        put_stats(hg[...], statf.at[2 * t + 1])
        exchange(
            statf.at[2 * t + 1], gotf.at[2 * t + 1], statf_s.at[2 * t + 1], gotf_r.at[2 * t + 1]
        )

        whole(gotc.at[t], statc_s.at[t], gotc_r.at[t]).wait_recv()
        total = statc[t] + jnp.sum(gotc[t], axis=0)
        scale, offset = norm_terms(total, cgain[...], cshift[...], ccount)
        cst[t] = jnp.maximum(hc[...] * scale + offset, 0.0).astype(BF16)

        @pl.when(t < ticks - 1)
        def _():
            @pl.when(turn)
            def _():
                send_up(t).start()

            @pl.when(jnp.logical_not(turn))
            def _():
                send_co(t).start()

        save_c(t).start()

        @pl.when(upper)
        def _():
            skc[hold_c + t] = dot(cst[t], mixc[...]).astype(BF16)

            @pl.when(hold_c + t < ticks)
            def _():
                send_skc(hold_c + t).start()

        later(seg == 0, t)

        whole(gotf.at[2 * t + 1], statf_s.at[2 * t + 1], gotf_r.at[2 * t + 1]).wait_recv()
        total = statf[2 * t + 1] + jnp.sum(gotf[2 * t + 1], axis=0)
        scale, offset = norm_terms(total, fgain[1:2, :], fshift[1:2, :], fcount)
        fst[t] = jnp.maximum(hg[...] * scale + offset, 0.0).astype(BF16)

        @pl.when(t < ticks - 1)
        def _():
            @pl.when(turn)
            def _():
                width = fst.shape[2]
                for i in range(width // LANES):
                    lanes = slice(i * LANES, (i + 1) * LANES)
                    upscr[i] = fst[t, :, lanes].astype(F32).reshape(cside, 2 * fside, LANES)
                lowered = None
                for a in range(2):
                    for c in range(2):
                        for i in range(width // LANES):
                            part = upscr[i, :, pl.ds(a * fside + c, cside, stride=2), :]
                            part = part.reshape(cside * cside, LANES).astype(BF16)
                            start = (2 * a + c) * width + i * LANES
                            term = dot(part, wd[start : start + LANES, :])
                            lowered = term if lowered is None else lowered + term
                dbuf[t] = lowered.astype(BF16)
                send_down(t).start()

            @pl.when(jnp.logical_and(jnp.logical_not(turn), seg < nseg - 1))
            def _():
                send_fo(t).start()

        save_f(t).start()

        @pl.when(lower)
        def _():
            skf[hold_f + t] = dot(fst[t], mixf[...]).astype(BF16)

            @pl.when(hold_f + t < ticks)
            def _():
                send_skf(hold_f + t).start()

        later(seg > 0, t)
        return carry

    lax.fori_loop(0, ticks, tick, 0)

    def back_f(first, src):
        return pltpu.make_async_copy(src, fback_out.at[first], save_sem.at[2, first])

    def back_c(first, src):
        return pltpu.make_async_copy(src, cback_out.at[first], save_sem.at[3, first])

    lower_backs = [back_f(j, skf.at[ticks + j]) for j in range(hold_f)]
    lower_backs += [
        back_c(j, skc.at[ticks + j] if j < recv_c else zc) for j in range(hold_c)
    ]
    upper_backs = [
        back_f(j, skf.at[ticks + j] if j < recv_f else zf) for j in range(hold_f)
    ]
    upper_backs += [back_c(j, skc.at[ticks + j]) for j in range(hold_c)]

    @pl.when(lower)
    def _():
        if own_fine:
            own_pend(9, fine_pend, skf, own_fine).wait()
        for j in range(max(ticks - recv_c, 0), ticks):
            send_skc(j).wait_recv()
        for item in lower_backs:
            item.start()
        for j in range(ticks):
            send_skf(j).wait_send()
        for item in lower_backs:
            item.wait()

    @pl.when(upper)
    def _():
        if own_coarse:
            own_pend(10, coarse_pend, skc, own_coarse).wait()
        for j in range(max(ticks - recv_f, 0), ticks):
            send_skf(j).wait_recv()
        for item in upper_backs:
            item.start()
        for j in range(ticks):
            send_skc(j).wait_send()
        for item in upper_backs:
            item.wait()

    @pl.when(turn)
    def _():
        for t in range(ticks - 1):
            send_up(t).wait_send()

    @pl.when(jnp.logical_and(jnp.logical_not(turn), seg < nseg - 1))
    def _():
        for t in range(ticks - 1):
            send_fo(t).wait_send()

    for t in range(ticks - 1):
        send_co(t).wait_send()
    for t in range(ticks):
        whole(gotf.at[2 * t], statf_s.at[2 * t], gotf_r.at[2 * t]).wait_send()
        whole(gotf.at[2 * t + 1], statf_s.at[2 * t + 1], gotf_r.at[2 * t + 1]).wait_send()
        whole(gotc.at[t], statc_s.at[t], gotc_r.at[t]).wait_send()
        save_f(t).wait()
        save_c(t).wait()


def sums_of(total):
    rows = total.shape[0] // 2
    sums = jnp.concatenate([total[row : row + 1] for row in range(rows)], axis=1)
    squares = jnp.concatenate([total[rows + row : rows + row + 1] for row in range(rows)], axis=1)
    return sums, squares


def moments(total, count):
    sums, squares = sums_of(total)
    center = sums * (1.0 / count)
    spread = jnp.maximum(squares * (1.0 / count) - center * center, 0.0)
    return center, lax.rsqrt(spread + EPSILON)


def pair_kernel(
    dims,
    fine_in, coarse_in, entries, fine_pend, coarse_pend,
    wf_hbm, mixf_hbm, fgain_hbm, fshift_hbm, wc_hbm, mixc_hbm, cgain_hbm, cshift_hbm,
    wd_hbm, wu_hbm,
    fst, cst, fback, cback,
    wf, mixf, mixe, wc, mixc, mixm, wd, wu, wu4, wuf,
    fin, cin, skf, skc, dbuf, dbuf_in, co_in, fgain, fshift, cgain, cshift, mate_fgain, mate_fshift, mate_cgain, mate_cshift,
    hf, hc, xs, hx, upscr, colf, colc, cold,
    rawf_out, rawf_in, rawc_out, rawc_in,
    stf, stc, gotf, gotc, farf, farc,
    load_sem, sf, rf, sc, rc, sfarf, rfarf, sfarc, rfarc,
    srawf, rrawf, srawc, rrawc, skf_s, skf_r, dbuf_s, dbuf_r, co_s, co_r, one_s, one_r, ready,
):
    nseg, ndp, ticks, fside, cside, hold_f, recv_f, hold_c, recv_c = dims
    seg = lax.axis_index("segment")
    me = lax.axis_index("dp")
    other = 1 - seg
    lower = seg == 0
    upper = seg == 1
    fcells, ccells = fside * fside, cside * cside
    fcount, ccount = ndp * fcells, ndp * ccells
    last = ticks - 1

    barrier = pltpu.get_barrier_semaphore()

    def load(k, src, dst):
        return pltpu.make_async_copy(src, dst, load_sem.at[k])

    get_fine = load(0, fine_in, fin.at[0])
    get_wf0 = load(1, wf_hbm.at[0], wf.at[0])
    get_mixf = load(2, mixf_hbm, mixf)
    get_coarse = load(3, coarse_in, cin)
    get_mixc = load(13, mixc_hbm, mixc)
    get_wc = load(5, wc_hbm, wc)
    get_wf1 = load(6, wf_hbm.at[1], wf.at[1])
    get_wd = load(7, wd_hbm, wd)
    get_entries = load(8, entries, fin.at[pl.ds(1, last)])
    get_pend = load(8, fine_pend.at[pl.ds(0, recv_f)], skf.at[pl.ds(0, recv_f)])
    get_wu = load(9, wu_hbm, wu4)
    get_norms = [
        load(10, fgain_hbm, fgain), load(11, fshift_hbm, fshift),
        load(12, cgain_hbm, cgain), load(4, cshift_hbm, cshift),
    ]

    get_fine.start()

    @pl.when(upper)
    def _():
        get_mixf.start()
        get_pend.start()

    get_wf0.start()

    bits = ndp.bit_length() - 1

    def partner(k):
        if 1 << bits != ndp:
            return lax.rem(me + k, ndp)
        to = 0
        for b in range(bits):
            bit = lax.rem(lax.div(me, 1 << b), 2)
            to = to + (1 << b) * (1 - bit if (k >> b) & 1 else bit)
        return to

    partners = [partner(k) for k in range(ndp)]
    twin = me + 1 - 2 * lax.rem(me, 2)
    for k in range(ndp - 1, 0, -1):
        pl.semaphore_signal(barrier, inc=1, device_id=(seg, partners[k]), device_id_type=MESH)
    pl.semaphore_signal(barrier, inc=1, device_id=(other, me), device_id_type=MESH)

    @pl.when(lower)
    def _():
        for item in (get_entries, get_wf1, get_mixf, get_coarse, get_mixc, get_wc, get_wd):
            item.start()

    @pl.when(upper)
    def _():
        for item in (get_coarse, get_wc, get_wf1, get_wd, get_wu, get_mixc):
            item.start()

    for item in get_norms:
        item.start()

    def push(src, dst, ssem, rsem):
        return pltpu.make_async_remote_copy(
            src_ref=src, dst_ref=dst, send_sem=ssem, recv_sem=rsem,
            device_id=(other, me), device_id_type=MESH,
        )

    def share(src, dst, ssem, rsem):
        for k in range(ndp - 1, 0, -1):
            pltpu.make_async_remote_copy(
                src_ref=src, dst_ref=dst.at[k - 1], send_sem=ssem, recv_sem=rsem,
                device_id=(seg, partners[k]), device_id_type=MESH,
            ).start()

    def cast_far(src, dst, ssem, rsem):
        for k in range(ndp - 1, -1, -1):
            pltpu.make_async_remote_copy(
                src_ref=src, dst_ref=dst.at[k], send_sem=ssem, recv_sem=rsem,
                device_id=(other, partners[k]), device_id_type=MESH,
            ).start()

    def of_f(n):
        return push(gotf.at[n], gotf.at[n], sf, rf.at[n])

    def of_c(t):
        return push(gotc.at[t], gotc.at[t], sc, rc.at[t])

    of_farf = push(farf, farf, sfarf, rfarf)
    send_rawf = push(rawf_out, rawf_in, srawf, rrawf)

    def of_farc(t):
        return push(farc.at[t - 1], farc.at[t - 1], sfarc, rfarc.at[t - 1])

    def send_rawc(t):
        return push(rawc_out.at[t - 1], rawc_in.at[t - 1], srawc, rrawc.at[t - 1])

    def send_down(t):
        return push(dbuf.at[t - 1], dbuf_in.at[t - 1], dbuf_s, dbuf_r.at[t - 1])

    def send_co(t):
        return push(cst.at[t], co_in.at[t], co_s, co_r.at[t])

    def send_skf(j):
        return push(skf.at[j], skf.at[recv_f + j], skf_s, skf_r.at[j])

    def send_pend_f(j):
        return push(fine_pend.at[j], skf.at[recv_f + j], skf_s, skf_r.at[j])

    send_pend_c = push(coarse_pend.at[0], skc, one_s.at[0], one_r.at[0])

    def rows_of(matrix, device):
        part = matrix.shape[0] // 2
        return pl.ds(pl.multiple_of(lax.rem(device, 2) * part, part), part)

    def send_half(src, dst):
        rows = rows_of(dst, me)
        return push(src.at[rows], dst.at[rows], one_s.at[1], one_r.at[1])

    def hand_half(matrix, device):
        rows = rows_of(matrix, device)
        return pltpu.make_async_remote_copy(
            src_ref=matrix.at[rows], dst_ref=matrix.at[rows],
            send_sem=one_s.at[6], recv_sem=one_r.at[6],
            device_id=(seg, twin), device_id_type=MESH,
        )

    send_mixc = send_half(mixc_hbm, mixm)
    send_mixf = send_half(mixf_hbm, mixe)
    send_norms = [
        push(fgain_hbm, mate_fgain, one_s.at[2], one_r.at[2]),
        push(fshift_hbm, mate_fshift, one_s.at[3], one_r.at[3]),
        push(cgain_hbm, mate_cgain, one_s.at[4], one_r.at[4]),
        push(cshift_hbm, mate_cshift, one_s.at[5], one_r.at[5]),
    ]

    def conv_fine(layer, out):
        spread_taps(xs[...], colf, fside)
        out[...] = dot(colf[...], wf[layer])

    def centred(h, stats, cells):
        sums, _ = sums_of(stats)
        return (h - sums * (1.0 / cells)).astype(BF16)

    def arrived(raw, got, mine, gain, shift, count, cells):
        center, inverse = moments(got, count)
        own, _ = sums_of(mine)
        scale = inverse * gain
        offset = shift + (own * (1.0 / cells) - center) * scale
        return jnp.maximum(raw[...].astype(F32) * scale + offset, 0.0).astype(BF16)

    def descended(x):
        width = x.shape[1]
        for i in range(width // LANES):
            lanes = slice(i * LANES, (i + 1) * LANES)
            upscr[i] = x[:, lanes].reshape(cside, 2 * fside, LANES)
        for a in range(2):
            for c in range(2):
                for i in range(width // LANES):
                    piece = upscr[i, :, pl.ds(a * fside + c, cside, stride=2), :]
                    start = (2 * a + c) * width + i * LANES
                    cold[:, start : start + LANES] = piece.reshape(ccells, LANES).astype(BF16)
        return dot(cold[...], wd[...]).astype(BF16)

    def normed(h, stats, got, gain, shift, count):
        center, inverse = moments(stats[...] + jnp.sum(got[...], axis=0), count)
        scale = inverse * gain
        return jnp.maximum(h[...] * scale + (shift - center * scale), 0.0).astype(BF16)

    def share_fine(n):
        share(stf.at[n], gotf.at[n], sf, rf.at[n])

    def conv_stats(layer, n):
        conv_fine(layer, hf.at[n])
        put_stats(hf[n], stf.at[n])

    def take_first(t):
        xs[...] = normed(
            hf.at[t], stf.at[t], gotf.at[t], fgain[0:1, :], fshift[0:1, :], fcount
        ).astype(F32)

    def finish_fine(t):
        n = ticks + t
        of_f(n).wait_recv()
        fst[t] = normed(hf.at[n], stf.at[n], gotf.at[n], fgain[1:2, :], fshift[1:2, :], fcount)

    def finish_coarse(t):
        of_c(t).wait_recv()
        cst[t] = normed(hc.at[t], stc.at[t], gotc.at[t], cgain[...], cshift[...], ccount)

    def coarse(t, raw):
        spread_taps(hx[...], colc, cside)
        hc[t] = dot(colc[...], wc[...])
        put_stats(hc[t], stc.at[t])

        @pl.when(raw)
        def _():
            cast_far(stc.at[t], farc.at[t - 1], sfarc, rfarc.at[t - 1])
            rawc_out[t - 1] = centred(hc[t], stc[t], ccells)
            send_rawc(t).start()

        share(stc.at[t], gotc.at[t], sc, rc.at[t])

    def mate_coarse(t):
        of_farc(t).wait_recv()
        send_rawc(t).wait_recv()
        return arrived(
            rawc_in.at[t - 1], jnp.sum(farc[t - 1], axis=0), farc[t - 1, 0], mate_cgain[...],
            mate_cshift[...], ccount, ccells,
        )

    def sent():
        for item in send_norms:
            item.wait_send()
        push(gotc, gotc, sc, rc.at[0]).wait_send()

    get_fine.wait()

    @pl.when(lower)
    def _():
        xs[...] = fin[0].astype(F32)

    @pl.when(upper)
    def _():
        get_mixf.wait()
        get_pend.wait()
        xs[...] = (dot(fin[0], mixf[...]) + skf[0].astype(F32)).astype(BF16).astype(F32)

    get_wf0.wait()
    conv_stats(0, 0)
    pl.semaphore_wait(barrier, ndp)
    share_fine(0)
    pl.semaphore_signal(ready, inc=1, device_id=(other, me), device_id_type=MESH)

    @pl.when(lower)
    def _():
        for item in send_norms:
            item.start()
        send_pend_f(0).start()
        send_mixf.start()
        get_entries.wait()

        def early(t, carry):
            xs[...] = fin[t].astype(F32)
            conv_stats(0, t)
            return carry

        lax.fori_loop(1, ticks, early, 0)
        rest = pl.ds(1, last)
        for k in range(ndp - 1, 0, -1):
            pltpu.make_async_remote_copy(
                src_ref=stf.at[rest], dst_ref=gotf.at[rest, k - 1], send_sem=sf, recv_sem=rf.at[1],
                device_id=(seg, partners[k]), device_id_type=MESH,
            ).start()
        for item in (get_wf1, get_mixf, get_coarse, get_mixc, get_wc, get_wd, *get_norms):
            item.wait()
        pl.semaphore_wait(ready, 1)

        def term(n, carry):
            t = jnp.where(n < last - 1, n + 1, jnp.where(n == last, last, 0))
            finish_fine(t)

            @pl.when(jnp.logical_and(t > 0, t < last))
            def _():
                dbuf[t - 1] = descended(fst[t].astype(F32))
                send_down(t).start()

            @pl.when(t > 0)
            def _():
                fresh = dot(fst[t], mixf[...]).astype(BF16)

                @pl.when(hold_f + t < ticks)
                def _():
                    skf[hold_f + t] = fresh

                @pl.when(hold_f + t >= ticks)
                def _():
                    fback[hold_f + t - ticks] = fresh

            return carry

        def encode(i, carry):
            t = jnp.maximum(i - last + 1, 0)

            @pl.when(i < ticks)
            def _():
                @pl.when(i == 0)
                def _():
                    of_f(0).wait_recv()

                @pl.when(i == 1)
                def _():
                    push(gotf.at[rest], gotf.at[rest], sf, rf.at[1]).wait_recv()

                take_first(i)
                conv_stats(1, ticks + i)

                @pl.when(i == 0)
                def _():
                    cast_far(stf.at[ticks], farf, sfarf, rfarf)
                    rawf_out[...] = centred(hf[ticks], stf[ticks], fcells)
                    send_rawf.start()

                share_fine(ticks + i)

                @pl.when(i == 1)
                def _():
                    for j in range(1, hold_f):
                        send_pend_f(j).start()

            @pl.when(i == 0)
            def _():
                send_pend_c.wait_recv()
                hx[...] = (dot(cin[...], mixc[...]) + skc[...].astype(F32)).astype(BF16).astype(F32)

            def mixed(taken):
                hx[...] = dot(taken, mixm[...]).astype(BF16).astype(F32)

            @pl.when(i == last)
            def _():
                send_mixc.wait_recv()
                hand_half(mixm, me).start()
                finish_coarse(0)
                send_co(0).start()
                hand_half(mixm, twin).wait_recv()
                hand_half(mixm, me).wait_send()
                mixm[...] = (mixm[...].astype(F32) + mixc[...].astype(F32)).astype(BF16)
                for item in send_norms:
                    item.wait_recv()
                send_co(0).wait_recv()
                mixed(co_in[0])

            @pl.when(i > last)
            def _():
                finish_coarse(t - 1)

                @pl.when(t < last)
                def _():
                    send_co(t - 1).start()

                mixed(mate_coarse(t - 1))

            @pl.when(jnp.logical_or(i == 0, i >= last))
            def _():
                coarse(t, t == last - 1)

            @pl.when(i == last)
            def _():
                lax.fori_loop(0, ticks, term, 0)

            @pl.when(t == last)
            def _():
                for j in range(hold_f + 1, ticks):
                    send_skf(j).start()

            return carry

        lax.fori_loop(0, 2 * ticks - 2, encode, 0)
        cback[...] = jnp.zeros_like(cback)
        of_farf.wait_send()
        send_rawf.wait_send()
        of_farc(last - 1).wait_send()
        send_rawc(last - 1).wait_send()
        push(co_in, co_in, co_s, co_r.at[0]).wait_send()
        push(dbuf, dbuf_in, dbuf_s, dbuf_r.at[0]).wait_send()
        terms = skf.at[pl.ds(0, ticks - 1)]
        push(terms, terms, skf_s, skf_r.at[0]).wait_send()
        send_mixf.wait_send()
        sent()
        finish_coarse(last)

    @pl.when(upper)
    def _():
        for item in send_norms:
            item.start()
        send_pend_c.start()
        send_mixc.start()
        get_coarse.wait()
        get_wc.wait()

        def spread_weights():
            width = wu4.shape[3]
            depth = wuf.shape[1] // 4

            def rows_of(n, carry):
                rows = pl.multiple_of(n * depth, depth)
                piece = wu4[pl.ds(rows, depth)].astype(F32).reshape(4 * depth, width)
                for i in range(width // LANES):
                    wuf[i] = piece[:, i * LANES : (i + 1) * LANES]
                for q in range(4):
                    for i in range(width // LANES):
                        start = q * width + i * LANES
                        part = wuf[i, pl.ds(q, depth, stride=4), :]
                        wu[pl.ds(rows, depth), start : start + LANES] = part.astype(BF16)
                return carry

            lax.fori_loop(0, wu4.shape[0] // depth, rows_of, 0)

        pl.semaphore_wait(ready, 1)

        def encode(t, carry):
            @pl.when(t == 0)
            def _():
                hx[...] = cin[...].astype(F32)

            @pl.when(t == 1)
            def _():
                for item in send_norms:
                    item.wait_recv()
                of_farf.wait_recv()
                send_rawf.wait_recv()
                taken = arrived(
                    rawf_in, jnp.sum(farf[...], axis=0), farf[0], mate_fgain[1:2, :],
                    mate_fshift[1:2, :], fcount, fcells,
                )
                fin[0] = taken
                hx[...] = descended(taken.astype(F32)).astype(F32)

            @pl.when(t > 1)
            def _():
                send_down(t - 1).wait_recv()
                hx[...] = dbuf_in[t - 2].astype(F32)

            coarse(t, jnp.logical_and(t > 0, t < last))
            return carry

        def raised(taken, t):
            spread = dot(taken, wu[...])
            width = spread.shape[1] // 4
            for a in range(2):
                for c in range(2):
                    start = (2 * a + c) * width
                    part = spread[:, start : start + width].reshape(cside, cside, width)
                    for i in range(width // LANES):
                        lanes = slice(i * LANES, (i + 1) * LANES)
                        upscr[i, :, pl.ds(a * fside + c, cside, stride=2), :] = part[:, :, lanes]
            for i in range(width // LANES):
                lanes = slice(i * LANES, (i + 1) * LANES)
                part = upscr[i].reshape(fcells, LANES) + skf[t, :, lanes].astype(F32)
                xs[:, lanes] = part.astype(BF16).astype(F32)

        def step(o, carry):
            coarse_end = jnp.where(o < 2, o + 1, jnp.where(o == 2, ticks, o))
            lax.fori_loop(o, coarse_end, encode, 0)
            half_o = lax.div(o, 2)
            odd = lax.rem(o, 2) == 1
            is_first = jnp.logical_or(
                o == 1, jnp.logical_and(jnp.logical_and(o > 1, o < 2 * last), jnp.logical_not(odd))
            )
            t = jnp.where(
                o == 0, 0, jnp.where(is_first, jnp.where(o == 1, 1, half_o + 1),
                                     jnp.where(o == 2 * last, last, half_o))
            )

            @pl.when(o == 0)
            def _():
                for item in (get_wf1, get_wd, get_wu, get_mixc, *get_norms):
                    item.wait()
                spread_weights()
                width = mixf.shape[0]
                for q in range(4):
                    lanes = slice(q * width, (q + 1) * width)
                    wu[:, lanes] = dot(wu[:, lanes], mixf[...]).astype(BF16)

            @pl.when(o == 1)
            def _():
                finish_fine(0)
                hand_half(mixe, twin).wait_recv()
                skf[recv_f + hold_f] = dot(fin[0], mixe[...]).astype(BF16)

            @pl.when(o == 2)
            def _():
                finish_coarse(1)

            @pl.when(is_first)
            def _():
                @pl.when(t - recv_f != hold_f)
                def _():
                    send_skf(t - recv_f).wait_recv()

                @pl.when(t < last)
                def _():
                    send_co(t - 1).wait_recv()
                    raised(co_in[t - 1], t)

                @pl.when(t == last)
                def _():
                    raised(mate_coarse(t - 1), t)

            @pl.when(jnp.logical_not(is_first))
            def _():
                of_f(t).wait_recv()
                take_first(t)

            layer = jnp.where(is_first, 0, 1)
            n = layer * ticks + t
            conv_stats(layer, n)
            share_fine(n)

            @pl.when(o == 0)
            def _():
                finish_coarse(0)
                send_co(0).start()
                send_mixf.wait_recv()
                hand_half(mixe, me).start()

            @pl.when(o == 2 * last - 2)
            def _():
                def rest(n, c):
                    finish_coarse(n)
                    return c

                lax.fori_loop(2, ticks, rest, 0)
                cback[0] = dot(cst[last], mixc[...]).astype(BF16)

            return carry

        lax.fori_loop(0, 2 * ticks - 1, step, 0)

        def rest_fine(n, c):
            finish_fine(n)
            return c

        lax.fori_loop(1, last - 1, rest_fine, 0)
        for j in range(max(ticks - recv_f, 0), ticks):
            send_skf(j).wait_recv()
        for j in range(hold_f):
            fback[j] = skf[ticks + j] if j < recv_f else jnp.zeros_like(skf[0])
        finish_fine(last - 1)
        send_pend_c.wait_send()
        send_mixc.wait_send()
        hand_half(mixe, me).wait_send()
        send_co(0).wait_send()
        push(farc, farc, sfarc, rfarc.at[0]).wait_send()
        push(rawc_in, rawc_in, srawc, rrawc.at[0]).wait_send()
        sent()
        finish_fine(last)

    push(gotf, gotf, sf, rf.at[0]).wait_send()


def put_out_kernel(*refs):
    count = (len(refs) - 1) // 2
    sources, results, sem = refs[:count], refs[count : 2 * count], refs[2 * count]
    given = [
        pltpu.make_async_copy(source, result, sem.at[i])
        for i, (source, result) in enumerate(zip(sources, results))
    ]
    for item in given:
        item.start()
    for item in given:
        item.wait()


def put_out(arrays):
    any_spec = pl.BlockSpec(memory_space=pl.ANY)
    vmem_spec = pl.BlockSpec(memory_space=pltpu.VMEM)
    held = [pltpu.with_memory_space_constraint(a, pltpu.VMEM) for a in arrays]
    return pl.pallas_call(
        put_out_kernel,
        out_shape=tuple(jax.ShapeDtypeStruct(a.shape, a.dtype) for a in arrays),
        in_specs=[vmem_spec] * len(arrays),
        out_specs=(any_spec,) * len(arrays),
        scratch_shapes=[pltpu.SemaphoreType.DMA((len(arrays),))],
    )(*held)


def run_pair(dims, fch, cch, args):
    nseg, ndp, ticks, fside, cside, hold_f, recv_f, hold_c, recv_c = dims
    fcells, ccells = fside * fside, cside * cside
    frows, crows = 2 * fch // LANES, 2 * cch // LANES
    last = ticks - 1
    any_spec = pl.BlockSpec(memory_space=pl.ANY)
    vmem_spec = pl.BlockSpec(memory_space=pltpu.VMEM)
    dma, vmem = pltpu.SemaphoreType.DMA, pltpu.VMEM
    outs = pl.pallas_call(
        functools.partial(pair_kernel, dims),
        out_shape=(
            vmem((ticks, fcells, fch), BF16),
            vmem((ticks, ccells, cch), BF16),
            vmem((hold_f, fcells, fch), BF16),
            vmem((hold_c, ccells, cch), BF16),
        ),
        in_specs=[any_spec] * 15,
        out_specs=(vmem_spec,) * 4,
        scratch_shapes=[
            vmem((2, 9 * fch, fch), BF16),
            vmem((fch, fch), BF16),
            vmem((fch, fch), BF16),
            vmem((9 * cch, cch), BF16),
            vmem((cch, cch), BF16),
            vmem((cch, cch), BF16),
            vmem((4 * fch, cch), BF16),
            vmem((cch, 4 * fch), BF16),
            vmem((cch, 2, 2, fch), BF16),
            vmem((fch // LANES, 256, LANES), F32),
            vmem((ticks, fcells, fch), BF16),
            vmem((ccells, cch), BF16),
            vmem((max(hold_f, recv_f) + ticks, fcells, fch), BF16),
            vmem((ccells, cch), BF16),
            vmem((last - 1, ccells, cch), BF16),
            vmem((last - 1, ccells, cch), BF16),
            vmem((last - 1, ccells, cch), BF16),
            vmem((2, fch), F32),
            vmem((2, fch), F32),
            vmem((1, cch), F32),
            vmem((1, cch), F32),
            vmem((2, fch), F32),
            vmem((2, fch), F32),
            vmem((1, cch), F32),
            vmem((1, cch), F32),
            vmem((2 * ticks, fcells, fch), F32),
            vmem((ticks, ccells, cch), F32),
            vmem((fcells, fch), F32),
            vmem((ccells, cch), F32),
            vmem((fch // LANES, cside, 2 * fside, LANES), F32),
            vmem((fcells, 9 * fch), BF16),
            vmem((ccells, 9 * cch), BF16),
            vmem((ccells, 4 * fch), BF16),
            vmem((fcells, fch), BF16),
            vmem((fcells, fch), BF16),
            vmem((last - 1, ccells, cch), BF16),
            vmem((last - 1, ccells, cch), BF16),
            vmem((2 * ticks, frows, LANES), F32),
            vmem((ticks, crows, LANES), F32),
            vmem((2 * ticks, ndp - 1, frows, LANES), F32),
            vmem((ticks, ndp - 1, crows, LANES), F32),
            vmem((ndp, frows, LANES), F32),
            vmem((last - 1, ndp, crows, LANES), F32),
            dma((14,)),
            dma, dma((2 * ticks,)), dma, dma((ticks,)),
            dma, dma, dma, dma((last - 1,)),
            dma, dma, dma, dma((last - 1,)),
            dma, dma((ticks,)), dma, dma((last - 1,)), dma, dma((last - 1,)),
            dma((7,)), dma((7,)),
            pltpu.SemaphoreType.REGULAR,
        ],
        compiler_params=pltpu.CompilerParams(
            collective_id=0, has_side_effects=True, vmem_limit_bytes=56 << 20
        ),
    )(*args)
    return put_out(outs)


def hand_over_kernel(*refs):
    count = (len(refs) - 2) // 3
    sources, results, held = refs[:count], refs[count : 2 * count], refs[2 * count : 3 * count]
    in_sem, out_sem = refs[3 * count :]
    taken, given = [], []
    for i in range(count):
        for j in range(held[i].shape[0]):
            taken.append(pltpu.make_async_copy(sources[i].at[j], held[i].at[j], in_sem.at[i, j]))
            given.append(pltpu.make_async_copy(held[i].at[j], results[i].at[j], out_sem.at[i, j]))
    for item in taken:
        item.start()
    for item, other in zip(taken, given):
        item.wait()
        other.start()
    for item in given:
        item.wait()


def hand_over(arrays):
    most = max(array.shape[0] for array in arrays)
    any_spec = pl.BlockSpec(memory_space=pl.ANY)
    return pl.pallas_call(
        hand_over_kernel,
        out_shape=tuple(jax.ShapeDtypeStruct(a.shape, a.dtype) for a in arrays),
        in_specs=[any_spec] * len(arrays),
        out_specs=(any_spec,) * len(arrays),
        scratch_shapes=[pltpu.VMEM(a.shape, a.dtype) for a in arrays]
        + [pltpu.SemaphoreType.DMA((len(arrays), most))] * 2,
    )(*arrays)


def on_device(
    fine_inflow, coarse_inflow, fine_entries, fine_pending, coarse_pending,
    fine_kernels, fine_mixing, fine_gains, fine_shifts,
    coarse_kernel, coarse_mixing, coarse_gains, coarse_shifts,
    descent_kernel, upsample_kernel,
):
    nseg = lax.axis_size("segment")
    ndp = lax.axis_size("dp")
    half = nseg // 2
    ticks = fine_entries.shape[0] + 1
    hold_f, hold_c = fine_pending.shape[1], coarse_pending.shape[1]
    recv_f, recv_c = 3 * half - hold_f, half - hold_c
    fside, fch = fine_inflow.shape[3], fine_inflow.shape[4]
    cside, cch = coarse_inflow.shape[3], coarse_inflow.shape[4]
    fcells, ccells = fside * fside, cside * cside
    dims = (nseg, ndp, ticks, fside, cside, hold_f, recv_f, hold_c, recv_c)
    frows, crows = 2 * fch // LANES, 2 * cch // LANES
    any_spec = pl.BlockSpec(memory_space=pl.ANY)
    vmem_spec = pl.BlockSpec(memory_space=pltpu.VMEM)
    dma = pltpu.SemaphoreType.DMA
    args = (
        fine_inflow.reshape(fcells, fch),
        coarse_inflow.reshape(ccells, cch),
        fine_entries.reshape(ticks - 1, fcells, fch),
        fine_pending.reshape(hold_f, fcells, fch),
        coarse_pending.reshape(hold_c, ccells, cch),
        fine_kernels.reshape(2, 9 * fch, fch),
        fine_mixing.reshape(fch, fch),
        fine_gains.reshape(2, fch),
        fine_shifts.reshape(2, fch),
        coarse_kernel.reshape(9 * cch, cch),
        coarse_mixing.reshape(cch, cch),
        coarse_gains.reshape(1, cch),
        coarse_shifts.reshape(1, cch),
        descent_kernel.reshape(4 * fch, cch),
        upsample_kernel,
    )
    paired = nseg == 2 and ndp % 2 == 0 and recv_f == 1 and recv_c == 0
    if paired and ticks > hold_f + recv_f:
        fst, cst, fback, cback = run_pair(dims, fch, cch, args)
    else:
        outs = pl.pallas_call(
            functools.partial(kernel, dims),
            out_shape=(
                jax.ShapeDtypeStruct((ticks, fcells, fch), BF16),
                jax.ShapeDtypeStruct((ticks, ccells, cch), BF16),
                jax.ShapeDtypeStruct((hold_f, fcells, fch), BF16),
                jax.ShapeDtypeStruct((hold_c, ccells, cch), BF16),
            ),
            in_specs=[any_spec] * 7 + [vmem_spec] * 2 + [any_spec] * 2 + [vmem_spec] * 2 + [any_spec] * 2,
            out_specs=(any_spec,) * 4,
            scratch_shapes=[
                pltpu.VMEM((2, 9 * fch, fch), BF16),
                pltpu.VMEM((fch, fch), BF16),
                pltpu.VMEM((9 * cch, cch), BF16),
                pltpu.VMEM((cch, cch), BF16),
                pltpu.VMEM((4 * fch, cch), BF16),
                pltpu.VMEM((cch, 4 * fch), BF16),
                pltpu.VMEM((ticks, fcells, fch), BF16),
                pltpu.VMEM((ticks, ccells, cch), BF16),
                pltpu.VMEM((ticks, ccells, cch), BF16),
                pltpu.VMEM((max(hold_f, recv_f) + ticks, fcells, fch), BF16),
                pltpu.VMEM((max(hold_c, recv_c) + ticks, ccells, cch), BF16),
                pltpu.VMEM((ticks, fcells, fch), BF16),
                pltpu.VMEM((ticks, ccells, cch), BF16),
                pltpu.VMEM((ticks, ccells, cch), BF16),
                pltpu.VMEM((fcells, fch), F32),
                pltpu.VMEM((fcells, fch), F32),
                pltpu.VMEM((fcells, fch), F32),
                pltpu.VMEM((ccells, cch), F32),
                pltpu.VMEM((fch // LANES, cside, 2 * fside, LANES), F32),
                pltpu.VMEM((fcells, 9 * fch), BF16),
                pltpu.VMEM((ccells, 9 * cch), BF16),
                pltpu.VMEM((fcells, fch), BF16),
                pltpu.VMEM((ccells, cch), BF16),
                pltpu.VMEM((2 * ticks, frows, LANES), F32),
                pltpu.VMEM((ticks, crows, LANES), F32),
                pltpu.VMEM((2 * ticks, ndp - 1, frows, LANES), F32),
                pltpu.VMEM((ticks, ndp - 1, crows, LANES), F32),
                pltpu.VMEM((cch, 2, 2, fch), BF16),
                pltpu.VMEM((fch // LANES, 256, LANES), F32),
                dma((12,)),
                dma((4, max(ticks, hold_f, hold_c))),
                dma((ticks,)), dma((ticks,)), dma((ticks,)), dma((ticks,)), dma((ticks,)),
                dma((ticks,)), dma((ticks,)), dma((ticks,)), dma((ticks,)), dma((ticks,)),
                dma((2 * ticks,)), dma((ticks,)), dma((2 * ticks,)), dma((ticks,)),
            ],
            compiler_params=pltpu.CompilerParams(
                collective_id=0, has_side_effects=True, vmem_limit_bytes=56 << 20
            ),
        )(*args)
        fst, cst, fback, cback = hand_over(outs)
    return (
        fst.reshape(1, ticks, 1, fside, fside, fch),
        cst.reshape(1, ticks, 1, cside, cside, cch),
        fback.reshape(1, hold_f, 1, fside, fside, fch),
        cback.reshape(1, hold_c, 1, cside, cside, cch),
    )


def solution(mesh):
    placed = (
        P("segment", "dp", None, None, None),
        P("segment", "dp", None, None, None),
        P(None, "dp", None, None, None),
        P("segment", None, "dp", None, None, None),
        P("segment", None, "dp", None, None, None),
        P("segment", None, None, None, None, None),
        P("segment", None, None),
        P("segment", None, None),
        P("segment", None, None),
        P("segment", None, None, None, None),
        P("segment", None, None),
        P("segment", None),
        P("segment", None),
        P(),
        P(),
    )
    return jax.shard_map(
        on_device,
        mesh=mesh,
        in_specs=placed,
        out_specs=(
            P("segment", None, "dp", None, None, None),
            P("segment", None, "dp", None, None, None),
            P("segment", None, "dp", None, None, None),
            P("segment", None, "dp", None, None, None),
        ),
        check_vma=False,
    )
```

```python
import functools

import jax
import jax.numpy as jnp
from jax import lax
from jax.experimental import pallas as pl
from jax.experimental.pallas import tpu as pltpu
from jax.sharding import PartitionSpec as P

EPSILON = 1e-05
LANES = 128
MESH = pl.DeviceIdType.MESH
F32 = jnp.float32
BF16 = jnp.bfloat16


def dot(a, b):
    return jnp.dot(a, b, preferred_element_type=F32)


def side_shifts(x, side):
    cells = x.shape[0]
    column = lax.rem(lax.broadcasted_iota(jnp.int32, x.shape, 0), side)
    before = jnp.where(column == 0, 0.0, pltpu.roll(x, 1, 0))
    after = jnp.where(column == side - 1, 0.0, pltpu.roll(x, cells - 1, 0))
    return before, x, after


def spread_taps(x, cols, side):
    cells, width = x.shape
    edge = jnp.zeros((side, width), F32)
    for dc, part in enumerate(side_shifts(x, side)):
        above = jnp.concatenate([edge, part[: cells - side]], axis=0)
        below = jnp.concatenate([part[side:], edge], axis=0)
        for dr, moved in enumerate((above, part, below)):
            start = (3 * dr + dc) * width
            cols[:, start : start + width] = moved.astype(BF16)


def put_stats(h, out):
    width = h.shape[1]
    rows = width // LANES
    total = jnp.sum(h, axis=0, keepdims=True)
    square = jnp.sum(h * h, axis=0, keepdims=True)
    for row in range(rows):
        lanes = slice(row * LANES, (row + 1) * LANES)
        out[row : row + 1, :] = total[:, lanes]
        out[rows + row : rows + row + 1, :] = square[:, lanes]


def norm_terms(total, gain, shift, count):
    rows = total.shape[0] // 2
    sums = jnp.concatenate([total[row : row + 1] for row in range(rows)], axis=1)
    squares = jnp.concatenate([total[rows + row : rows + row + 1] for row in range(rows)], axis=1)
    center = sums * (1.0 / count)
    spread = jnp.maximum(squares * (1.0 / count) - center * center, 0.0)
    scale = lax.rsqrt(spread + EPSILON) * gain
    return scale, shift - center * scale


def kernel(
    dims,
    fine_in, coarse_in, entries, fine_pend, coarse_pend,
    wf_hbm, mixf_hbm, fgain, fshift, wc_hbm, mixc_hbm, cgain, cshift, wd_hbm, wu_hbm,
    fst_out, cst_out, fback_out, cback_out,
    wf, mixf, wc, mixc, wd, wu,
    fin, cin, upin, skf, skc, fst, cst, dbuf,
    xs, hf, hg, hc, upscr, colf, colc, zf, zc,
    statf, statc, gotf, gotc,
    wu4, wuf, load_sem, save_sem,
    fin_r, cin_r, up_r, skf_r, skc_r,
    fin_s, cin_s, up_s, skf_s, skc_s,
    gotf_r, gotc_r, statf_s, statc_s,
):
    nseg, ndp, ticks, fside, cside, hold_f, recv_f, hold_c, recv_c = dims
    half = nseg // 2
    seg = lax.axis_index("segment")
    me = lax.axis_index("dp")
    lower = seg < half
    upper = seg >= half
    turn = seg == half - 1
    after = lax.rem(seg + 1, nseg)
    mate = lax.rem(seg + half, nseg)

    def load(k, src, dst):
        return pltpu.make_async_copy(src, dst, load_sem.at[k])

    get_fine = load(0, fine_in, fin.at[0])
    get_wf0 = load(1, wf_hbm.at[0], wf.at[0])
    get_mixf = load(2, mixf_hbm, mixf)
    get_coarse = load(3, coarse_in, cin.at[0])
    get_mixc = load(4, mixc_hbm, mixc)
    get_wc = load(5, wc_hbm, wc)
    get_wf1 = load(6, wf_hbm.at[1], wf.at[1])
    get_wd = load(7, wd_hbm, wd)
    get_wu = load(11, wu_hbm, wu4)
    own_entries = load(8, entries, fin.at[pl.ds(1, ticks - 1)])
    own_fine = hold_f if hold_f > ticks else 0
    own_coarse = hold_c if hold_c > ticks else 0

    def own_pend(k, src, dst, count):
        return load(k, src.at[pl.ds(0, count)], dst.at[pl.ds(0, count)])

    barrier = pltpu.get_barrier_semaphore()
    offsets = sorted({1 % nseg, nseg - 1, half})

    def greet(k, carry):
        pl.semaphore_signal(
            barrier, inc=1, device_id=(seg, lax.rem(me + k, ndp)), device_id_type=MESH
        )
        return carry

    lax.fori_loop(1, ndp, greet, 0)
    for offset in offsets:
        pl.semaphore_signal(
            barrier, inc=1, device_id=(lax.rem(seg + offset, nseg), me), device_id_type=MESH
        )
    @pl.when(upper)
    def _():
        if recv_f:
            own_pend(9, fine_pend, skf, recv_f).start()

    for item in (get_fine, get_wf0, get_mixf, get_coarse, get_mixc, get_wc, get_wf1):
        item.start()

    @pl.when(lower)
    def _():
        if recv_c:
            own_pend(10, coarse_pend, skc, recv_c).start()
        if own_fine:
            own_pend(9, fine_pend, skf, own_fine).start()

    @pl.when(upper)
    def _():
        if own_coarse:
            own_pend(10, coarse_pend, skc, own_coarse).start()

    @pl.when(seg == 0)
    def _():
        own_entries.start()

    @pl.when(turn)
    def _():
        get_wd.start()

    @pl.when(seg == half)
    def _():
        get_wu.start()

    zf[...] = jnp.zeros_like(zf)
    zc[...] = jnp.zeros_like(zc)
    pl.semaphore_wait(barrier, ndp - 1 + len(offsets))

    def push(src, dst, ssem, rsem, to):
        return pltpu.make_async_remote_copy(
            src_ref=src, dst_ref=dst, send_sem=ssem, recv_sem=rsem,
            device_id=(to, me), device_id_type=MESH,
        )

    def send_skf(j):
        return push(skf.at[j], skf.at[recv_f + j], skf_s.at[j], skf_r.at[j], mate)

    def send_pend_f(j):
        return push(fine_pend.at[j], skf.at[recv_f + j], skf_s.at[j], skf_r.at[j], mate)

    def send_pend_c(j):
        return push(coarse_pend.at[j], skc.at[recv_c + j], skc_s.at[j], skc_r.at[j], mate)

    def send_skc(j):
        return push(skc.at[j], skc.at[recv_c + j], skc_s.at[j], skc_r.at[j], mate)

    def send_up(t):
        return push(cst.at[t], upin.at[t], up_s.at[t], up_r.at[t], after)

    def send_co(t):
        return push(cst.at[t], cin.at[t + 1], cin_s.at[t], cin_r.at[t], after)

    def send_down(t):
        return push(dbuf.at[t], cin.at[t + 1], cin_s.at[t], cin_r.at[t], after)

    def send_fo(t):
        return push(fst.at[t], fin.at[t + 1], fin_s.at[t], fin_r.at[t], after)

    def exchange(src, dst, ssem, rsem):
        def one(k, carry):
            pltpu.make_async_remote_copy(
                src_ref=src, dst_ref=dst.at[k - 1], send_sem=ssem, recv_sem=rsem,
                device_id=(seg, lax.rem(me + k, ndp)), device_id_type=MESH,
            ).start()
            return carry

        lax.fori_loop(1, ndp, one, 0)

    def whole(dst, ssem, rsem):
        return pltpu.make_async_remote_copy(
            src_ref=dst, dst_ref=dst, send_sem=ssem, recv_sem=rsem,
            device_id=(seg, lax.rem(me + 1, ndp)), device_id_type=MESH,
        )

    @pl.when(lower)
    def _():
        for j in range(min(hold_f, ticks)):
            send_pend_f(j).start()

    @pl.when(upper)
    def _():
        for j in range(min(hold_c, ticks)):
            send_pend_c(j).start()

    fcount = ndp * fside * fside
    ccount = ndp * cside * cside

    def save_f(t):
        return pltpu.make_async_copy(fst.at[t], fst_out.at[t], save_sem.at[0, t])

    def save_c(t):
        return pltpu.make_async_copy(cst.at[t], cst_out.at[t], save_sem.at[1, t])

    def first(t, *items):
        @pl.when(t == 0)
        def _():
            for item in items:
                item.wait()

    def front(t):
        first(t, get_fine, get_mixf)

        @pl.when(lower)
        def _():
            @pl.when(jnp.logical_and(seg > 0, t > 0))
            def _():
                send_fo(t - 1).wait_recv()

            xs[...] = fin[t].astype(F32)

        @pl.when(upper)
        def _():
            @pl.when(jnp.logical_and(seg == half, t > 0))
            def _():
                send_up(t - 1).wait_recv()
                spread = dot(upin[t - 1], wu[...])
                width = spread.shape[1] // 4
                for a in range(2):
                    for c in range(2):
                        start = (2 * a + c) * width
                        part = spread[:, start : start + width].reshape(cside, cside, width)
                        for i in range(width // LANES):
                            lanes = slice(i * LANES, (i + 1) * LANES)
                            upscr[i, :, pl.ds(a * fside + c, cside, stride=2), :] = part[:, :, lanes]
                for i in range(width // LANES):
                    lanes = slice(i * LANES, (i + 1) * LANES)
                    fin[t, :, lanes] = upscr[i].reshape(fside * fside, LANES).astype(BF16)

            @pl.when(jnp.logical_and(seg != half, t > 0))
            def _():
                send_fo(t - 1).wait_recv()

            if recv_f:
                first(t, own_pend(9, fine_pend, skf, recv_f))

            @pl.when(t >= recv_f)
            def _():
                send_skf(t - recv_f).wait_recv()

            xs[...] = (dot(fin[t], mixf[...]) + skf[t].astype(F32)).astype(BF16).astype(F32)

        spread_taps(xs[...], colf, fside)
        first(t, get_wf0)
        hf[...] = dot(colf[...], wf[0])
        put_stats(hf[...], statf.at[2 * t])
        exchange(statf.at[2 * t], gotf.at[2 * t], statf_s.at[2 * t], gotf_r.at[2 * t])

    def later(which, t):
        @pl.when(jnp.logical_and(which, t < ticks - 1))
        def _():
            front(t + 1)

    def own_pieces(t):
        @pl.when(t == 0)
        def _():
            get_wf1.wait()

            @pl.when(turn)
            def _():
                get_wd.wait()

            @pl.when(seg == 0)
            def _():
                own_entries.wait()

            @pl.when(seg == half)
            def _():
                get_wu.wait()
                width = wu4.shape[3]
                depth = wuf.shape[1] // 4

                def rows_of(n, carry):
                    rows = pl.multiple_of(n * depth, depth)
                    piece = wu4[pl.ds(rows, depth)].astype(F32).reshape(4 * depth, width)
                    for i in range(width // LANES):
                        wuf[i] = piece[:, i * LANES : (i + 1) * LANES]
                    for q in range(4):
                        for i in range(width // LANES):
                            start = q * width + i * LANES
                            part = wuf[i, pl.ds(q, depth, stride=4), :]
                            wu[pl.ds(rows, depth), start : start + LANES] = part.astype(BF16)
                    return carry

                lax.fori_loop(0, wu4.shape[0] // depth, rows_of, 0)

    front(jnp.int32(0))
    own_pieces(jnp.int32(0))

    def tick(t, carry):
        first(t, get_coarse, get_mixc)

        @pl.when(t > 0)
        def _():
            send_co(t - 1).wait_recv()

        @pl.when(lower)
        def _():
            if recv_c:
                first(t, own_pend(10, coarse_pend, skc, recv_c))

            @pl.when(t >= recv_c)
            def _():
                send_skc(t - recv_c).wait_recv()

            hc[...] = (dot(cin[t], mixc[...]) + skc[t].astype(F32)).astype(BF16).astype(F32)

        @pl.when(upper)
        def _():
            hc[...] = cin[t].astype(F32)

        spread_taps(hc[...], colc, cside)
        first(t, get_wc)
        hc[...] = dot(colc[...], wc[...])
        put_stats(hc[...], statc.at[t])
        exchange(statc.at[t], gotc.at[t], statc_s.at[t], gotc_r.at[t])

        whole(gotf.at[2 * t], statf_s.at[2 * t], gotf_r.at[2 * t]).wait_recv()
        total = statf[2 * t] + jnp.sum(gotf[2 * t], axis=0)
        scale, offset = norm_terms(total, fgain[0:1, :], fshift[0:1, :], fcount)
        xs[...] = jnp.maximum(hf[...] * scale + offset, 0.0).astype(BF16).astype(F32)
        spread_taps(xs[...], colf, fside)
        hg[...] = dot(colf[...], wf[1])
        put_stats(hg[...], statf.at[2 * t + 1])
        exchange(
            statf.at[2 * t + 1], gotf.at[2 * t + 1], statf_s.at[2 * t + 1], gotf_r.at[2 * t + 1]
        )

        whole(gotc.at[t], statc_s.at[t], gotc_r.at[t]).wait_recv()
        total = statc[t] + jnp.sum(gotc[t], axis=0)
        scale, offset = norm_terms(total, cgain[...], cshift[...], ccount)
        cst[t] = jnp.maximum(hc[...] * scale + offset, 0.0).astype(BF16)

        @pl.when(t < ticks - 1)
        def _():
            @pl.when(turn)
            def _():
                send_up(t).start()

            @pl.when(jnp.logical_not(turn))
            def _():
                send_co(t).start()

        save_c(t).start()

        @pl.when(upper)
        def _():
            skc[hold_c + t] = dot(cst[t], mixc[...]).astype(BF16)

            @pl.when(hold_c + t < ticks)
            def _():
                send_skc(hold_c + t).start()

        later(seg == 0, t)

        whole(gotf.at[2 * t + 1], statf_s.at[2 * t + 1], gotf_r.at[2 * t + 1]).wait_recv()
        total = statf[2 * t + 1] + jnp.sum(gotf[2 * t + 1], axis=0)
        scale, offset = norm_terms(total, fgain[1:2, :], fshift[1:2, :], fcount)
        fst[t] = jnp.maximum(hg[...] * scale + offset, 0.0).astype(BF16)

        @pl.when(t < ticks - 1)
        def _():
            @pl.when(turn)
            def _():
                width = fst.shape[2]
                for i in range(width // LANES):
                    lanes = slice(i * LANES, (i + 1) * LANES)
                    upscr[i] = fst[t, :, lanes].astype(F32).reshape(cside, 2 * fside, LANES)
                lowered = None
                for a in range(2):
                    for c in range(2):
                        for i in range(width // LANES):
                            part = upscr[i, :, pl.ds(a * fside + c, cside, stride=2), :]
                            part = part.reshape(cside * cside, LANES).astype(BF16)
                            start = (2 * a + c) * width + i * LANES
                            term = dot(part, wd[start : start + LANES, :])
                            lowered = term if lowered is None else lowered + term
                dbuf[t] = lowered.astype(BF16)
                send_down(t).start()

            @pl.when(jnp.logical_and(jnp.logical_not(turn), seg < nseg - 1))
            def _():
                send_fo(t).start()

        save_f(t).start()

        @pl.when(lower)
        def _():
            skf[hold_f + t] = dot(fst[t], mixf[...]).astype(BF16)

            @pl.when(hold_f + t < ticks)
            def _():
                send_skf(hold_f + t).start()

        later(seg > 0, t)
        return carry

    lax.fori_loop(0, ticks, tick, 0)

    def back_f(first, src):
        return pltpu.make_async_copy(src, fback_out.at[first], save_sem.at[2, first])

    def back_c(first, src):
        return pltpu.make_async_copy(src, cback_out.at[first], save_sem.at[3, first])

    lower_backs = [back_f(j, skf.at[ticks + j]) for j in range(hold_f)]
    lower_backs += [
        back_c(j, skc.at[ticks + j] if j < recv_c else zc) for j in range(hold_c)
    ]
    upper_backs = [
        back_f(j, skf.at[ticks + j] if j < recv_f else zf) for j in range(hold_f)
    ]
    upper_backs += [back_c(j, skc.at[ticks + j]) for j in range(hold_c)]

    @pl.when(lower)
    def _():
        if own_fine:
            own_pend(9, fine_pend, skf, own_fine).wait()
        for j in range(max(ticks - recv_c, 0), ticks):
            send_skc(j).wait_recv()
        for item in lower_backs:
            item.start()
        for j in range(ticks):
            send_skf(j).wait_send()
        for item in lower_backs:
            item.wait()

    @pl.when(upper)
    def _():
        if own_coarse:
            own_pend(10, coarse_pend, skc, own_coarse).wait()
        for j in range(max(ticks - recv_f, 0), ticks):
            send_skf(j).wait_recv()
        for item in upper_backs:
            item.start()
        for j in range(ticks):
            send_skc(j).wait_send()
        for item in upper_backs:
            item.wait()

    @pl.when(turn)
    def _():
        for t in range(ticks - 1):
            send_up(t).wait_send()

    @pl.when(jnp.logical_and(jnp.logical_not(turn), seg < nseg - 1))
    def _():
        for t in range(ticks - 1):
            send_fo(t).wait_send()

    for t in range(ticks - 1):
        send_co(t).wait_send()
    for t in range(ticks):
        whole(gotf.at[2 * t], statf_s.at[2 * t], gotf_r.at[2 * t]).wait_send()
        whole(gotf.at[2 * t + 1], statf_s.at[2 * t + 1], gotf_r.at[2 * t + 1]).wait_send()
        whole(gotc.at[t], statc_s.at[t], gotc_r.at[t]).wait_send()
        save_f(t).wait()
        save_c(t).wait()


def sums_of(total):
    rows = total.shape[0] // 2
    sums = jnp.concatenate([total[row : row + 1] for row in range(rows)], axis=1)
    squares = jnp.concatenate([total[rows + row : rows + row + 1] for row in range(rows)], axis=1)
    return sums, squares


def moments(total, count):
    sums, squares = sums_of(total)
    center = sums * (1.0 / count)
    spread = jnp.maximum(squares * (1.0 / count) - center * center, 0.0)
    return center, lax.rsqrt(spread + EPSILON)


def pair_kernel(
    dims,
    fine_in, coarse_in, entries, fine_pend, coarse_pend,
    wf_hbm, mixf_hbm, fgain_hbm, fshift_hbm, wc_hbm, mixc_hbm, cgain_hbm, cshift_hbm,
    wd_hbm, wu_hbm,
    fst, cst, fback, cback,
    wf, mixf, mixe, wc, mixc, mixm, wd, wu, wu4, wuf,
    fin, cin, skf, skc, dbuf, dbuf_in, co_in, ec_out, ec_in, fnorm, cnorm, mate_fnorm, mate_cnorm,
    hf, hc, xs, hx, upscr, colf, colc, cold,
    rawf_out, rawf_in, rawc_out, rawc_in,
    stf, stc, gotf, gotc, farf, farc,
    fsum_out, fsum_in,
    load_sem, rf, rc, rfarf, rfarc, rrawf, rrawc, skf_r, dbuf_r, co_r, one_s, one_r, ready,
):
    nseg, ndp, ticks, fside, cside, hold_f, recv_f, hold_c, recv_c = dims
    seg = lax.axis_index("segment")
    me = lax.axis_index("dp")
    other = 1 - seg
    lower = seg == 0
    upper = seg == 1
    fcells, ccells = fside * fside, cside * cside
    fcount, ccount = ndp * fcells, ndp * ccells
    last = ticks - 1
    fgain, fshift, cgain, cshift = fnorm.at[0], fnorm.at[1], cnorm.at[0], cnorm.at[1]
    sf, skf_s, co_s, sc, sfarf = (load_sem.at[k] for k in range(5))
    sfarc, srawf, srawc, dbuf_s = (load_sem.at[k] for k in range(5, 9))

    barrier = pltpu.get_barrier_semaphore()

    bits = ndp.bit_length() - 1

    def partner(k):
        if 1 << bits != ndp:
            return lax.rem(me + k, ndp)
        to = 0
        for b in range(bits):
            bit = lax.rem(lax.div(me, 1 << b), 2)
            to = to + (1 << b) * (1 - bit if (k >> b) & 1 else bit)
        return to

    partners = [partner(k) for k in range(ndp)]
    twin = me + 1 - 2 * lax.rem(me, 2)
    for k in range(ndp - 1, 0, -1):
        pl.semaphore_signal(barrier, inc=1, device_id=(seg, partners[k]), device_id_type=MESH)
    pl.semaphore_signal(barrier, inc=1, device_id=(other, me), device_id_type=MESH)

    def load(k, src, dst):
        return pltpu.make_async_copy(src, dst, load_sem.at[k])

    get_fine = load(0, fine_in, fin.at[0])
    get_wf0 = load(1, wf_hbm.at[0], wf.at[0])
    get_mixf = load(2, mixf_hbm, mixf)
    get_coarse = load(3, coarse_in, cin)
    get_wc = load(4, wc_hbm, wc)
    get_wf1 = load(5, wf_hbm.at[1], wf.at[1])
    get_wd = load(6, wd_hbm, wd)
    get_entries = load(7, entries, fin.at[pl.ds(1, last)])
    get_pend = load(7, fine_pend.at[pl.ds(0, recv_f)], skf.at[pl.ds(0, recv_f)])
    get_norms = [
        load(8, fgain_hbm, fgain), load(8, fshift_hbm, fshift),
        load(9, cgain_hbm, cgain), load(9, cshift_hbm, cshift),
    ]
    have_norms = [load(8, fnorm, fnorm), load(9, cnorm, cnorm)]
    get_mixc = load(10, mixc_hbm, mixc)
    get_wu = load(11, wu_hbm, wu4)

    get_fine.start()

    @pl.when(upper)
    def _():
        get_mixf.start()
        get_pend.start()

    get_wf0.start()

    @pl.when(lower)
    def _():
        for item in (get_entries, get_wf1, get_mixf, get_coarse, get_mixc, get_wc, get_wd):
            item.start()

    @pl.when(upper)
    def _():
        for item in (get_coarse, get_wc, get_wf1, get_wd, get_wu, get_mixc):
            item.start()

    for item in get_norms:
        item.start()

    def push(src, dst, ssem, rsem):
        return pltpu.make_async_remote_copy(
            src_ref=src, dst_ref=dst, send_sem=ssem, recv_sem=rsem,
            device_id=(other, me), device_id_type=MESH,
        )

    def share(src, dst, ssem, rsem):
        for k in range(ndp - 1, 0, -1):
            pltpu.make_async_remote_copy(
                src_ref=src, dst_ref=dst.at[k - 1], send_sem=ssem, recv_sem=rsem,
                device_id=(seg, partners[k]), device_id_type=MESH,
            ).start()

    def cast_far(src, dst, ssem, rsem, step=1):
        for k in range(ndp - step, -1, -step):
            pltpu.make_async_remote_copy(
                src_ref=src, dst_ref=dst.at[k // step], send_sem=ssem, recv_sem=rsem,
                device_id=(other, partners[k]), device_id_type=MESH,
            ).start()

    def of_f(n):
        return push(gotf.at[n], gotf.at[n], sf, rf.at[n])

    def of_c(t):
        return push(gotc.at[t], gotc.at[t], sc, rc.at[t])

    of_farf = push(farf, farf, sfarf, rfarf)
    send_rawf = push(rawf_out, rawf_in, srawf, rrawf)

    def of_farc(t):
        return push(farc.at[t - 1], farc.at[t - 1], sfarc, rfarc.at[t - 1])

    def send_rawc(t):
        return push(rawc_out.at[t - 1], rawc_in.at[t - 1], srawc, rrawc.at[t - 1])

    def send_down(t):
        return push(dbuf.at[t - 1], dbuf_in.at[t - 1], dbuf_s, dbuf_r.at[t - 1])

    def send_co(t):
        return push(cst.at[t], co_in.at[t], co_s, co_r.at[t])

    def send_skf(j):
        return push(skf.at[j], skf.at[recv_f + j], skf_s, skf_r.at[j])

    def send_pend_f(j):
        return push(fine_pend.at[j], skf.at[recv_f + j], skf_s, skf_r.at[j])

    send_pend_c = push(coarse_pend.at[0], skc, one_s.at[0], one_r.at[0])

    def rows_of(matrix, device):
        part = matrix.shape[0] // 2
        return pl.ds(pl.multiple_of(lax.rem(device, 2) * part, part), part)

    def send_half(src, dst):
        rows = rows_of(dst, me)
        return push(src.at[rows], dst.at[rows], one_s.at[1], one_r.at[1])

    def hand_half(matrix, device):
        rows = rows_of(matrix, device)
        return pltpu.make_async_remote_copy(
            src_ref=matrix.at[rows], dst_ref=matrix.at[rows],
            send_sem=one_s.at[4], recv_sem=one_r.at[4],
            device_id=(seg, twin), device_id_type=MESH,
        )

    def send_mixc(piece):
        part = mixm.shape[0] // 8
        start = (4 * lax.rem(me, 2) + 3 * piece) * part
        rows = pl.ds(pl.multiple_of(start, part), (1 if piece else 3) * part)
        return push(mixc_hbm.at[rows], mixm.at[rows], one_s.at[1], one_r.at[1])

    all_mixc = send_half(mixc_hbm, mixm)
    send_mixf = send_half(mixf_hbm, mixe)
    send_norms = [
        push(fnorm, mate_fnorm, one_s.at[2], one_r.at[2]),
        push(cnorm, mate_cnorm, one_s.at[3], one_r.at[3]),
    ]
    send_ec = push(ec_out, ec_in, one_s.at[5], one_r.at[5])
    share_sum = pltpu.make_async_remote_copy(
        src_ref=fsum_out, dst_ref=fsum_in, send_sem=one_s.at[6], recv_sem=one_r.at[6],
        device_id=(seg, twin), device_id_type=MESH,
    )

    def conv_fine(layer, out):
        spread_taps(xs[...], colf, fside)
        out[...] = dot(colf[...], wf[layer])

    def centred(h, stats, cells):
        sums, _ = sums_of(stats)
        return (h - sums * (1.0 / cells)).astype(BF16)

    def arrived(raw, got, mine, gain, shift, count, cells):
        center, inverse = moments(got, count)
        own, _ = sums_of(mine)
        scale = inverse * gain
        offset = shift + (own * (1.0 / cells) - center) * scale
        return jnp.maximum(raw[...].astype(F32) * scale + offset, 0.0).astype(BF16)

    def descended(x):
        width = x.shape[1]
        for i in range(width // LANES):
            lanes = slice(i * LANES, (i + 1) * LANES)
            upscr[i] = x[:, lanes].reshape(cside, 2 * fside, LANES)
        for a in range(2):
            for c in range(2):
                for i in range(width // LANES):
                    piece = upscr[i, :, pl.ds(a * fside + c, cside, stride=2), :]
                    start = (2 * a + c) * width + i * LANES
                    cold[:, start : start + LANES] = piece.reshape(ccells, LANES).astype(BF16)
        return dot(cold[...], wd[...]).astype(BF16)

    def normed(h, stats, got, gain, shift, count):
        center, inverse = moments(stats[...] + jnp.sum(got[...], axis=0), count)
        scale = inverse * gain
        return jnp.maximum(h[...] * scale + (shift - center * scale), 0.0).astype(BF16)

    def share_fine(n):
        share(stf.at[n], gotf.at[n], sf, rf.at[n])

    def conv_stats(layer, n):
        conv_fine(layer, hf.at[n])
        put_stats(hf[n], stf.at[n])

    def take_first(t):
        xs[...] = normed(
            hf.at[t], stf.at[t], gotf.at[t], fgain[0:1, :], fshift[0:1, :], fcount
        ).astype(F32)

    def finish_fine(t):
        n = ticks + t
        of_f(n).wait_recv()
        fst[t] = normed(hf.at[n], stf.at[n], gotf.at[n], fgain[1:2, :], fshift[1:2, :], fcount)

    def finish_coarse(t):
        of_c(t).wait_recv()
        cst[t] = normed(hc.at[t], stc.at[t], gotc.at[t], cgain[...], cshift[...], ccount)

    def coarse(t, raw):
        spread_taps(hx[...], colc, cside)
        hc[t] = dot(colc[...], wc[...])
        put_stats(hc[t], stc.at[t])

        @pl.when(raw)
        def _():
            cast_far(stc.at[t], farc.at[t - 1], sfarc, rfarc.at[t - 1])
            rawc_out[t - 1] = centred(hc[t], stc[t], ccells)
            send_rawc(t).start()

        share(stc.at[t], gotc.at[t], sc, rc.at[t])

    def mate_coarse(t):
        of_farc(t).wait_recv()
        send_rawc(t).wait_recv()
        return arrived(
            rawc_in.at[t - 1], jnp.sum(farc[t - 1], axis=0), farc[t - 1, 0], mate_cnorm[0],
            mate_cnorm[1], ccount, ccells,
        )

    def sent():
        for item in send_norms:
            item.wait_send()
        push(gotc, gotc, sc, rc.at[0]).wait_send()

    get_fine.wait()

    @pl.when(lower)
    def _():
        xs[...] = fin[0].astype(F32)

    @pl.when(upper)
    def _():
        get_mixf.wait()
        get_pend.wait()
        xs[...] = (dot(fin[0], mixf[...]) + skf[0].astype(F32)).astype(BF16).astype(F32)

    get_wf0.wait()
    conv_stats(0, 0)
    pl.semaphore_wait(barrier, ndp)
    share_fine(0)
    pl.semaphore_signal(ready, inc=1, device_id=(other, me), device_id_type=MESH)

    @pl.when(lower)
    def _():
        send_pend_f(0).start()
        send_mixf.start()
        get_entries.wait()

        def early(t, carry):
            xs[...] = fin[t].astype(F32)
            conv_stats(0, t)
            return carry

        lax.fori_loop(1, ticks, early, 0)
        rest = pl.ds(1, last)
        for k in range(ndp - 1, 0, -1):
            pltpu.make_async_remote_copy(
                src_ref=stf.at[rest], dst_ref=gotf.at[rest, k - 1], send_sem=sf, recv_sem=rf.at[1],
                device_id=(seg, partners[k]), device_id_type=MESH,
            ).start()
        for item in (get_wf1, get_mixf, get_coarse, get_mixc, get_wc, get_wd, *have_norms):
            item.wait()
        for item in send_norms:
            item.start()
        pl.semaphore_wait(ready, 1)

        def term(n, carry):
            t = jnp.where(n < last - 1, n + 1, jnp.where(n == last, last, 0))
            finish_fine(t)

            @pl.when(jnp.logical_and(t > 0, t < last))
            def _():
                dbuf[t - 1] = descended(fst[t].astype(F32))
                send_down(t).start()

            @pl.when(t > 0)
            def _():
                fresh = dot(fst[t], mixf[...]).astype(BF16)

                @pl.when(hold_f + t < ticks)
                def _():
                    skf[hold_f + t] = fresh

                @pl.when(hold_f + t >= ticks)
                def _():
                    fback[hold_f + t - ticks] = fresh

            return carry

        def encode(i, carry):
            t = jnp.maximum(i - last + 1, 0)

            @pl.when(i < ticks)
            def _():
                @pl.when(i == 0)
                def _():
                    of_f(0).wait_recv()

                @pl.when(i == 1)
                def _():
                    push(gotf.at[rest], gotf.at[rest], sf, rf.at[1]).wait_recv()

                take_first(i)
                conv_stats(1, ticks + i)

                @pl.when(i == 0)
                def _():
                    cast_far(stf.at[ticks], farf, sfarf, rfarf, 2)
                    rawf_out[...] = centred(hf[ticks], stf[ticks], fcells)
                    send_rawf.start()

                share_fine(ticks + i)

                @pl.when(i == 1)
                def _():
                    for j in range(1, hold_f):
                        send_pend_f(j).start()

            @pl.when(i == 0)
            def _():
                send_pend_c.wait_recv()
                hx[...] = (dot(cin[...], mixc[...]) + skc[...].astype(F32)).astype(BF16).astype(F32)

            @pl.when(i == last)
            def _():
                finish_coarse(0)
                send_co(0).start()
                for item in send_norms:
                    item.wait_recv()
                send_co(0).wait_recv()
                send_ec.wait_recv()
                hx[...] = (dot(co_in[0], mixc[...]) + ec_in[...].astype(F32)).astype(BF16).astype(F32)

            @pl.when(i > last)
            def _():
                @pl.when(i == last + 1)
                def _():
                    hand_half(mixm, twin).wait_recv()
                    hand_half(mixm, me).wait_send()
                    mixm[...] = (mixm[...].astype(F32) + mixc[...].astype(F32)).astype(BF16)

                finish_coarse(t - 1)

                @pl.when(t < last)
                def _():
                    send_co(t - 1).start()

                hx[...] = dot(mate_coarse(t - 1), mixm[...]).astype(BF16).astype(F32)

            @pl.when(jnp.logical_or(i == 0, i >= last))
            def _():
                coarse(t, t == last - 1)

            @pl.when(i == last)
            def _():
                lax.fori_loop(0, ticks - 1, term, 0)
                all_mixc.wait_recv()
                hand_half(mixm, me).start()
                term(last, 0)

            @pl.when(t == last)
            def _():
                for j in range(hold_f + 1, ticks):
                    send_skf(j).start()

            return carry

        lax.fori_loop(0, 2 * ticks - 2, encode, 0)
        cback[...] = jnp.zeros_like(cback)
        of_farf.wait_send()
        send_rawf.wait_send()
        of_farc(last - 1).wait_send()
        send_rawc(last - 1).wait_send()
        push(co_in, co_in, co_s, co_r.at[0]).wait_send()
        push(dbuf, dbuf_in, dbuf_s, dbuf_r.at[0]).wait_send()
        terms = skf.at[pl.ds(0, ticks - 1)]
        push(terms, terms, skf_s, skf_r.at[0]).wait_send()
        send_mixf.wait_send()
        sent()
        finish_coarse(last)

    @pl.when(upper)
    def _():
        send_pend_c.start()
        send_mixc(0).start()
        get_coarse.wait()
        get_wc.wait()

        def spread_weights():
            width = wu4.shape[3]
            depth = wuf.shape[1] // 4

            def rows_of(n, carry):
                rows = pl.multiple_of(n * depth, depth)
                piece = wu4[pl.ds(rows, depth)].astype(F32).reshape(4 * depth, width)
                for i in range(width // LANES):
                    wuf[i] = piece[:, i * LANES : (i + 1) * LANES]
                for q in range(4):
                    for i in range(width // LANES):
                        start = q * width + i * LANES
                        part = wuf[i, pl.ds(q, depth, stride=4), :]
                        wu[pl.ds(rows, depth), start : start + LANES] = part.astype(BF16)
                return carry

            lax.fori_loop(0, wu4.shape[0] // depth, rows_of, 0)

        pl.semaphore_wait(ready, 1)

        def encode(t, carry):
            @pl.when(t == 0)
            def _():
                hx[...] = cin[...].astype(F32)

            @pl.when(t == 1)
            def _():
                for item in send_norms:
                    item.wait_recv()
                of_farf.wait_recv()
                fsum_out[...] = jnp.sum(farf[...], axis=0)
                share_sum.start()
                send_rawf.wait_recv()
                share_sum.wait_recv()
                send_mixc(1).start()
                taken = arrived(
                    rawf_in, fsum_out[...] + fsum_in[...], farf[0], mate_fnorm[0, 1:2, :],
                    mate_fnorm[1, 1:2, :], fcount, fcells,
                )
                fin[0] = taken
                hx[...] = descended(taken.astype(F32)).astype(F32)

            @pl.when(t > 1)
            def _():
                send_down(t - 1).wait_recv()
                hx[...] = dbuf_in[t - 2].astype(F32)

            coarse(t, jnp.logical_and(t > 0, t < last))
            return carry

        def raised(taken, t):
            spread = dot(taken, wu[...])
            width = spread.shape[1] // 4
            for a in range(2):
                for c in range(2):
                    start = (2 * a + c) * width
                    part = spread[:, start : start + width].reshape(cside, cside, width)
                    for i in range(width // LANES):
                        lanes = slice(i * LANES, (i + 1) * LANES)
                        upscr[i, :, pl.ds(a * fside + c, cside, stride=2), :] = part[:, :, lanes]
            for i in range(width // LANES):
                lanes = slice(i * LANES, (i + 1) * LANES)
                part = upscr[i].reshape(fcells, LANES) + skf[t, :, lanes].astype(F32)
                xs[:, lanes] = part.astype(BF16).astype(F32)

        def step(o, carry):
            coarse_end = jnp.where(o < 2, o + 1, jnp.where(o == 2, ticks, o))
            lax.fori_loop(o, coarse_end, encode, 0)
            half_o = lax.div(o, 2)
            odd = lax.rem(o, 2) == 1
            is_first = jnp.logical_or(
                o == 1, jnp.logical_and(jnp.logical_and(o > 1, o < 2 * last), jnp.logical_not(odd))
            )
            t = jnp.where(
                o == 0, 0, jnp.where(is_first, jnp.where(o == 1, 1, half_o + 1),
                                     jnp.where(o == 2 * last, last, half_o))
            )

            @pl.when(o == 0)
            def _():
                for item in (get_wf1, get_wd, get_wu, get_mixc, *have_norms):
                    item.wait()
                for item in send_norms:
                    item.start()
                spread_weights()
                width = mixf.shape[0]
                for q in range(4):
                    lanes = slice(q * width, (q + 1) * width)
                    wu[:, lanes] = dot(wu[:, lanes], mixf[...]).astype(BF16)

            @pl.when(o == 1)
            def _():
                finish_fine(0)
                hand_half(mixe, twin).wait_recv()
                skf[recv_f + hold_f] = dot(fin[0], mixe[...]).astype(BF16)

            @pl.when(o == 2)
            def _():
                finish_coarse(1)

            @pl.when(is_first)
            def _():
                @pl.when(t - recv_f != hold_f)
                def _():
                    send_skf(t - recv_f).wait_recv()

                @pl.when(t < last)
                def _():
                    send_co(t - 1).wait_recv()
                    raised(co_in[t - 1], t)

                @pl.when(t == last)
                def _():
                    raised(mate_coarse(t - 1), t)

            @pl.when(jnp.logical_not(is_first))
            def _():
                of_f(t).wait_recv()
                take_first(t)

            layer = jnp.where(is_first, 0, 1)
            n = layer * ticks + t
            conv_stats(layer, n)
            share_fine(n)

            @pl.when(o == 0)
            def _():
                finish_coarse(0)
                send_co(0).start()
                ec_out[...] = dot(cst[0], mixc[...]).astype(BF16)
                send_ec.start()
                send_mixf.wait_recv()
                hand_half(mixe, me).start()

            @pl.when(o == 2 * last - 2)
            def _():
                def rest(n, c):
                    finish_coarse(n)
                    return c

                lax.fori_loop(2, ticks, rest, 0)
                cback[0] = dot(cst[last], mixc[...]).astype(BF16)

            return carry

        lax.fori_loop(0, 2 * ticks - 1, step, 0)

        def rest_fine(n, c):
            finish_fine(n)
            return c

        lax.fori_loop(1, last - 1, rest_fine, 0)
        for j in range(max(ticks - recv_f, 0), ticks):
            send_skf(j).wait_recv()
        for j in range(hold_f):
            fback[j] = skf[ticks + j] if j < recv_f else jnp.zeros_like(skf[0])
        finish_fine(last - 1)
        send_pend_c.wait_send()
        all_mixc.wait_send()
        send_ec.wait_send()
        share_sum.wait_send()
        hand_half(mixe, me).wait_send()
        send_co(0).wait_send()
        push(farc, farc, sfarc, rfarc.at[0]).wait_send()
        push(rawc_in, rawc_in, srawc, rrawc.at[0]).wait_send()
        sent()
        finish_fine(last)

    push(gotf, gotf, sf, rf.at[0]).wait_send()


def put_out_kernel(*refs):
    count = (len(refs) - 1) // 2
    sources, results, sem = refs[:count], refs[count : 2 * count], refs[2 * count]
    given = [
        pltpu.make_async_copy(source, result, sem.at[i])
        for i, (source, result) in enumerate(zip(sources, results))
    ]
    for item in given:
        item.start()
    for item in given:
        item.wait()


def put_out(arrays):
    any_spec = pl.BlockSpec(memory_space=pl.ANY)
    vmem_spec = pl.BlockSpec(memory_space=pltpu.VMEM)
    held = [pltpu.with_memory_space_constraint(a, pltpu.VMEM) for a in arrays]
    return pl.pallas_call(
        put_out_kernel,
        out_shape=tuple(jax.ShapeDtypeStruct(a.shape, a.dtype) for a in arrays),
        in_specs=[vmem_spec] * len(arrays),
        out_specs=(any_spec,) * len(arrays),
        scratch_shapes=[pltpu.SemaphoreType.DMA((len(arrays),))],
    )(*held)


def run_pair(dims, fch, cch, args):
    nseg, ndp, ticks, fside, cside, hold_f, recv_f, hold_c, recv_c = dims
    fcells, ccells = fside * fside, cside * cside
    frows, crows = 2 * fch // LANES, 2 * cch // LANES
    last = ticks - 1
    any_spec = pl.BlockSpec(memory_space=pl.ANY)
    vmem_spec = pl.BlockSpec(memory_space=pltpu.VMEM)
    dma, vmem = pltpu.SemaphoreType.DMA, pltpu.VMEM
    outs = pl.pallas_call(
        functools.partial(pair_kernel, dims),
        out_shape=(
            vmem((ticks, fcells, fch), BF16),
            vmem((ticks, ccells, cch), BF16),
            vmem((hold_f, fcells, fch), BF16),
            vmem((hold_c, ccells, cch), BF16),
        ),
        in_specs=[any_spec] * 15,
        out_specs=(vmem_spec,) * 4,
        scratch_shapes=[
            vmem((2, 9 * fch, fch), BF16),
            vmem((fch, fch), BF16),
            vmem((fch, fch), BF16),
            vmem((9 * cch, cch), BF16),
            vmem((cch, cch), BF16),
            vmem((cch, cch), BF16),
            vmem((4 * fch, cch), BF16),
            vmem((cch, 4 * fch), BF16),
            vmem((cch, 2, 2, fch), BF16),
            vmem((fch // LANES, 256, LANES), F32),
            vmem((ticks, fcells, fch), BF16),
            vmem((ccells, cch), BF16),
            vmem((max(hold_f, recv_f) + ticks, fcells, fch), BF16),
            vmem((ccells, cch), BF16),
            vmem((last - 1, ccells, cch), BF16),
            vmem((last - 1, ccells, cch), BF16),
            vmem((last - 1, ccells, cch), BF16),
            vmem((ccells, cch), BF16),
            vmem((ccells, cch), BF16),
            vmem((2, 2, fch), F32),
            vmem((2, 1, cch), F32),
            vmem((2, 2, fch), F32),
            vmem((2, 1, cch), F32),
            vmem((2 * ticks, fcells, fch), F32),
            vmem((ticks, ccells, cch), F32),
            vmem((fcells, fch), F32),
            vmem((ccells, cch), F32),
            vmem((fch // LANES, cside, 2 * fside, LANES), F32),
            vmem((fcells, 9 * fch), BF16),
            vmem((ccells, 9 * cch), BF16),
            vmem((ccells, 4 * fch), BF16),
            vmem((fcells, fch), BF16),
            vmem((fcells, fch), BF16),
            vmem((last - 1, ccells, cch), BF16),
            vmem((last - 1, ccells, cch), BF16),
            vmem((2 * ticks, frows, LANES), F32),
            vmem((ticks, crows, LANES), F32),
            vmem((2 * ticks, ndp - 1, frows, LANES), F32),
            vmem((ticks, ndp - 1, crows, LANES), F32),
            vmem((ndp // 2, frows, LANES), F32),
            vmem((last - 1, ndp, crows, LANES), F32),
            vmem((frows, LANES), F32),
            vmem((frows, LANES), F32),
            dma((12,)), dma((2 * ticks,)), dma((ticks,)), dma, dma((last - 1,)), dma, dma((last - 1,)),
            dma((ticks,)), dma((last - 1,)), dma((last - 1,)), dma((7,)), dma((7,)),
            pltpu.SemaphoreType.REGULAR,
        ],
        compiler_params=pltpu.CompilerParams(
            collective_id=0, has_side_effects=True, vmem_limit_bytes=56 << 20
        ),
    )(*args)
    return put_out(outs)


def hand_over_kernel(*refs):
    count = (len(refs) - 2) // 3
    sources, results, held = refs[:count], refs[count : 2 * count], refs[2 * count : 3 * count]
    in_sem, out_sem = refs[3 * count :]
    taken, given = [], []
    for i in range(count):
        for j in range(held[i].shape[0]):
            taken.append(pltpu.make_async_copy(sources[i].at[j], held[i].at[j], in_sem.at[i, j]))
            given.append(pltpu.make_async_copy(held[i].at[j], results[i].at[j], out_sem.at[i, j]))
    for item in taken:
        item.start()
    for item, other in zip(taken, given):
        item.wait()
        other.start()
    for item in given:
        item.wait()


def hand_over(arrays):
    most = max(array.shape[0] for array in arrays)
    any_spec = pl.BlockSpec(memory_space=pl.ANY)
    return pl.pallas_call(
        hand_over_kernel,
        out_shape=tuple(jax.ShapeDtypeStruct(a.shape, a.dtype) for a in arrays),
        in_specs=[any_spec] * len(arrays),
        out_specs=(any_spec,) * len(arrays),
        scratch_shapes=[pltpu.VMEM(a.shape, a.dtype) for a in arrays]
        + [pltpu.SemaphoreType.DMA((len(arrays), most))] * 2,
    )(*arrays)


def on_device(
    fine_inflow, coarse_inflow, fine_entries, fine_pending, coarse_pending,
    fine_kernels, fine_mixing, fine_gains, fine_shifts,
    coarse_kernel, coarse_mixing, coarse_gains, coarse_shifts,
    descent_kernel, upsample_kernel,
):
    nseg = lax.axis_size("segment")
    ndp = lax.axis_size("dp")
    half = nseg // 2
    ticks = fine_entries.shape[0] + 1
    hold_f, hold_c = fine_pending.shape[1], coarse_pending.shape[1]
    recv_f, recv_c = 3 * half - hold_f, half - hold_c
    fside, fch = fine_inflow.shape[3], fine_inflow.shape[4]
    cside, cch = coarse_inflow.shape[3], coarse_inflow.shape[4]
    fcells, ccells = fside * fside, cside * cside
    dims = (nseg, ndp, ticks, fside, cside, hold_f, recv_f, hold_c, recv_c)
    frows, crows = 2 * fch // LANES, 2 * cch // LANES
    any_spec = pl.BlockSpec(memory_space=pl.ANY)
    vmem_spec = pl.BlockSpec(memory_space=pltpu.VMEM)
    dma = pltpu.SemaphoreType.DMA
    args = (
        fine_inflow.reshape(fcells, fch),
        coarse_inflow.reshape(ccells, cch),
        fine_entries.reshape(ticks - 1, fcells, fch),
        fine_pending.reshape(hold_f, fcells, fch),
        coarse_pending.reshape(hold_c, ccells, cch),
        fine_kernels.reshape(2, 9 * fch, fch),
        fine_mixing.reshape(fch, fch),
        fine_gains.reshape(2, fch),
        fine_shifts.reshape(2, fch),
        coarse_kernel.reshape(9 * cch, cch),
        coarse_mixing.reshape(cch, cch),
        coarse_gains.reshape(1, cch),
        coarse_shifts.reshape(1, cch),
        descent_kernel.reshape(4 * fch, cch),
        upsample_kernel,
    )
    paired = nseg == 2 and ndp % 2 == 0 and recv_f == 1 and recv_c == 0
    if paired and ticks > hold_f + recv_f:
        fst, cst, fback, cback = run_pair(dims, fch, cch, args)
    else:
        outs = pl.pallas_call(
            functools.partial(kernel, dims),
            out_shape=(
                jax.ShapeDtypeStruct((ticks, fcells, fch), BF16),
                jax.ShapeDtypeStruct((ticks, ccells, cch), BF16),
                jax.ShapeDtypeStruct((hold_f, fcells, fch), BF16),
                jax.ShapeDtypeStruct((hold_c, ccells, cch), BF16),
            ),
            in_specs=[any_spec] * 7 + [vmem_spec] * 2 + [any_spec] * 2 + [vmem_spec] * 2 + [any_spec] * 2,
            out_specs=(any_spec,) * 4,
            scratch_shapes=[
                pltpu.VMEM((2, 9 * fch, fch), BF16),
                pltpu.VMEM((fch, fch), BF16),
                pltpu.VMEM((9 * cch, cch), BF16),
                pltpu.VMEM((cch, cch), BF16),
                pltpu.VMEM((4 * fch, cch), BF16),
                pltpu.VMEM((cch, 4 * fch), BF16),
                pltpu.VMEM((ticks, fcells, fch), BF16),
                pltpu.VMEM((ticks, ccells, cch), BF16),
                pltpu.VMEM((ticks, ccells, cch), BF16),
                pltpu.VMEM((max(hold_f, recv_f) + ticks, fcells, fch), BF16),
                pltpu.VMEM((max(hold_c, recv_c) + ticks, ccells, cch), BF16),
                pltpu.VMEM((ticks, fcells, fch), BF16),
                pltpu.VMEM((ticks, ccells, cch), BF16),
                pltpu.VMEM((ticks, ccells, cch), BF16),
                pltpu.VMEM((fcells, fch), F32),
                pltpu.VMEM((fcells, fch), F32),
                pltpu.VMEM((fcells, fch), F32),
                pltpu.VMEM((ccells, cch), F32),
                pltpu.VMEM((fch // LANES, cside, 2 * fside, LANES), F32),
                pltpu.VMEM((fcells, 9 * fch), BF16),
                pltpu.VMEM((ccells, 9 * cch), BF16),
                pltpu.VMEM((fcells, fch), BF16),
                pltpu.VMEM((ccells, cch), BF16),
                pltpu.VMEM((2 * ticks, frows, LANES), F32),
                pltpu.VMEM((ticks, crows, LANES), F32),
                pltpu.VMEM((2 * ticks, ndp - 1, frows, LANES), F32),
                pltpu.VMEM((ticks, ndp - 1, crows, LANES), F32),
                pltpu.VMEM((cch, 2, 2, fch), BF16),
                pltpu.VMEM((fch // LANES, 256, LANES), F32),
                dma((12,)),
                dma((4, max(ticks, hold_f, hold_c))),
                dma((ticks,)), dma((ticks,)), dma((ticks,)), dma((ticks,)), dma((ticks,)),
                dma((ticks,)), dma((ticks,)), dma((ticks,)), dma((ticks,)), dma((ticks,)),
                dma((2 * ticks,)), dma((ticks,)), dma((2 * ticks,)), dma((ticks,)),
            ],
            compiler_params=pltpu.CompilerParams(
                collective_id=0, has_side_effects=True, vmem_limit_bytes=56 << 20
            ),
        )(*args)
        fst, cst, fback, cback = hand_over(outs)
    return (
        fst.reshape(1, ticks, 1, fside, fside, fch),
        cst.reshape(1, ticks, 1, cside, cside, cch),
        fback.reshape(1, hold_f, 1, fside, fside, fch),
        cback.reshape(1, hold_c, 1, cside, cside, cch),
    )


def solution(mesh):
    placed = (
        P("segment", "dp", None, None, None),
        P("segment", "dp", None, None, None),
        P(None, "dp", None, None, None),
        P("segment", None, "dp", None, None, None),
        P("segment", None, "dp", None, None, None),
        P("segment", None, None, None, None, None),
        P("segment", None, None),
        P("segment", None, None),
        P("segment", None, None),
        P("segment", None, None, None, None),
        P("segment", None, None),
        P("segment", None),
        P("segment", None),
        P(),
        P(),
    )
    return jax.shard_map(
        on_device,
        mesh=mesh,
        in_specs=placed,
        out_specs=(
            P("segment", None, "dp", None, None, None),
            P("segment", None, "dp", None, None, None),
            P("segment", None, "dp", None, None, None),
            P("segment", None, "dp", None, None, None),
        ),
        check_vma=False,
    )
```

```python
import functools

import jax
import jax.numpy as jnp
from jax import lax
from jax.experimental import pallas as pl
from jax.experimental.pallas import tpu as pltpu
from jax.sharding import PartitionSpec as P

EPSILON = 1e-05
LANES = 128
MESH = pl.DeviceIdType.MESH
F32 = jnp.float32
BF16 = jnp.bfloat16


def dot(a, b):
    return jnp.dot(a, b, preferred_element_type=F32)


def side_shifts(x, side):
    cells = x.shape[0]
    column = lax.rem(lax.broadcasted_iota(jnp.int32, x.shape, 0), side)
    before = jnp.where(column == 0, 0.0, pltpu.roll(x, 1, 0))
    after = jnp.where(column == side - 1, 0.0, pltpu.roll(x, cells - 1, 0))
    return before, x, after


def spread_taps(x, cols, side):
    cells, width = x.shape
    edge = jnp.zeros((side, width), F32)
    for dc, part in enumerate(side_shifts(x, side)):
        above = jnp.concatenate([edge, part[: cells - side]], axis=0)
        below = jnp.concatenate([part[side:], edge], axis=0)
        for dr, moved in enumerate((above, part, below)):
            start = (3 * dr + dc) * width
            cols[:, start : start + width] = moved.astype(BF16)


def put_stats(h, out):
    width = h.shape[1]
    rows = width // LANES
    total = jnp.sum(h, axis=0, keepdims=True)
    square = jnp.sum(h * h, axis=0, keepdims=True)
    for row in range(rows):
        lanes = slice(row * LANES, (row + 1) * LANES)
        out[row : row + 1, :] = total[:, lanes]
        out[rows + row : rows + row + 1, :] = square[:, lanes]


def norm_terms(total, gain, shift, count):
    rows = total.shape[0] // 2
    sums = jnp.concatenate([total[row : row + 1] for row in range(rows)], axis=1)
    squares = jnp.concatenate([total[rows + row : rows + row + 1] for row in range(rows)], axis=1)
    center = sums * (1.0 / count)
    spread = jnp.maximum(squares * (1.0 / count) - center * center, 0.0)
    scale = lax.rsqrt(spread + EPSILON) * gain
    return scale, shift - center * scale


def kernel(
    dims,
    fine_in, coarse_in, entries, fine_pend, coarse_pend,
    wf_hbm, mixf_hbm, fgain, fshift, wc_hbm, mixc_hbm, cgain, cshift, wd_hbm, wu_hbm,
    fst_out, cst_out, fback_out, cback_out,
    wf, mixf, wc, mixc, wd, wu,
    fin, cin, upin, skf, skc, fst, cst, dbuf,
    xs, hf, hg, hc, upscr, colf, colc, zf, zc,
    statf, statc, gotf, gotc,
    wu4, wuf, load_sem, save_sem,
    fin_r, cin_r, up_r, skf_r, skc_r,
    fin_s, cin_s, up_s, skf_s, skc_s,
    gotf_r, gotc_r, statf_s, statc_s,
):
    nseg, ndp, ticks, fside, cside, hold_f, recv_f, hold_c, recv_c = dims
    half = nseg // 2
    seg = lax.axis_index("segment")
    me = lax.axis_index("dp")
    lower = seg < half
    upper = seg >= half
    turn = seg == half - 1
    after = lax.rem(seg + 1, nseg)
    mate = lax.rem(seg + half, nseg)

    def load(k, src, dst):
        return pltpu.make_async_copy(src, dst, load_sem.at[k])

    get_fine = load(0, fine_in, fin.at[0])
    get_wf0 = load(1, wf_hbm.at[0], wf.at[0])
    get_mixf = load(2, mixf_hbm, mixf)
    get_coarse = load(3, coarse_in, cin.at[0])
    get_mixc = load(4, mixc_hbm, mixc)
    get_wc = load(5, wc_hbm, wc)
    get_wf1 = load(6, wf_hbm.at[1], wf.at[1])
    get_wd = load(7, wd_hbm, wd)
    get_wu = load(11, wu_hbm, wu4)
    own_entries = load(8, entries, fin.at[pl.ds(1, ticks - 1)])
    own_fine = hold_f if hold_f > ticks else 0
    own_coarse = hold_c if hold_c > ticks else 0

    def own_pend(k, src, dst, count):
        return load(k, src.at[pl.ds(0, count)], dst.at[pl.ds(0, count)])

    barrier = pltpu.get_barrier_semaphore()
    offsets = sorted({1 % nseg, nseg - 1, half})

    def greet(k, carry):
        pl.semaphore_signal(
            barrier, inc=1, device_id=(seg, lax.rem(me + k, ndp)), device_id_type=MESH
        )
        return carry

    lax.fori_loop(1, ndp, greet, 0)
    for offset in offsets:
        pl.semaphore_signal(
            barrier, inc=1, device_id=(lax.rem(seg + offset, nseg), me), device_id_type=MESH
        )
    @pl.when(upper)
    def _():
        if recv_f:
            own_pend(9, fine_pend, skf, recv_f).start()

    for item in (get_fine, get_wf0, get_mixf, get_coarse, get_mixc, get_wc, get_wf1):
        item.start()

    @pl.when(lower)
    def _():
        if recv_c:
            own_pend(10, coarse_pend, skc, recv_c).start()
        if own_fine:
            own_pend(9, fine_pend, skf, own_fine).start()

    @pl.when(upper)
    def _():
        if own_coarse:
            own_pend(10, coarse_pend, skc, own_coarse).start()

    @pl.when(seg == 0)
    def _():
        own_entries.start()

    @pl.when(turn)
    def _():
        get_wd.start()

    @pl.when(seg == half)
    def _():
        get_wu.start()

    zf[...] = jnp.zeros_like(zf)
    zc[...] = jnp.zeros_like(zc)
    pl.semaphore_wait(barrier, ndp - 1 + len(offsets))

    def push(src, dst, ssem, rsem, to):
        return pltpu.make_async_remote_copy(
            src_ref=src, dst_ref=dst, send_sem=ssem, recv_sem=rsem,
            device_id=(to, me), device_id_type=MESH,
        )

    def send_skf(j):
        return push(skf.at[j], skf.at[recv_f + j], skf_s.at[j], skf_r.at[j], mate)

    def send_pend_f(j):
        return push(fine_pend.at[j], skf.at[recv_f + j], skf_s.at[j], skf_r.at[j], mate)

    def send_pend_c(j):
        return push(coarse_pend.at[j], skc.at[recv_c + j], skc_s.at[j], skc_r.at[j], mate)

    def send_skc(j):
        return push(skc.at[j], skc.at[recv_c + j], skc_s.at[j], skc_r.at[j], mate)

    def send_up(t):
        return push(cst.at[t], upin.at[t], up_s.at[t], up_r.at[t], after)

    def send_co(t):
        return push(cst.at[t], cin.at[t + 1], cin_s.at[t], cin_r.at[t], after)

    def send_down(t):
        return push(dbuf.at[t], cin.at[t + 1], cin_s.at[t], cin_r.at[t], after)

    def send_fo(t):
        return push(fst.at[t], fin.at[t + 1], fin_s.at[t], fin_r.at[t], after)

    def exchange(src, dst, ssem, rsem):
        def one(k, carry):
            pltpu.make_async_remote_copy(
                src_ref=src, dst_ref=dst.at[k - 1], send_sem=ssem, recv_sem=rsem,
                device_id=(seg, lax.rem(me + k, ndp)), device_id_type=MESH,
            ).start()
            return carry

        lax.fori_loop(1, ndp, one, 0)

    def whole(dst, ssem, rsem):
        return pltpu.make_async_remote_copy(
            src_ref=dst, dst_ref=dst, send_sem=ssem, recv_sem=rsem,
            device_id=(seg, lax.rem(me + 1, ndp)), device_id_type=MESH,
        )

    @pl.when(lower)
    def _():
        for j in range(min(hold_f, ticks)):
            send_pend_f(j).start()

    @pl.when(upper)
    def _():
        for j in range(min(hold_c, ticks)):
            send_pend_c(j).start()

    fcount = ndp * fside * fside
    ccount = ndp * cside * cside

    def save_f(t):
        return pltpu.make_async_copy(fst.at[t], fst_out.at[t], save_sem.at[0, t])

    def save_c(t):
        return pltpu.make_async_copy(cst.at[t], cst_out.at[t], save_sem.at[1, t])

    def first(t, *items):
        @pl.when(t == 0)
        def _():
            for item in items:
                item.wait()

    def front(t):
        first(t, get_fine, get_mixf)

        @pl.when(lower)
        def _():
            @pl.when(jnp.logical_and(seg > 0, t > 0))
            def _():
                send_fo(t - 1).wait_recv()

            xs[...] = fin[t].astype(F32)

        @pl.when(upper)
        def _():
            @pl.when(jnp.logical_and(seg == half, t > 0))
            def _():
                send_up(t - 1).wait_recv()
                spread = dot(upin[t - 1], wu[...])
                width = spread.shape[1] // 4
                for a in range(2):
                    for c in range(2):
                        start = (2 * a + c) * width
                        part = spread[:, start : start + width].reshape(cside, cside, width)
                        for i in range(width // LANES):
                            lanes = slice(i * LANES, (i + 1) * LANES)
                            upscr[i, :, pl.ds(a * fside + c, cside, stride=2), :] = part[:, :, lanes]
                for i in range(width // LANES):
                    lanes = slice(i * LANES, (i + 1) * LANES)
                    fin[t, :, lanes] = upscr[i].reshape(fside * fside, LANES).astype(BF16)

            @pl.when(jnp.logical_and(seg != half, t > 0))
            def _():
                send_fo(t - 1).wait_recv()

            if recv_f:
                first(t, own_pend(9, fine_pend, skf, recv_f))

            @pl.when(t >= recv_f)
            def _():
                send_skf(t - recv_f).wait_recv()

            xs[...] = (dot(fin[t], mixf[...]) + skf[t].astype(F32)).astype(BF16).astype(F32)

        spread_taps(xs[...], colf, fside)
        first(t, get_wf0)
        hf[...] = dot(colf[...], wf[0])
        put_stats(hf[...], statf.at[2 * t])
        exchange(statf.at[2 * t], gotf.at[2 * t], statf_s.at[2 * t], gotf_r.at[2 * t])

    def later(which, t):
        @pl.when(jnp.logical_and(which, t < ticks - 1))
        def _():
            front(t + 1)

    def own_pieces(t):
        @pl.when(t == 0)
        def _():
            get_wf1.wait()

            @pl.when(turn)
            def _():
                get_wd.wait()

            @pl.when(seg == 0)
            def _():
                own_entries.wait()

            @pl.when(seg == half)
            def _():
                get_wu.wait()
                width = wu4.shape[3]
                depth = wuf.shape[1] // 4

                def rows_of(n, carry):
                    rows = pl.multiple_of(n * depth, depth)
                    piece = wu4[pl.ds(rows, depth)].astype(F32).reshape(4 * depth, width)
                    for i in range(width // LANES):
                        wuf[i] = piece[:, i * LANES : (i + 1) * LANES]
                    for q in range(4):
                        for i in range(width // LANES):
                            start = q * width + i * LANES
                            part = wuf[i, pl.ds(q, depth, stride=4), :]
                            wu[pl.ds(rows, depth), start : start + LANES] = part.astype(BF16)
                    return carry

                lax.fori_loop(0, wu4.shape[0] // depth, rows_of, 0)

    front(jnp.int32(0))
    own_pieces(jnp.int32(0))

    def tick(t, carry):
        first(t, get_coarse, get_mixc)

        @pl.when(t > 0)
        def _():
            send_co(t - 1).wait_recv()

        @pl.when(lower)
        def _():
            if recv_c:
                first(t, own_pend(10, coarse_pend, skc, recv_c))

            @pl.when(t >= recv_c)
            def _():
                send_skc(t - recv_c).wait_recv()

            hc[...] = (dot(cin[t], mixc[...]) + skc[t].astype(F32)).astype(BF16).astype(F32)

        @pl.when(upper)
        def _():
            hc[...] = cin[t].astype(F32)

        spread_taps(hc[...], colc, cside)
        first(t, get_wc)
        hc[...] = dot(colc[...], wc[...])
        put_stats(hc[...], statc.at[t])
        exchange(statc.at[t], gotc.at[t], statc_s.at[t], gotc_r.at[t])

        whole(gotf.at[2 * t], statf_s.at[2 * t], gotf_r.at[2 * t]).wait_recv()
        total = statf[2 * t] + jnp.sum(gotf[2 * t], axis=0)
        scale, offset = norm_terms(total, fgain[0:1, :], fshift[0:1, :], fcount)
        xs[...] = jnp.maximum(hf[...] * scale + offset, 0.0).astype(BF16).astype(F32)
        spread_taps(xs[...], colf, fside)
        hg[...] = dot(colf[...], wf[1])
        put_stats(hg[...], statf.at[2 * t + 1])
        exchange(
            statf.at[2 * t + 1], gotf.at[2 * t + 1], statf_s.at[2 * t + 1], gotf_r.at[2 * t + 1]
        )

        whole(gotc.at[t], statc_s.at[t], gotc_r.at[t]).wait_recv()
        total = statc[t] + jnp.sum(gotc[t], axis=0)
        scale, offset = norm_terms(total, cgain[...], cshift[...], ccount)
        cst[t] = jnp.maximum(hc[...] * scale + offset, 0.0).astype(BF16)

        @pl.when(t < ticks - 1)
        def _():
            @pl.when(turn)
            def _():
                send_up(t).start()

            @pl.when(jnp.logical_not(turn))
            def _():
                send_co(t).start()

        save_c(t).start()

        @pl.when(upper)
        def _():
            skc[hold_c + t] = dot(cst[t], mixc[...]).astype(BF16)

            @pl.when(hold_c + t < ticks)
            def _():
                send_skc(hold_c + t).start()

        later(seg == 0, t)

        whole(gotf.at[2 * t + 1], statf_s.at[2 * t + 1], gotf_r.at[2 * t + 1]).wait_recv()
        total = statf[2 * t + 1] + jnp.sum(gotf[2 * t + 1], axis=0)
        scale, offset = norm_terms(total, fgain[1:2, :], fshift[1:2, :], fcount)
        fst[t] = jnp.maximum(hg[...] * scale + offset, 0.0).astype(BF16)

        @pl.when(t < ticks - 1)
        def _():
            @pl.when(turn)
            def _():
                width = fst.shape[2]
                for i in range(width // LANES):
                    lanes = slice(i * LANES, (i + 1) * LANES)
                    upscr[i] = fst[t, :, lanes].astype(F32).reshape(cside, 2 * fside, LANES)
                lowered = None
                for a in range(2):
                    for c in range(2):
                        for i in range(width // LANES):
                            part = upscr[i, :, pl.ds(a * fside + c, cside, stride=2), :]
                            part = part.reshape(cside * cside, LANES).astype(BF16)
                            start = (2 * a + c) * width + i * LANES
                            term = dot(part, wd[start : start + LANES, :])
                            lowered = term if lowered is None else lowered + term
                dbuf[t] = lowered.astype(BF16)
                send_down(t).start()

            @pl.when(jnp.logical_and(jnp.logical_not(turn), seg < nseg - 1))
            def _():
                send_fo(t).start()

        save_f(t).start()

        @pl.when(lower)
        def _():
            skf[hold_f + t] = dot(fst[t], mixf[...]).astype(BF16)

            @pl.when(hold_f + t < ticks)
            def _():
                send_skf(hold_f + t).start()

        later(seg > 0, t)
        return carry

    lax.fori_loop(0, ticks, tick, 0)

    def back_f(first, src):
        return pltpu.make_async_copy(src, fback_out.at[first], save_sem.at[2, first])

    def back_c(first, src):
        return pltpu.make_async_copy(src, cback_out.at[first], save_sem.at[3, first])

    lower_backs = [back_f(j, skf.at[ticks + j]) for j in range(hold_f)]
    lower_backs += [
        back_c(j, skc.at[ticks + j] if j < recv_c else zc) for j in range(hold_c)
    ]
    upper_backs = [
        back_f(j, skf.at[ticks + j] if j < recv_f else zf) for j in range(hold_f)
    ]
    upper_backs += [back_c(j, skc.at[ticks + j]) for j in range(hold_c)]

    @pl.when(lower)
    def _():
        if own_fine:
            own_pend(9, fine_pend, skf, own_fine).wait()
        for j in range(max(ticks - recv_c, 0), ticks):
            send_skc(j).wait_recv()
        for item in lower_backs:
            item.start()
        for j in range(ticks):
            send_skf(j).wait_send()
        for item in lower_backs:
            item.wait()

    @pl.when(upper)
    def _():
        if own_coarse:
            own_pend(10, coarse_pend, skc, own_coarse).wait()
        for j in range(max(ticks - recv_f, 0), ticks):
            send_skf(j).wait_recv()
        for item in upper_backs:
            item.start()
        for j in range(ticks):
            send_skc(j).wait_send()
        for item in upper_backs:
            item.wait()

    @pl.when(turn)
    def _():
        for t in range(ticks - 1):
            send_up(t).wait_send()

    @pl.when(jnp.logical_and(jnp.logical_not(turn), seg < nseg - 1))
    def _():
        for t in range(ticks - 1):
            send_fo(t).wait_send()

    for t in range(ticks - 1):
        send_co(t).wait_send()
    for t in range(ticks):
        whole(gotf.at[2 * t], statf_s.at[2 * t], gotf_r.at[2 * t]).wait_send()
        whole(gotf.at[2 * t + 1], statf_s.at[2 * t + 1], gotf_r.at[2 * t + 1]).wait_send()
        whole(gotc.at[t], statc_s.at[t], gotc_r.at[t]).wait_send()
        save_f(t).wait()
        save_c(t).wait()


def sums_of(total):
    rows = total.shape[0] // 2
    sums = jnp.concatenate([total[row : row + 1] for row in range(rows)], axis=1)
    squares = jnp.concatenate([total[rows + row : rows + row + 1] for row in range(rows)], axis=1)
    return sums, squares


def moments(total, count):
    sums, squares = sums_of(total)
    center = sums * (1.0 / count)
    spread = jnp.maximum(squares * (1.0 / count) - center * center, 0.0)
    return center, lax.rsqrt(spread + EPSILON)


def pair_kernel(
    dims,
    fine_in, coarse_in, entries, fine_pend, coarse_pend,
    wf_hbm, mixf_hbm, fgain_hbm, fshift_hbm, wc_hbm, mixc_hbm, cgain_hbm, cshift_hbm,
    wd_hbm, wu_hbm,
    fst, cst, fback, cback,
    wf, mixf, mixe, wc, mixc, mixm, wd, wu, wu4, wuf,
    fin, cin, skf, skc, dbuf, dbuf_in, co_in, ec_out, ec_in, fnorm, cnorm, mate_fnorm, mate_cnorm,
    hf, hc, xs, hx, upscr, colf, colc, cold,
    rawf_out, rawf_in, rawc_out, rawc_in,
    stf, stc, gotf, gotc, farf, farc,
    fsum_out, fsum_in,
    load_sem, rf, rc, rfarf, rfarc, rrawf, rrawc, skf_r, dbuf_r, co_r, one_s, one_r, ready,
):
    nseg, ndp, ticks, fside, cside, hold_f, recv_f, hold_c, recv_c = dims
    seg = lax.axis_index("segment")
    me = lax.axis_index("dp")
    other = 1 - seg
    lower = seg == 0
    upper = seg == 1
    fcells, ccells = fside * fside, cside * cside
    fcount, ccount = ndp * fcells, ndp * ccells
    last = ticks - 1
    fgain, fshift, cgain, cshift = fnorm.at[0], fnorm.at[1], cnorm.at[0], cnorm.at[1]
    sf, skf_s, co_s, sc, sfarf = (load_sem.at[k] for k in range(5))
    sfarc, srawf, srawc, dbuf_s = (load_sem.at[k] for k in range(5, 9))
    fnorm_s, cnorm_s, hand_s = (load_sem.at[k] for k in range(9, 12))

    barrier = pltpu.get_barrier_semaphore()

    bits = ndp.bit_length() - 1

    def partner(k):
        if 1 << bits != ndp:
            return lax.rem(me + k, ndp)
        to = 0
        for b in range(bits):
            bit = lax.rem(lax.div(me, 1 << b), 2)
            to = to + (1 << b) * (1 - bit if (k >> b) & 1 else bit)
        return to

    partners = [partner(k) for k in range(ndp)]
    twin = me + 1 - 2 * lax.rem(me, 2)
    for k in range(ndp - 1, 0, -1):
        pl.semaphore_signal(barrier, inc=1, device_id=(seg, partners[k]), device_id_type=MESH)
    pl.semaphore_signal(barrier, inc=1, device_id=(other, me), device_id_type=MESH)

    def load(k, src, dst):
        return pltpu.make_async_copy(src, dst, load_sem.at[k])

    get_fine = load(0, fine_in, fin.at[0])
    get_wf0 = load(1, wf_hbm.at[0], wf.at[0])
    get_mixf = load(2, mixf_hbm, mixf)
    get_coarse = load(3, coarse_in, cin)
    get_wc = load(4, wc_hbm, wc)
    get_wf1 = load(5, wf_hbm.at[1], wf.at[1])
    get_wd = load(6, wd_hbm, wd)
    get_entries = load(7, entries, fin.at[pl.ds(1, last)])
    get_pend = load(7, fine_pend.at[pl.ds(0, recv_f)], skf.at[pl.ds(0, recv_f)])
    get_norms = [
        load(8, fgain_hbm, fgain), load(8, fshift_hbm, fshift),
        load(9, cgain_hbm, cgain), load(9, cshift_hbm, cshift),
    ]
    have_norms = [load(8, fnorm, fnorm), load(9, cnorm, cnorm)]
    get_mixc = load(10, mixc_hbm, mixc)
    get_wu = load(11, wu_hbm, wu4)

    get_fine.start()

    @pl.when(upper)
    def _():
        get_mixf.start()
        get_pend.start()

    get_wf0.start()

    @pl.when(lower)
    def _():
        for item in (
            get_entries, get_wf1, get_mixf, get_coarse, get_mixc, get_wc, get_wd, *get_norms
        ):
            item.start()

    @pl.when(upper)
    def _():
        get_coarse.start()
        get_wc.start()

    def push(src, dst, ssem, rsem):
        return pltpu.make_async_remote_copy(
            src_ref=src, dst_ref=dst, send_sem=ssem, recv_sem=rsem,
            device_id=(other, me), device_id_type=MESH,
        )

    def share(src, dst, ssem, rsem):
        for k in range(ndp - 1, 0, -1):
            pltpu.make_async_remote_copy(
                src_ref=src, dst_ref=dst.at[k - 1], send_sem=ssem, recv_sem=rsem,
                device_id=(seg, partners[k]), device_id_type=MESH,
            ).start()

    def cast_far(src, dst, ssem, rsem, step=1):
        for k in range(ndp - step, -1, -step):
            pltpu.make_async_remote_copy(
                src_ref=src, dst_ref=dst.at[k // step], send_sem=ssem, recv_sem=rsem,
                device_id=(other, partners[k]), device_id_type=MESH,
            ).start()

    def of_f(n):
        return push(gotf.at[n], gotf.at[n], sf, rf.at[n])

    def of_c(t):
        return push(gotc.at[t], gotc.at[t], sc, rc.at[t])

    of_farf = push(farf, farf, sfarf, rfarf)
    send_rawf = push(rawf_out, rawf_in, srawf, rrawf)

    def of_farc(t):
        return push(farc.at[t - 1], farc.at[t - 1], sfarc, rfarc.at[t - 1])

    def send_rawc(t):
        return push(rawc_out.at[t - 1], rawc_in.at[t - 1], srawc, rrawc.at[t - 1])

    def send_down(t):
        return push(dbuf.at[t - 1], dbuf_in.at[t - 1], dbuf_s, dbuf_r.at[t - 1])

    def send_co(t):
        return push(cst.at[t], co_in.at[t], co_s, co_r.at[t])

    def send_skf(j):
        return push(skf.at[j], skf.at[recv_f + j], skf_s, skf_r.at[j])

    def send_pend_f(j):
        return push(fine_pend.at[j], skf.at[recv_f + j], skf_s, skf_r.at[j])

    send_pend_c = push(coarse_pend.at[0], skc, skf_s, one_r.at[0])

    def rows_of(matrix, device):
        part = matrix.shape[0] // 2
        return pl.ds(pl.multiple_of(lax.rem(device, 2) * part, part), part)

    def send_half(src, dst):
        rows = rows_of(dst, me)
        return push(src.at[rows], dst.at[rows], one_s, one_r.at[1])

    def hand_half(matrix, device):
        rows = rows_of(matrix, device)
        return pltpu.make_async_remote_copy(
            src_ref=matrix.at[rows], dst_ref=matrix.at[rows],
            send_sem=hand_s, recv_sem=one_r.at[4],
            device_id=(seg, twin), device_id_type=MESH,
        )

    def send_mixc(piece):
        part = mixm.shape[0] // 8
        start = (4 * lax.rem(me, 2) + 3 * piece) * part
        rows = pl.ds(pl.multiple_of(start, part), (1 if piece else 3) * part)
        return push(mixc_hbm.at[rows], mixm.at[rows], one_s, one_r.at[1])

    all_mixc = send_half(mixc_hbm, mixm)
    send_mixf = send_half(mixf_hbm, mixe)
    send_norms = [
        push(fnorm, mate_fnorm, fnorm_s, one_r.at[2]),
        push(cnorm, mate_cnorm, cnorm_s, one_r.at[3]),
    ]
    send_ec = push(ec_out, ec_in, sfarf, one_r.at[5])
    share_sum = pltpu.make_async_remote_copy(
        src_ref=fsum_out, dst_ref=fsum_in, send_sem=srawf, recv_sem=one_r.at[0],
        device_id=(seg, twin), device_id_type=MESH,
    )

    def conv_fine(layer, out):
        spread_taps(xs[...], colf, fside)
        out[...] = dot(colf[...], wf[layer])

    def centred(h, stats, cells):
        sums, _ = sums_of(stats)
        return (h - sums * (1.0 / cells)).astype(BF16)

    def arrived(raw, got, mine, gain, shift, count, cells):
        center, inverse = moments(got, count)
        own, _ = sums_of(mine)
        scale = inverse * gain
        offset = shift + (own * (1.0 / cells) - center) * scale
        return jnp.maximum(raw[...].astype(F32) * scale + offset, 0.0).astype(BF16)

    def descended(x):
        width = x.shape[1]
        for i in range(width // LANES):
            lanes = slice(i * LANES, (i + 1) * LANES)
            upscr[i] = x[:, lanes].reshape(cside, 2 * fside, LANES)
        for a in range(2):
            for c in range(2):
                for i in range(width // LANES):
                    piece = upscr[i, :, pl.ds(a * fside + c, cside, stride=2), :]
                    start = (2 * a + c) * width + i * LANES
                    cold[:, start : start + LANES] = piece.reshape(ccells, LANES).astype(BF16)
        return dot(cold[...], wd[...]).astype(BF16)

    def normed(h, stats, got, gain, shift, count):
        center, inverse = moments(stats[...] + jnp.sum(got[...], axis=0), count)
        scale = inverse * gain
        return jnp.maximum(h[...] * scale + (shift - center * scale), 0.0).astype(BF16)

    def share_fine(n):
        share(stf.at[n], gotf.at[n], sf, rf.at[n])

    def conv_stats(layer, n):
        conv_fine(layer, hf.at[n])
        put_stats(hf[n], stf.at[n])

    def take_first(t):
        xs[...] = normed(
            hf.at[t], stf.at[t], gotf.at[t], fgain[0:1, :], fshift[0:1, :], fcount
        ).astype(F32)

    def finish_fine(t):
        n = ticks + t
        of_f(n).wait_recv()
        fst[t] = normed(hf.at[n], stf.at[n], gotf.at[n], fgain[1:2, :], fshift[1:2, :], fcount)

    def finish_coarse(t):
        of_c(t).wait_recv()
        cst[t] = normed(hc.at[t], stc.at[t], gotc.at[t], cgain[...], cshift[...], ccount)

    def coarse(t, raw):
        spread_taps(hx[...], colc, cside)
        hc[t] = dot(colc[...], wc[...])
        put_stats(hc[t], stc.at[t])

        @pl.when(raw)
        def _():
            cast_far(stc.at[t], farc.at[t - 1], sfarc, rfarc.at[t - 1])
            rawc_out[t - 1] = centred(hc[t], stc[t], ccells)
            send_rawc(t).start()

        share(stc.at[t], gotc.at[t], sc, rc.at[t])

    def mate_coarse(t):
        of_farc(t).wait_recv()
        send_rawc(t).wait_recv()
        return arrived(
            rawc_in.at[t - 1], jnp.sum(farc[t - 1], axis=0), farc[t - 1, 0], mate_cnorm[0],
            mate_cnorm[1], ccount, ccells,
        )

    def sent():
        for item in send_norms:
            item.wait_send()
        push(gotc, gotc, sc, rc.at[0]).wait_send()

    get_fine.wait()

    @pl.when(lower)
    def _():
        xs[...] = fin[0].astype(F32)

    @pl.when(upper)
    def _():
        get_mixf.wait()
        get_pend.wait()
        xs[...] = (dot(fin[0], mixf[...]) + skf[0].astype(F32)).astype(BF16).astype(F32)

    get_wf0.wait()
    conv_stats(0, 0)
    pl.semaphore_wait(barrier, ndp)
    share_fine(0)
    pl.semaphore_signal(ready, inc=1, device_id=(other, me), device_id_type=MESH)

    @pl.when(lower)
    def _():
        send_pend_f(0).start()
        send_mixf.start()
        get_entries.wait()

        def early(t, carry):
            xs[...] = fin[t].astype(F32)
            conv_stats(0, t)
            return carry

        lax.fori_loop(1, ticks, early, 0)
        rest = pl.ds(1, last)
        for k in range(ndp - 1, 0, -1):
            pltpu.make_async_remote_copy(
                src_ref=stf.at[rest], dst_ref=gotf.at[rest, k - 1], send_sem=sf, recv_sem=rf.at[1],
                device_id=(seg, partners[k]), device_id_type=MESH,
            ).start()
        for item in (get_wf1, get_mixf, get_coarse, get_mixc, get_wc, get_wd, *have_norms):
            item.wait()
        for item in send_norms:
            item.start()
        pl.semaphore_wait(ready, 1)

        def term(n, carry):
            t = jnp.where(n < last - 1, n + 1, jnp.where(n == last, last, 0))
            finish_fine(t)

            @pl.when(jnp.logical_and(t > 0, t < last))
            def _():
                dbuf[t - 1] = descended(fst[t].astype(F32))
                send_down(t).start()

            @pl.when(t > 0)
            def _():
                fresh = dot(fst[t], mixf[...]).astype(BF16)

                @pl.when(hold_f + t < ticks)
                def _():
                    skf[hold_f + t] = fresh

                @pl.when(hold_f + t >= ticks)
                def _():
                    fback[hold_f + t - ticks] = fresh

            return carry

        def encode(i, carry):
            t = jnp.maximum(i - last + 1, 0)

            @pl.when(i < ticks)
            def _():
                @pl.when(i == 0)
                def _():
                    of_f(0).wait_recv()

                @pl.when(i == 1)
                def _():
                    push(gotf.at[rest], gotf.at[rest], sf, rf.at[1]).wait_recv()

                take_first(i)
                conv_stats(1, ticks + i)

                @pl.when(i == 0)
                def _():
                    cast_far(stf.at[ticks], farf, sfarf, rfarf, 2)
                    rawf_out[...] = centred(hf[ticks], stf[ticks], fcells)
                    send_rawf.start()

                share_fine(ticks + i)

                @pl.when(i == 1)
                def _():
                    for j in range(1, hold_f):
                        send_pend_f(j).start()

            @pl.when(i == 0)
            def _():
                send_pend_c.wait_recv()
                hx[...] = (dot(cin[...], mixc[...]) + skc[...].astype(F32)).astype(BF16).astype(F32)

            @pl.when(i == last)
            def _():
                finish_coarse(0)
                send_co(0).start()
                for item in send_norms:
                    item.wait_recv()
                send_co(0).wait_recv()
                send_ec.wait_recv()
                hx[...] = (dot(co_in[0], mixc[...]) + ec_in[...].astype(F32)).astype(BF16).astype(F32)

            @pl.when(i > last)
            def _():
                @pl.when(i == last + 1)
                def _():
                    hand_half(mixm, twin).wait_recv()
                    hand_half(mixm, me).wait_send()
                    mixm[...] = (mixm[...].astype(F32) + mixc[...].astype(F32)).astype(BF16)

                finish_coarse(t - 1)

                @pl.when(t < last)
                def _():
                    send_co(t - 1).start()

                hx[...] = dot(mate_coarse(t - 1), mixm[...]).astype(BF16).astype(F32)

            @pl.when(jnp.logical_or(i == 0, i >= last))
            def _():
                coarse(t, t == last - 1)

            @pl.when(i == last)
            def _():
                lax.fori_loop(0, ticks - 1, term, 0)
                all_mixc.wait_recv()
                hand_half(mixm, me).start()
                term(last, 0)

            @pl.when(t == last)
            def _():
                for j in range(hold_f + 1, ticks):
                    send_skf(j).start()

            return carry

        lax.fori_loop(0, 2 * ticks - 2, encode, 0)
        cback[...] = jnp.zeros_like(cback)
        of_farf.wait_send()
        send_rawf.wait_send()
        of_farc(last - 1).wait_send()
        send_rawc(last - 1).wait_send()
        push(co_in, co_in, co_s, co_r.at[0]).wait_send()
        push(dbuf, dbuf_in, dbuf_s, dbuf_r.at[0]).wait_send()
        terms = skf.at[pl.ds(0, ticks - 1)]
        push(terms, terms, skf_s, skf_r.at[0]).wait_send()
        send_mixf.wait_send()
        sent()
        finish_coarse(last)

    @pl.when(upper)
    def _():
        send_pend_c.start()
        send_mixc(0).start()
        get_coarse.wait()
        get_wc.wait()
        later = (get_wf1, get_wd, get_wu, get_mixc)
        for item in (*later, *get_norms):
            item.start()

        def spread_weights():
            width = wu4.shape[3]
            depth = wuf.shape[1] // 4

            def rows_of(n, carry):
                rows = pl.multiple_of(n * depth, depth)
                piece = wu4[pl.ds(rows, depth)].astype(F32).reshape(4 * depth, width)
                for i in range(width // LANES):
                    wuf[i] = piece[:, i * LANES : (i + 1) * LANES]
                for q in range(4):
                    for i in range(width // LANES):
                        start = q * width + i * LANES
                        part = wuf[i, pl.ds(q, depth, stride=4), :]
                        wu[pl.ds(rows, depth), start : start + LANES] = part.astype(BF16)
                return carry

            lax.fori_loop(0, wu4.shape[0] // depth, rows_of, 0)

        def encode(t, carry):
            @pl.when(t == 0)
            def _():
                hx[...] = cin[...].astype(F32)

            @pl.when(t == 1)
            def _():
                for item in send_norms:
                    item.wait_recv()
                pl.semaphore_wait(ready, 1)
                of_farf.wait_recv()
                fsum_out[...] = jnp.sum(farf[...], axis=0)
                share_sum.start()
                send_rawf.wait_recv()
                share_sum.wait_recv()
                send_mixc(1).start()
                taken = arrived(
                    rawf_in, fsum_out[...] + fsum_in[...], farf[0], mate_fnorm[0, 1:2, :],
                    mate_fnorm[1, 1:2, :], fcount, fcells,
                )
                fin[0] = taken
                hx[...] = descended(taken.astype(F32)).astype(F32)

            @pl.when(t > 1)
            def _():
                send_down(t - 1).wait_recv()
                hx[...] = dbuf_in[t - 2].astype(F32)

            coarse(t, jnp.logical_and(t > 0, t < last))
            return carry

        def raised(taken, t):
            spread = dot(taken, wu[...])
            width = spread.shape[1] // 4
            for a in range(2):
                for c in range(2):
                    start = (2 * a + c) * width
                    part = spread[:, start : start + width].reshape(cside, cside, width)
                    for i in range(width // LANES):
                        lanes = slice(i * LANES, (i + 1) * LANES)
                        upscr[i, :, pl.ds(a * fside + c, cside, stride=2), :] = part[:, :, lanes]
            for i in range(width // LANES):
                lanes = slice(i * LANES, (i + 1) * LANES)
                part = upscr[i].reshape(fcells, LANES) + skf[t, :, lanes].astype(F32)
                xs[:, lanes] = part.astype(BF16).astype(F32)

        def step(o, carry):
            coarse_end = jnp.where(o < 2, o + 1, jnp.where(o == 2, ticks, o))
            lax.fori_loop(o, coarse_end, encode, 0)
            half_o = lax.div(o, 2)
            odd = lax.rem(o, 2) == 1
            is_first = jnp.logical_or(
                o == 1, jnp.logical_and(jnp.logical_and(o > 1, o < 2 * last), jnp.logical_not(odd))
            )
            t = jnp.where(
                o == 0, 0, jnp.where(is_first, jnp.where(o == 1, 1, half_o + 1),
                                     jnp.where(o == 2 * last, last, half_o))
            )

            @pl.when(o == 0)
            def _():
                for item in (*later, *have_norms):
                    item.wait()
                for item in send_norms:
                    item.start()
                spread_weights()
                width = mixf.shape[0]
                for q in range(4):
                    lanes = slice(q * width, (q + 1) * width)
                    wu[:, lanes] = dot(wu[:, lanes], mixf[...]).astype(BF16)

            @pl.when(o == 1)
            def _():
                finish_fine(0)
                hand_half(mixe, twin).wait_recv()
                skf[recv_f + hold_f] = dot(fin[0], mixe[...]).astype(BF16)

            @pl.when(o == 2)
            def _():
                finish_coarse(1)

            @pl.when(is_first)
            def _():
                @pl.when(t - recv_f != hold_f)
                def _():
                    send_skf(t - recv_f).wait_recv()

                @pl.when(t < last)
                def _():
                    send_co(t - 1).wait_recv()
                    raised(co_in[t - 1], t)

                @pl.when(t == last)
                def _():
                    raised(mate_coarse(t - 1), t)

            @pl.when(jnp.logical_not(is_first))
            def _():
                of_f(t).wait_recv()
                take_first(t)

            layer = jnp.where(is_first, 0, 1)
            n = layer * ticks + t
            conv_stats(layer, n)
            share_fine(n)

            @pl.when(o == 0)
            def _():
                finish_coarse(0)
                send_co(0).start()
                ec_out[...] = dot(cst[0], mixc[...]).astype(BF16)
                send_ec.start()
                send_mixf.wait_recv()
                hand_half(mixe, me).start()

            @pl.when(o == 2 * last - 2)
            def _():
                def rest(n, c):
                    finish_coarse(n)
                    return c

                lax.fori_loop(2, ticks, rest, 0)
                cback[0] = dot(cst[last], mixc[...]).astype(BF16)

            return carry

        lax.fori_loop(0, 2 * ticks - 1, step, 0)

        def rest_fine(n, c):
            finish_fine(n)
            return c

        lax.fori_loop(1, last - 1, rest_fine, 0)
        for j in range(max(ticks - recv_f, 0), ticks):
            send_skf(j).wait_recv()
        for j in range(hold_f):
            fback[j] = skf[ticks + j] if j < recv_f else jnp.zeros_like(skf[0])
        finish_fine(last - 1)
        send_pend_c.wait_send()
        all_mixc.wait_send()
        send_ec.wait_send()
        share_sum.wait_send()
        hand_half(mixe, me).wait_send()
        send_co(0).wait_send()
        push(farc, farc, sfarc, rfarc.at[0]).wait_send()
        push(rawc_in, rawc_in, srawc, rrawc.at[0]).wait_send()
        sent()
        finish_fine(last)

    push(gotf, gotf, sf, rf.at[0]).wait_send()


def put_out_kernel(*refs):
    count = (len(refs) - 1) // 2
    sources, results, sem = refs[:count], refs[count : 2 * count], refs[2 * count]
    given = [
        pltpu.make_async_copy(source, result, sem.at[i])
        for i, (source, result) in enumerate(zip(sources, results))
    ]
    for item in given:
        item.start()
    for item in given:
        item.wait()


def put_out(arrays):
    any_spec = pl.BlockSpec(memory_space=pl.ANY)
    vmem_spec = pl.BlockSpec(memory_space=pltpu.VMEM)
    held = [pltpu.with_memory_space_constraint(a, pltpu.VMEM) for a in arrays]
    return pl.pallas_call(
        put_out_kernel,
        out_shape=tuple(jax.ShapeDtypeStruct(a.shape, a.dtype) for a in arrays),
        in_specs=[vmem_spec] * len(arrays),
        out_specs=(any_spec,) * len(arrays),
        scratch_shapes=[pltpu.SemaphoreType.DMA((len(arrays),))],
    )(*held)


def run_pair(dims, fch, cch, args):
    nseg, ndp, ticks, fside, cside, hold_f, recv_f, hold_c, recv_c = dims
    fcells, ccells = fside * fside, cside * cside
    frows, crows = 2 * fch // LANES, 2 * cch // LANES
    last = ticks - 1
    any_spec = pl.BlockSpec(memory_space=pl.ANY)
    vmem_spec = pl.BlockSpec(memory_space=pltpu.VMEM)
    dma, vmem = pltpu.SemaphoreType.DMA, pltpu.VMEM
    outs = pl.pallas_call(
        functools.partial(pair_kernel, dims),
        out_shape=(
            vmem((ticks, fcells, fch), BF16),
            vmem((ticks, ccells, cch), BF16),
            vmem((hold_f, fcells, fch), BF16),
            vmem((hold_c, ccells, cch), BF16),
        ),
        in_specs=[any_spec] * 15,
        out_specs=(vmem_spec,) * 4,
        scratch_shapes=[
            vmem((2, 9 * fch, fch), BF16),
            vmem((fch, fch), BF16),
            vmem((fch, fch), BF16),
            vmem((9 * cch, cch), BF16),
            vmem((cch, cch), BF16),
            vmem((cch, cch), BF16),
            vmem((4 * fch, cch), BF16),
            vmem((cch, 4 * fch), BF16),
            vmem((cch, 2, 2, fch), BF16),
            vmem((fch // LANES, 256, LANES), F32),
            vmem((ticks, fcells, fch), BF16),
            vmem((ccells, cch), BF16),
            vmem((max(hold_f, recv_f) + ticks, fcells, fch), BF16),
            vmem((ccells, cch), BF16),
            vmem((last - 1, ccells, cch), BF16),
            vmem((last - 1, ccells, cch), BF16),
            vmem((last - 1, ccells, cch), BF16),
            vmem((ccells, cch), BF16),
            vmem((ccells, cch), BF16),
            vmem((2, 2, fch), F32),
            vmem((2, 1, cch), F32),
            vmem((2, 2, fch), F32),
            vmem((2, 1, cch), F32),
            vmem((2 * ticks, fcells, fch), F32),
            vmem((ticks, ccells, cch), F32),
            vmem((fcells, fch), F32),
            vmem((ccells, cch), F32),
            vmem((fch // LANES, cside, 2 * fside, LANES), F32),
            vmem((fcells, 9 * fch), BF16),
            vmem((ccells, 9 * cch), BF16),
            vmem((ccells, 4 * fch), BF16),
            vmem((fcells, fch), BF16),
            vmem((fcells, fch), BF16),
            vmem((last - 1, ccells, cch), BF16),
            vmem((last - 1, ccells, cch), BF16),
            vmem((2 * ticks, frows, LANES), F32),
            vmem((ticks, crows, LANES), F32),
            vmem((2 * ticks, ndp - 1, frows, LANES), F32),
            vmem((ticks, ndp - 1, crows, LANES), F32),
            vmem((ndp // 2, frows, LANES), F32),
            vmem((last - 1, ndp, crows, LANES), F32),
            vmem((frows, LANES), F32),
            vmem((frows, LANES), F32),
            dma((12,)), dma((2 * ticks,)), dma((ticks,)), dma, dma((last - 1,)), dma, dma((last - 1,)),
            dma((ticks,)), dma((last - 1,)), dma((last - 1,)), dma, dma((6,)),
            pltpu.SemaphoreType.REGULAR,
        ],
        compiler_params=pltpu.CompilerParams(
            collective_id=0, has_side_effects=True, vmem_limit_bytes=56 << 20
        ),
    )(*args)
    return put_out(outs)


def hand_over_kernel(*refs):
    count = (len(refs) - 2) // 3
    sources, results, held = refs[:count], refs[count : 2 * count], refs[2 * count : 3 * count]
    in_sem, out_sem = refs[3 * count :]
    taken, given = [], []
    for i in range(count):
        for j in range(held[i].shape[0]):
            taken.append(pltpu.make_async_copy(sources[i].at[j], held[i].at[j], in_sem.at[i, j]))
            given.append(pltpu.make_async_copy(held[i].at[j], results[i].at[j], out_sem.at[i, j]))
    for item in taken:
        item.start()
    for item, other in zip(taken, given):
        item.wait()
        other.start()
    for item in given:
        item.wait()


def hand_over(arrays):
    most = max(array.shape[0] for array in arrays)
    any_spec = pl.BlockSpec(memory_space=pl.ANY)
    return pl.pallas_call(
        hand_over_kernel,
        out_shape=tuple(jax.ShapeDtypeStruct(a.shape, a.dtype) for a in arrays),
        in_specs=[any_spec] * len(arrays),
        out_specs=(any_spec,) * len(arrays),
        scratch_shapes=[pltpu.VMEM(a.shape, a.dtype) for a in arrays]
        + [pltpu.SemaphoreType.DMA((len(arrays), most))] * 2,
    )(*arrays)


def on_device(
    fine_inflow, coarse_inflow, fine_entries, fine_pending, coarse_pending,
    fine_kernels, fine_mixing, fine_gains, fine_shifts,
    coarse_kernel, coarse_mixing, coarse_gains, coarse_shifts,
    descent_kernel, upsample_kernel,
):
    nseg = lax.axis_size("segment")
    ndp = lax.axis_size("dp")
    half = nseg // 2
    ticks = fine_entries.shape[0] + 1
    hold_f, hold_c = fine_pending.shape[1], coarse_pending.shape[1]
    recv_f, recv_c = 3 * half - hold_f, half - hold_c
    fside, fch = fine_inflow.shape[3], fine_inflow.shape[4]
    cside, cch = coarse_inflow.shape[3], coarse_inflow.shape[4]
    fcells, ccells = fside * fside, cside * cside
    dims = (nseg, ndp, ticks, fside, cside, hold_f, recv_f, hold_c, recv_c)
    frows, crows = 2 * fch // LANES, 2 * cch // LANES
    any_spec = pl.BlockSpec(memory_space=pl.ANY)
    vmem_spec = pl.BlockSpec(memory_space=pltpu.VMEM)
    dma = pltpu.SemaphoreType.DMA
    args = (
        fine_inflow.reshape(fcells, fch),
        coarse_inflow.reshape(ccells, cch),
        fine_entries.reshape(ticks - 1, fcells, fch),
        fine_pending.reshape(hold_f, fcells, fch),
        coarse_pending.reshape(hold_c, ccells, cch),
        fine_kernels.reshape(2, 9 * fch, fch),
        fine_mixing.reshape(fch, fch),
        fine_gains.reshape(2, fch),
        fine_shifts.reshape(2, fch),
        coarse_kernel.reshape(9 * cch, cch),
        coarse_mixing.reshape(cch, cch),
        coarse_gains.reshape(1, cch),
        coarse_shifts.reshape(1, cch),
        descent_kernel.reshape(4 * fch, cch),
        upsample_kernel,
    )
    paired = nseg == 2 and ndp % 2 == 0 and recv_f == 1 and recv_c == 0
    if paired and ticks > hold_f + recv_f:
        fst, cst, fback, cback = run_pair(dims, fch, cch, args)
    else:
        outs = pl.pallas_call(
            functools.partial(kernel, dims),
            out_shape=(
                jax.ShapeDtypeStruct((ticks, fcells, fch), BF16),
                jax.ShapeDtypeStruct((ticks, ccells, cch), BF16),
                jax.ShapeDtypeStruct((hold_f, fcells, fch), BF16),
                jax.ShapeDtypeStruct((hold_c, ccells, cch), BF16),
            ),
            in_specs=[any_spec] * 7 + [vmem_spec] * 2 + [any_spec] * 2 + [vmem_spec] * 2 + [any_spec] * 2,
            out_specs=(any_spec,) * 4,
            scratch_shapes=[
                pltpu.VMEM((2, 9 * fch, fch), BF16),
                pltpu.VMEM((fch, fch), BF16),
                pltpu.VMEM((9 * cch, cch), BF16),
                pltpu.VMEM((cch, cch), BF16),
                pltpu.VMEM((4 * fch, cch), BF16),
                pltpu.VMEM((cch, 4 * fch), BF16),
                pltpu.VMEM((ticks, fcells, fch), BF16),
                pltpu.VMEM((ticks, ccells, cch), BF16),
                pltpu.VMEM((ticks, ccells, cch), BF16),
                pltpu.VMEM((max(hold_f, recv_f) + ticks, fcells, fch), BF16),
                pltpu.VMEM((max(hold_c, recv_c) + ticks, ccells, cch), BF16),
                pltpu.VMEM((ticks, fcells, fch), BF16),
                pltpu.VMEM((ticks, ccells, cch), BF16),
                pltpu.VMEM((ticks, ccells, cch), BF16),
                pltpu.VMEM((fcells, fch), F32),
                pltpu.VMEM((fcells, fch), F32),
                pltpu.VMEM((fcells, fch), F32),
                pltpu.VMEM((ccells, cch), F32),
                pltpu.VMEM((fch // LANES, cside, 2 * fside, LANES), F32),
                pltpu.VMEM((fcells, 9 * fch), BF16),
                pltpu.VMEM((ccells, 9 * cch), BF16),
                pltpu.VMEM((fcells, fch), BF16),
                pltpu.VMEM((ccells, cch), BF16),
                pltpu.VMEM((2 * ticks, frows, LANES), F32),
                pltpu.VMEM((ticks, crows, LANES), F32),
                pltpu.VMEM((2 * ticks, ndp - 1, frows, LANES), F32),
                pltpu.VMEM((ticks, ndp - 1, crows, LANES), F32),
                pltpu.VMEM((cch, 2, 2, fch), BF16),
                pltpu.VMEM((fch // LANES, 256, LANES), F32),
                dma((12,)),
                dma((4, max(ticks, hold_f, hold_c))),
                dma((ticks,)), dma((ticks,)), dma((ticks,)), dma((ticks,)), dma((ticks,)),
                dma((ticks,)), dma((ticks,)), dma((ticks,)), dma((ticks,)), dma((ticks,)),
                dma((2 * ticks,)), dma((ticks,)), dma((2 * ticks,)), dma((ticks,)),
            ],
            compiler_params=pltpu.CompilerParams(
                collective_id=0, has_side_effects=True, vmem_limit_bytes=56 << 20
            ),
        )(*args)
        fst, cst, fback, cback = hand_over(outs)
    return (
        fst.reshape(1, ticks, 1, fside, fside, fch),
        cst.reshape(1, ticks, 1, cside, cside, cch),
        fback.reshape(1, hold_f, 1, fside, fside, fch),
        cback.reshape(1, hold_c, 1, cside, cside, cch),
    )


def solution(mesh):
    placed = (
        P("segment", "dp", None, None, None),
        P("segment", "dp", None, None, None),
        P(None, "dp", None, None, None),
        P("segment", None, "dp", None, None, None),
        P("segment", None, "dp", None, None, None),
        P("segment", None, None, None, None, None),
        P("segment", None, None),
        P("segment", None, None),
        P("segment", None, None),
        P("segment", None, None, None, None),
        P("segment", None, None),
        P("segment", None),
        P("segment", None),
        P(),
        P(),
    )
    return jax.shard_map(
        on_device,
        mesh=mesh,
        in_specs=placed,
        out_specs=(
            P("segment", None, "dp", None, None, None),
            P("segment", None, "dp", None, None, None),
            P("segment", None, "dp", None, None, None),
            P("segment", None, "dp", None, None, None),
        ),
        check_vma=False,
    )
```
